256 devices in a mesh: gx: 4 (over x), gy: 4 (over y), gz: 16 (over z, core).
Axes of the slice: x: 4, y: 4, z: 8, core: 2. Of those that a mesh axis runs over, the one named last changes fastest.
Arguments:
- phase: int32 [32, 256, 2048], P('gx', 'gy', 'gz'), may hold values 0 or 1
- density: float32 [32, 256, 2048], P('gx', 'gy', 'gz'), may hold values from 0.5 to 2
- rhs: float32 [1, 32, 256, 2048], P(None, 'gx', 'gy', 'gz'), may hold values from -6 to 6
Outputs:
- scaled_solution: float32 [1, 32, 256, 2048], P(None, 'gx', 'gy', 'gz')
- residual: float32 [1, 32, 256, 2048], P(None, 'gx', 'gy', 'gz')
The draws below stay inside these ranges and needn't reach their ends.
All inputs are finite; a program needn't handle non-finite values. No bound on the sum of `phase` on one device may be relied on, other than what follows from the above.
Results may differ from the reference program's by a relative error of at most 0.0003.
Values sent between devices are 32-bit elements; how exact they have to be, the bound alone decides.
A program may use at most 128 MiB of HBM per device.

```python
import math
import jax
import jax.numpy as jnp
from jax import lax

NRHS = 1
LEVELS = 4
SWEEPS = 2
COARSE_SWEEPS = 4
NX = 32
NY = 256
NZ = 2048


def draw_rhs(key, part):
    shape = (NRHS, NX, NY, NZ)
    values = jnp.clip(jax.random.normal(key, shape, jnp.float32), -6.0, 6.0)
    return values.astype(jnp.float32)


def plant(result, key, smallest, largest):
    longest = result.shape.index(max(result.shape))
    spots = []
    for shift in (0, 1):
        where = [jax.random.randint(jax.random.fold_in(key, axis), (), 0, length) for axis, length in enumerate(result.shape)]
        where[longest] = (where[longest] + shift) % result.shape[longest]
        spots.append(tuple(where))
    return result.at[spots[0]].set(smallest).at[spots[1]].set(largest)


def steps_of(key, dims, shards, least, top_value):
    level, own = 1.0, jax.random.fold_in(key, 6)
    for axis_at, blocks in shards:
        steps = jnp.exp(jax.random.uniform(jax.random.fold_in(own, axis_at), (blocks,), jnp.float32, least / len(shards), top_value / len(shards)))
        level = level * jnp.repeat(steps, dims[axis_at] // blocks).reshape([-1 if axis == axis_at else 1 for axis in range(len(dims))])
    return level


def setup_inputs(seed: int = 0) -> dict:
    streams_of = jax.random.split(jax.random.key(seed), 4)
    phase = plant((jax.random.randint(streams_of[0], (NX, NY, NZ), 0, 3) < 1).astype(jnp.int32), jax.random.fold_in(streams_of[0], 1), 0, 1)
    density = jnp.clip(jnp.exp(math.log(2.0) - 1.3862944 * jax.random.uniform(streams_of[1], (NX, NY, NZ), jnp.float32) ** steps_of(streams_of[1], (NX, NY, NZ), ((0, 4), (1, 4), (2, 16)), -0.2, 0.2)), 0.5, 2.0)
    rhs = draw_rhs(jax.random.fold_in(streams_of[3], 71), 0)
    return {"phase": phase, "density": density, "rhs": rhs}


damping = 2.0 / 3.0


def face_pair(rho, up_nb, down_nb, top, bottom):
    face_up = 2.0 / (rho + up_nb)
    face_down = 2.0 / (rho + down_nb)
    return face_up, face_down, jnp.where(top, 0.0, face_up), jnp.where(bottom, 0.0, face_down)


def make_coef(rho):
    nx, ny, nz = rho.shape
    ext = jnp.pad(rho, 1, mode="edge")
    row_x = lax.broadcasted_iota(jnp.int32, (nx, 1, 1), 0)
    row_y = lax.broadcasted_iota(jnp.int32, (1, ny, 1), 1)
    row_z = lax.broadcasted_iota(jnp.int32, (1, 1, nz), 2)
    fxu, fxd, kxu, kxd = face_pair(rho, ext[2:, 1:-1, 1:-1], ext[:-2, 1:-1, 1:-1], row_x == nx - 1, row_x == 0)
    fyu, fyd, kyu, kyd = face_pair(rho, ext[1:-1, 2:, 1:-1], ext[1:-1, :-2, 1:-1], row_y == ny - 1, row_y == 0)
    fzu, fzd, kzu, kzd = face_pair(rho, ext[1:-1, 1:-1, 2:], ext[1:-1, 1:-1, :-2], row_z == nz - 1, row_z == 0)
    diag = fxu + fxd + fyu + fyd + fzu + fzd
    return jnp.stack([diag, kxu, kxd, kyu, kyd, kzu, kzd])


def blocks(a):
    s = a.shape
    lead = s[:-3]
    return a.reshape(lead + (s[-3] // 2, 2, s[-2] // 2, 2, s[-1] // 2, 2)).sum(axis=(-5, -3, -1))


def prolong(e):
    s = e.shape
    lead = s[:-3]
    wide = e.reshape(lead + (s[-3], 1, s[-2], 1, s[-1], 1))
    wide = jnp.broadcast_to(wide, lead + (s[-3], 2, s[-2], 2, s[-1], 2))
    return wide.reshape(lead + (2 * s[-3], 2 * s[-2], 2 * s[-1]))


def face_x(a, offset):
    b = a[offset::2]
    n0, n1, n2 = b.shape
    return b.reshape(n0, n1 // 2, 2, n2 // 2, 2).sum(axis=(2, 4))


def face_y(a, offset):
    b = a[:, offset::2]
    n0, n1, n2 = b.shape
    return b.reshape(n0 // 2, 2, n1, n2 // 2, 2).sum(axis=(1, 4))


def face_z(a, offset):
    b = a[:, :, offset::2]
    n0, n1, n2 = b.shape
    return b.reshape(n0 // 2, 2, n1 // 2, 2, n2).sum(axis=(1, 3))


def coarsen(coef):
    inner = face_x(coef[1], 0) + face_y(coef[3], 0) + face_z(coef[5], 0)
    diag = blocks(coef[0]) - 2.0 * inner
    return jnp.stack([diag, face_x(coef[1], 1), face_x(coef[2], 0), face_y(coef[3], 1), face_y(coef[4], 0), face_z(coef[5], 1), face_z(coef[6], 0)])


def stencil(padded, field, coef):
    beside = coef[1] * padded[:, 2:, 1:-1, 1:-1] + coef[2] * padded[:, :-2, 1:-1, 1:-1]
    beside = beside + coef[3] * padded[:, 1:-1, 2:, 1:-1] + coef[4] * padded[:, 1:-1, :-2, 1:-1]
    beside = beside + coef[5] * padded[:, 1:-1, 1:-1, 2:] + coef[6] * padded[:, 1:-1, 1:-1, :-2]
    return coef[0] * field - beside


def apply_op(field, coef):
    return stencil(jnp.pad(field, ((0, 0), (1, 1), (1, 1), (1, 1))), field, coef)


def sweep(field, source, coef):
    return field + (damping * (source - apply_op(field, coef))) / coef[0]


def vcycle(level, source, coefs):
    coef = coefs[level]
    field = jnp.zeros_like(source)
    if level == LEVELS - 1:
        for step in range(COARSE_SWEEPS):
            field = sweep(field, source, coef)
        return field
    for step in range(SWEEPS):
        field = sweep(field, source, coef)
    remain = source - apply_op(field, coef)
    correction = vcycle(level + 1, blocks(remain), coefs)
    field = field + prolong(correction)
    for step in range(SWEEPS):
        field = sweep(field, source, coef)
    return field


def reference(phase, density, rhs):
    rho = jnp.where(phase == 1, 1000.0, 1.0).astype(jnp.float32) * density
    coefs = [make_coef(rho)]
    for level in range(LEVELS - 1):
        coefs.append(coarsen(coefs[-1]))
    solution = vcycle(0, rhs, coefs)
    scaled_solution = coefs[0][0] * solution
    residual = rhs - apply_op(solution, coefs[0])
    return scaled_solution, residual
```

```python
import functools

import jax
import jax.numpy as jnp
from jax import lax
from jax.experimental import pallas as pl
from jax.experimental.pallas import tpu as pltpu
from jax.sharding import PartitionSpec as P

MESH = pl.DeviceIdType.MESH
F32 = jnp.float32
W = 2.0 / 3.0
THIRD = 1.0 / 3.0
HI = lax.Precision.HIGHEST


def lanes(shape):
    return lax.broadcasted_iota(jnp.int32, shape, len(shape) - 1)


def roll(v, shift):
    return pltpu.roll(v, shift, 1)


def loop(count, body, init=0):
    return lax.fori_loop(0, count, body, init, unroll=True)


def each(count, body):
    def step(i, carry):
        body(i)
        return carry

    lax.fori_loop(0, count, step, 0, unroll=True)


def maps():
    row = lax.broadcasted_iota(jnp.int32, (128, 128), 0)
    col = lax.broadcasted_iota(jnp.int32, (128, 128), 1)
    hit = col == 32 + row // 2
    both = jnp.where(hit, 1.0, 0.0).astype(F32)
    odd = jnp.where(hit & (row % 2 == 1), 1.0, 0.0).astype(F32)
    even = jnp.where(hit & (row % 2 == 0), 1.0, 0.0).astype(F32)
    back = jnp.where(row == 32 + col // 2, 1.0, 0.0).astype(F32)
    return both, odd, even, back


def mm(a, b):
    return lax.dot(a, b, precision=HI, preferred_element_type=F32)


def kernel(
    ph_h, de_h, rh_h, os_h, or_h,
    ph, de, f0, rp, u0, fx, fy, fzu, fzd, w0, d0,
    rys, ryr, rzs, rzr, ys0, yr0, zs0, zr0,
    u1, f1, fx1, fy1u, fy1d, fz1u, fz1d, w1, d1,
    ys1, yr1, zs1, zr1,
    mb, mo, me, mt, t0, t1, t2,
    cc, gg,
    f2, u2, fx2, fy2, fz2, w2, d2,
    f3, u3, fx3, fy3, fz3, w3,
    osol, ores,
    in_sem, out_sem, rss, rrs, s0s, r0s, s1s, r1s, csx, crx, csn, crn, gsx, grx, gsn, grn,
):
    gx, gy, gz = lax.axis_index("gx"), lax.axis_index("gy"), lax.axis_index("gz")
    nx, ny, nz = lax.axis_size("gx"), lax.axis_size("gy"), lax.axis_size("gz")
    near = [
        ({"gx": gx + 1}, gx < nx - 1, gx > 0),
        ({"gx": gx - 1}, gx > 0, gx < nx - 1),
        ({"gy": gy + 1}, gy < ny - 1, gy > 0),
        ({"gy": gy - 1}, gy > 0, gy < ny - 1),
        ({"gz": gz + 1}, gz < nz - 1, gz > 0),
        ({"gz": gz - 1}, gz > 0, gz < nz - 1),
    ]

    loads = [
        pltpu.make_async_copy(ph_h, ph, in_sem.at[0]),
        pltpu.make_async_copy(de_h, de, in_sem.at[1]),
        pltpu.make_async_copy(rh_h.at[0], f0, in_sem.at[2]),
    ]
    for c in loads:
        c.start()

    for b in range(2):
        for x in (0, 9):
            u0[b, x, 8:72, :] = jnp.zeros((64, 128), F32)
        for x in (0, 5):
            u1[b, x, 8:40, :] = jnp.zeros((32, 128), F32)
        for ref in (yr0, zr0, yr1, zr1):
            for s in range(2):
                ref[b, s] = jnp.zeros((8, 128), F32)

    @pl.when((gy == 0) | (gy == ny - 1) | (gz == 0) | (gz == nz - 1))
    def _():
        for z in range(3):
            for y in range(3):
                if (z, y) != (1, 1):
                    cc[z, y] = jnp.zeros(cc.shape[2:], F32)
                    gg[z, y] = jnp.zeros(gg.shape[2:], F32)

    barrier = pltpu.get_barrier_semaphore()
    for d in range(1, 4):
        pl.semaphore_signal(barrier, inc=1, device_id={"gx": lax.rem(gx + d, nx)}, device_id_type=MESH)
    for where, ok, _ in near[2:]:
        @pl.when(ok)
        def _(where=where):
            pl.semaphore_signal(barrier, inc=1, device_id=where, device_id_type=MESH)
    arrivals = 3 + sum(jnp.where(ok, 1, 0) for _, ok, _ in near[2:])

    def faces(buf, n, rows, ys, yr, zs, zr, ss, rs):
        body = pl.ds(8, rows)
        pairs = [
            (buf.at[n, body], buf.at[0, body]),
            (buf.at[1, body], buf.at[n + 1, body]),
            (ys.at[1], yr.at[0]),
            (ys.at[0], yr.at[1]),
            (zs.at[1], zr.at[0]),
            (zs.at[0], zr.at[1]),
        ]

        def copy(d):
            src, dst = pairs[d]
            return pltpu.make_async_remote_copy(
                src_ref=src, dst_ref=dst, send_sem=ss.at[d], recv_sem=rs.at[d],
                device_id=near[d][0], device_id_type=MESH,
            )

        def start():
            for d in range(6):
                @pl.when(near[d][1])
                def _(d=d):
                    copy(d).start()

        def wait():
            for d in range(6):
                @pl.when(near[d][1])
                def _(d=d):
                    copy(d).wait_send()

                @pl.when(near[d][2])
                def _(d=d):
                    copy(d).wait_recv()

        return start, wait

    lane8 = lanes((8, 128))
    lane64 = lanes((64, 128))
    lane32 = lanes((32, 128))

    zero8 = jnp.zeros((8, 128), F32)

    def pack0(carry, plane, x):
        lo, hi = carry
        for t in range(8):
            v = plane[8 * t : 8 * t + 8]
            k = x * 8 + t
            here = lane8 == k
            lo = jnp.where(here, roll(v, k), lo)
            hi = jnp.where(here, roll(v, k + 1), hi)
        return lo, hi

    def z_beside0(plane, x, lo, hi):
        right = jnp.concatenate([roll(hi, 127 - (x * 8 + t)) for t in range(8)], axis=0)
        left = jnp.concatenate([roll(lo, lax.rem(128 - (x * 8 + t), 128)) for t in range(8)], axis=0)
        return (
            jnp.where(lane64 == 127, right, roll(plane, 127)),
            jnp.where(lane64 == 0, left, roll(plane, 1)),
        )

    def keep0(buf, ys, x, plane):
        buf[x + 1, 8:72, :] = plane
        ys[0, pl.ds(x, 1), :] = plane[0:1]
        ys[1, pl.ds(x, 1), :] = plane[63:64]

    def y_in(buf, yr, n, rows):
        def body(x):
            buf[x + 1, 7:8, :] = yr[0, pl.ds(x, 1), :]
            buf[x + 1, 8 + rows : 9 + rows, :] = yr[1, pl.ds(x, 1), :]

        each(n, body)

    def beside0(buf, x, lo, hi):
        c = buf[x + 1, 8:72, :]
        up, down = z_beside0(c, x, lo, hi)
        s = fx[x + 1] * buf[x + 2, 8:72, :] + fx[x] * buf[x, 8:72, :]
        s = s + fy[x, 8:72, :] * buf[x + 1, 9:73, :] + fy[x, 7:71, :] * buf[x + 1, 7:71, :]
        s = s + fzu[x] * up + fzd[x] * down
        return c, s

    def sweep0(src, dst, zr, ys, zs, out):
        lo, hi = zr[0], zr[1]

        def body(x, carry):
            c, s = beside0(src, x, lo, hi)
            new = c * THIRD + w0[x] * (f0[x] + s)
            keep0(dst, ys, x, new)
            if out:
                osol[x] = d0[x] * new
            return pack0(carry, new, x)

        packed = loop(8, body, (zero8, zero8))
        zs[0] = packed[0]
        zs[1] = packed[1]

    for c in loads[:2]:
        c.wait()

    def body(x, carry):
        plane = jnp.where(ph[x] == 1, 1000.0, 1.0).astype(F32) * de[x]
        keep0(rp, rys, x, plane)
        return pack0(carry, plane, x)

    packed = loop(8, body, (zero8, zero8))
    rzs[0] = packed[0]
    rzs[1] = packed[1]

    pl.semaphore_wait(barrier, arrivals)
    start, wait = faces(rp, 8, 64, rys, ryr, rzs, rzr, rss, rrs)
    start()
    both, odd, even, back = maps()
    mb[...] = both
    mo[...] = odd
    me[...] = even
    mt[...] = back
    loads[2].wait()
    wait()

    @pl.when(gx == 0)
    def _():
        rp[0, 8:72, :] = rp[1, 8:72, :]

    @pl.when(gx == nx - 1)
    def _():
        rp[9, 8:72, :] = rp[8, 8:72, :]

    for ok, got, own, s in ((gy == 0, ryr, rys, 0), (gy == ny - 1, ryr, rys, 1), (gz == 0, rzr, rzs, 0), (gz == nz - 1, rzr, rzs, 1)):
        @pl.when(ok)
        def _(got=got, own=own, s=s):
            got[s] = own[s]

    y_in(rp, ryr, 8, 64)
    lo, hi = rzr[0], rzr[1]
    fx[0] = 2.0 / (rp[0, 8:72, :] + rp[1, 8:72, :])

    def body(x, carry):
        c = rp[x + 1, 8:72, :]
        up, down = z_beside0(c, x, lo, hi)
        xu = 2.0 / (c + rp[x + 2, 8:72, :])
        yu = 2.0 / (c + rp[x + 1, 9:73, :])
        zu = 2.0 / (c + up)
        zd = 2.0 / (c + down)
        fx[x + 1] = xu
        fy[x, 8:72, :] = yu
        fy[x, 7:8, :] = 2.0 / (c[0:1] + rp[x + 1, 7:8, :])
        fzu[x] = zu
        fzd[x] = zd
        diag = xu + fx[x] + yu + fy[x, 7:71, :] + zu + zd
        d0[x] = diag
        w = W / diag
        w0[x] = w
        first = w * f0[x]
        keep0(u0.at[0], ys0.at[0], x, first)
        return pack0(carry, first, x)

    packed = loop(8, body, (zero8, zero8))
    zs0[0, 0] = packed[0]
    zs0[0, 1] = packed[1]

    def round0(b):
        return faces(u0.at[b], 8, 64, ys0.at[b], yr0.at[b], zs0.at[b], zr0.at[b], s0s.at[b], r0s.at[b])

    def round1(b):
        return faces(u1.at[b], 4, 32, ys1.at[b], yr1.at[b], zs1.at[b], zr1.at[b], s1s.at[b], r1s.at[b])

    start, wait = round0(0)
    start()

    own1 = (lane32 >= 32) & (lane32 < 96)

    def rows_of(ref, base, n, off):
        return ref[pl.ds(base + off, n, stride=2), :]

    def pair_rows(ref, base, n):
        return rows_of(ref, base, n, 0) + rows_of(ref, base, n, 1)

    for i in range(5):
        t0[0:64, :] = fx[2 * i]
        fx1[i] = mm(pair_rows(t0, 0, 32), mb[...])

    def body(i):
        yu = fy[2 * i, pl.ds(9, 32, stride=2), :] + fy[2 * i + 1, pl.ds(9, 32, stride=2), :]
        yd = fy[2 * i, pl.ds(7, 32, stride=2), :] + fy[2 * i + 1, pl.ds(7, 32, stride=2), :]
        t1[i, 0] = fzu[2 * i] + fzu[2 * i + 1]
        t1[i, 1] = fzd[2 * i] + fzd[2 * i + 1]
        zu = t1[i, 0, pl.ds(0, 32, stride=2), :] + t1[i, 0, pl.ds(1, 32, stride=2), :]
        zd = t1[i, 1, pl.ds(0, 32, stride=2), :] + t1[i, 1, pl.ds(1, 32, stride=2), :]
        yu, yd, zu, zd = mm(yu, mb[...]), mm(yd, mb[...]), mm(zu, mo[...]), mm(zd, me[...])
        fy1u[i] = yu
        fy1d[i] = yd
        fz1u[i] = zu
        fz1d[i] = zd
        diag = fx1[i] + fx1[i + 1] + yu + yd + zu + zd
        d1[i] = diag
        w1[i] = jnp.where(own1, W / jnp.where(own1, diag, 1.0), 0.0)

    each(4, body)

    def pack2(planes):
        out = zero8
        for x in range(2):
            for t in range(2):
                g = 2 * x + t
                v = roll(planes[x][8 * t : 8 * t + 8], (32 * g - 48) % 128)
                out = jnp.where((lane8 >= 32 * g) & (lane8 < 32 * g + 32), v, out)
        return out

    xu, yu, zu, dg = [], [], [], []
    for i in range(2):
        t0[0:32, :] = fx1[2 * i]
        t0[32:64, :] = fx1[2 * i + 2]
        t0[64:96, :] = fz1u[2 * i] + fz1u[2 * i + 1]
        t0[96:128, :] = fz1d[2 * i] + fz1d[2 * i + 1]
        t0[128:160, :] = fy1u[2 * i] + fy1u[2 * i + 1]
        t0[160:192, :] = fy1d[2 * i] + fy1d[2 * i + 1]
        xd_, xu_ = mm(pair_rows(t0, 0, 16), mb[...]), mm(pair_rows(t0, 32, 16), mb[...])
        zu_, zd_ = mm(pair_rows(t0, 64, 16), mo[...]), mm(pair_rows(t0, 96, 16), me[...])
        yu_, yd_ = mm(rows_of(t0, 128, 16, 1), mb[...]), mm(rows_of(t0, 160, 16, 0), mb[...])
        xu.append(xu_)
        yu.append(yu_)
        zu.append(zu_)
        dg.append(xu_ + xd_ + yu_ + yd_ + zu_ + zd_)
    for a, planes in enumerate((dg, xu, yu, zu)):
        cc[1, 1, gx, a] = pack2(planes)

    def gather(buf, sx, rx, sn, rn):
        def xcopy(d):
            return pltpu.make_async_remote_copy(
                src_ref=buf.at[1, 1, gx], dst_ref=buf.at[1, 1, gx], send_sem=sx.at[d - 1], recv_sem=rx.at[d - 1],
                device_id={"gx": lax.rem(gx + d, nx)}, device_id_type=MESH,
            )

        def ncopy(d):
            src = buf.at[1, 1] if d < 4 else buf.at[1]
            dst = [buf.at[1, 0], buf.at[1, 2], buf.at[0], buf.at[2]][d - 2]
            return pltpu.make_async_remote_copy(
                src_ref=src, dst_ref=dst, send_sem=sn.at[d - 2], recv_sem=rn.at[d - 2],
                device_id=near[d][0], device_id_type=MESH,
            )

        def xstart():
            for d in range(1, 4):
                xcopy(d).start()

        def xwait():
            for d in range(1, 4):
                pltpu.make_async_remote_copy(
                    src_ref=buf.at[1, 1, gx], dst_ref=buf.at[1, 1, lax.rem(gx + 4 - d, nx)],
                    send_sem=sx.at[d - 1], recv_sem=rx.at[d - 1],
                    device_id={"gx": lax.rem(gx + d, nx)}, device_id_type=MESH,
                ).wait()

        def nstart(ds):
            for d in ds:
                @pl.when(near[d][1])
                def _(d=d):
                    ncopy(d).start()

        def nwait(ds):
            for d in ds:
                @pl.when(near[d][1])
                def _(d=d):
                    ncopy(d).wait_send()

                @pl.when(near[d][2])
                def _(d=d):
                    ncopy(d).wait_recv()

        return (
            xstart, xwait,
            lambda: nstart((2, 3)), lambda: nwait((2, 3)),
            lambda: nstart((4, 5)), lambda: nwait((4, 5)),
        )

    cg = gather(cc, csx, crx, csn, crn)
    cg[0]()

    wait()
    y_in(u0.at[0], yr0.at[0], 8, 64)
    sweep0(u0.at[0], u0.at[1], zr0.at[0], ys0.at[1], zs0.at[1], False)
    start, wait = round0(1)
    start()
    cg[1]()
    cg[2]()
    wait()
    y_in(u0.at[1], yr0.at[1], 8, 64)

    lo, hi = zr0[1, 0], zr0[1, 1]

    def body(i):
        total = None
        for j in range(2):
            x = 2 * i + j
            c, s = beside0(u0.at[1], x, lo, hi)
            r = f0[x] - d0[x] * c + s
            total = r if total is None else total + r
        t1[i, 0] = total
        f1[i] = mm(t1[i, 0, pl.ds(0, 32, stride=2), :] + t1[i, 0, pl.ds(1, 32, stride=2), :], mb[...])

    each(4, body)

    def pack1(carry, plane, x):
        lo, hi = carry
        for t in range(4):
            v = plane[8 * t : 8 * t + 8]
            k = x * 4 + t
            here = lane8 // 8 == k
            lo = jnp.where(here, roll(v, lax.rem(8 * k + 96, 128)), lo)
            hi = jnp.where(here, roll(v, lax.rem(8 * k + 40, 128)), hi)
        return lo, hi

    def z_in1(plane, x, lo, hi):
        right = jnp.concatenate([roll(hi, lax.rem(96 + 128 - 8 * (x * 4 + t), 128)) for t in range(4)], axis=0)
        left = jnp.concatenate([roll(lo, lax.rem(24 + 128 - 8 * (x * 4 + t), 128)) for t in range(4)], axis=0)
        return jnp.where(lane32 >= 96, right, jnp.where(lane32 < 32, left, plane))

    def keep1(buf, ys, x, plane):
        buf[x + 1, 8:40, :] = plane
        ys[0, pl.ds(x, 1), :] = plane[0:1]
        ys[1, pl.ds(x, 1), :] = plane[31:32]

    def beside1(buf, x, lo, hi):
        c = buf[x + 1, 8:40, :]
        wide = z_in1(c, x, lo, hi)
        s = fx1[x + 1] * buf[x + 2, 8:40, :] + fx1[x] * buf[x, 8:40, :]
        s = s + fy1u[x] * buf[x + 1, 9:41, :] + fy1d[x] * buf[x + 1, 7:39, :]
        s = s + fz1u[x] * roll(wide, 127) + fz1d[x] * roll(wide, 1)
        return c, s

    def sweep1(src, dst, zr, ys, zs):
        lo, hi = zr[0], zr[1]

        def body(x, carry):
            c, s = beside1(src, x, lo, hi)
            new = c * THIRD + w1[x] * (f1[x] + s)
            keep1(dst, ys, x, new)
            return pack1(carry, new, x)

        packed = loop(4, body, (zero8, zero8))
        zs[0] = packed[0]
        zs[1] = packed[1]

    def body(x, carry):
        new = w1[x] * f1[x]
        keep1(u1.at[0], ys1.at[0], x, new)
        return pack1(carry, new, x)

    packed = loop(4, body, (zero8, zero8))
    zs1[0, 0] = packed[0]
    zs1[0, 1] = packed[1]
    start, wait = round1(0)
    start()
    cg[3]()
    cg[4]()
    wait()
    y_in(u1.at[0], yr1.at[0], 4, 32)
    sweep1(u1.at[0], u1.at[1], zr1.at[0], ys1.at[1], zs1.at[1])
    start, wait = round1(1)
    start()
    wait()
    y_in(u1.at[1], yr1.at[1], 4, 32)
    lo, hi = zr1[1, 0], zr1[1, 1]

    src2 = []
    for i in range(2):
        total = None
        for j in range(2):
            x = 2 * i + j
            c, s = beside1(u1.at[1], x, lo, hi)
            r = f1[x] - d1[x] * c + s
            total = r if total is None else total + r
        t0[32 * i : 32 * i + 32, :] = jnp.where(own1, total, 0.0)
        src2.append(mm(pair_rows(t0, 32 * i, 16), mb[...]))
    gg[1, 1, gx] = pack2(src2)
    fg = gather(gg, gsx, grx, gsn, grn)
    fg[0]()
    cg[5]()

    def spread2(get, put):
        def body(b):
            for y in range(3):
                v = [get(z, y, b) for z in range(3)]
                for x in range(2):
                    for t in range(2):
                        g = 2 * x + t
                        left = roll(v[0], (16 - 32 * g) % 128)
                        mid = roll(v[1], (48 - 32 * g) % 128)
                        right = roll(v[2], (80 - 32 * g) % 128)
                        out = jnp.where(lane8 < 48, left, jnp.where(lane8 < 80, mid, right))
                        out = jnp.where((lane8 >= 16) & (lane8 < 112), out, 0.0)
                        put(2 * b + x, 16 * y + 8 * t, out)

        each(4, body)

    def put_d(p, r, v):
        d2[p, r : r + 8, :] = v
        ok = v > 0.0
        w2[p, r : r + 8, :] = jnp.where(ok, W / jnp.where(ok, v, 1.0), 0.0)

    def put_x(p, r, v):
        fx2[p + 1, r : r + 8, :] = v

    def put_y(p, r, v):
        fy2[p, 8 + r : 16 + r, :] = v

    def put_z(p, r, v):
        fz2[p, r : r + 8, :] = v

    def put_f(p, r, v):
        f2[p, r : r + 8, :] = v
        u2[0, p + 1, 8 + r : 16 + r, :] = w2[p, r : r + 8, :] * v

    for a, put in enumerate((put_d, put_x, put_y, put_z)):
        spread2(lambda z, y, b, a=a: cc[z, y, b, a], put)
    fx2[0] = jnp.zeros((48, 128), F32)
    fx3[0] = jnp.zeros((24, 128), F32)

    def zero_rows(ref, n, rows):
        def body(p):
            ref[p, 0:8, :] = zero8
            ref[p, 8 + rows : 16 + rows, :] = zero8

        each(n, body)

    zero_rows(fy2, 8, 48)
    zero_rows(fy3, 4, 24)
    for b in range(2):
        zero_rows(u2.at[b], 10, 48)
        zero_rows(u3.at[b], 6, 24)
        for p in (0, 9):
            u2[b, p, 8:56, :] = jnp.zeros((48, 128), F32)
        for p in (0, 5):
            u3[b, p, 8:32, :] = jnp.zeros((24, 128), F32)

    lane48 = lanes((48, 128))
    row48 = lax.broadcasted_iota(jnp.int32, (48, 128), 0)

    def body(p):
        a, b = 2 * p, 2 * p + 1
        t2[p, 0] = fx2[b + 1]
        t2[p, 1] = fz2[a] + fz2[b]
        ysum = fy2[a, 8:56, :] + fy2[b, 8:56, :]
        t2[p, 2] = ysum
        inner = fx2[a + 1]
        inner = inner + jnp.where(row48 % 2 == 0, ysum, 0.0)
        inner = inner + jnp.where(lane48 % 2 == 0, fz2[a] + fz2[b], 0.0)
        t2[p, 3] = d2[a] + d2[b] - 2.0 * inner
        pick = lambda q, off: t2[p, q, pl.ds(off, 24, stride=2), :]
        fx3[p + 1] = mm(pick(0, 0) + pick(0, 1), mb[...])
        fz3[p] = mm(pick(1, 0) + pick(1, 1), mo[...])
        fy3[p, 8:32, :] = mm(pick(2, 1), mb[...])
        diag = mm(pick(3, 0) + pick(3, 1), mb[...])
        ok = diag > 0.0
        w3[p] = jnp.where(ok, W / jnp.where(ok, diag, 1.0), 0.0)

    each(4, body)

    fg[1]()
    fg[2]()
    fg[3]()
    fg[4]()
    fg[5]()
    spread2(lambda z, y, b: gg[z, y, b], put_f)

    def beside(buf, fxr, fyr, fzr, p, rows):
        c = buf[p + 1, 8 : 8 + rows, :]
        s = fxr[p + 1] * buf[p + 2, 8 : 8 + rows, :] + fxr[p] * buf[p, 8 : 8 + rows, :]
        s = s + fyr[p, 8 : 8 + rows, :] * buf[p + 1, 9 : 9 + rows, :]
        s = s + fyr[p, 7 : 7 + rows, :] * buf[p + 1, 7 : 7 + rows, :]
        z = fzr[p]
        return c, s + z * roll(c, 127) + roll(z * c, 1)

    def sweep2(src, dst):
        def body(p):
            c, s = beside(u2.at[src], fx2, fy2, fz2, p, 48)
            u2[dst, p + 1, 8:56, :] = c * THIRD + w2[p] * (f2[p] + s)

        each(8, body)

    def sweep3(src, dst):
        def body(p):
            c, s = beside(u3.at[src], fx3, fy3, fz3, p, 24)
            u3[dst, p + 1, 8:32, :] = c * THIRD + w3[p] * (f3[p] + s)

        each(4, body)

    sweep2(0, 1)

    def body(p):
        total = None
        for j in range(2):
            c, s = beside(u2.at[1], fx2, fy2, fz2, 2 * p + j, 48)
            r = f2[2 * p + j] - d2[2 * p + j] * c + s
            total = r if total is None else total + r
        t2[p, 0] = total
        src = mm(t2[p, 0, pl.ds(0, 24, stride=2), :] + t2[p, 0, pl.ds(1, 24, stride=2), :], mb[...])
        f3[p] = src
        u3[0, p + 1, 8:32, :] = w3[p] * src

    each(4, body)
    sweep3(0, 1)
    sweep3(1, 0)
    sweep3(0, 1)

    def body(p):
        e = mm(u3[1, p + 1, 8:32, :], mt[...])
        t2[p, 1, pl.ds(0, 24, stride=2), :] = e
        t2[p, 1, pl.ds(1, 24, stride=2), :] = e
        wide = t2[p, 1]
        for j in range(2):
            q = 2 * p + j
            u2[0, q + 1, 8:56, :] = u2[1, q + 1, 8:56, :] + jnp.where(d2[q] > 0.0, wide, 0.0)

    each(4, body)
    sweep2(0, 1)
    sweep2(1, 0)

    corr = []
    for i in range(2):
        e = mm(u2[0, 2 * gx + 1 + i, 24:40, :], mt[...])
        t0[pl.ds(32 * i, 16, stride=2), :] = e
        t0[pl.ds(32 * i + 1, 16, stride=2), :] = e
        corr.append(jnp.where(own1, t0[32 * i : 32 * i + 32, :], 0.0))
    carry = (zero8, zero8)
    for x in range(4):
        new = u1[1, x + 1, 8:40, :] + corr[x // 2]
        keep1(u1.at[0], ys1.at[0], x, new)
        carry = pack1(carry, new, x)
    zs1[0, 0] = carry[0]
    zs1[0, 1] = carry[1]
    for b in range(2):
        start, wait = round1(b)
        start()
        wait()
        y_in(u1.at[b], yr1.at[b], 4, 32)
        sweep1(u1.at[b], u1.at[1 - b], zr1.at[b], ys1.at[1 - b], zs1.at[1 - b])

    def body(i, carry):
        e = mm(u1[0, i + 1, 8:40, :], mt[...])
        t1[i, 0, pl.ds(0, 32, stride=2), :] = e
        t1[i, 0, pl.ds(1, 32, stride=2), :] = e
        wide = t1[i, 0]
        for j in range(2):
            x = 2 * i + j
            new = u0[1, x + 1, 8:72, :] + wide
            keep0(u0.at[0], ys0.at[0], x, new)
            carry = pack0(carry, new, x)
        return carry

    packed = loop(4, body, (zero8, zero8))
    zs0[0, 0] = packed[0]
    zs0[0, 1] = packed[1]
    for b in range(2):
        start, wait = round0(b)
        start()
        wait()
        y_in(u0.at[b], yr0.at[b], 8, 64)
        sweep0(u0.at[b], u0.at[1 - b], zr0.at[b], ys0.at[1 - b], zs0.at[1 - b], b == 1)

    start, wait = round0(0)
    start()
    out0 = pltpu.make_async_copy(osol, os_h.at[0], out_sem.at[0])
    out0.start()
    wait()
    y_in(u0.at[0], yr0.at[0], 8, 64)
    lo, hi = zr0[0, 0], zr0[0, 1]

    def body(x):
        c, s = beside0(u0.at[0], x, lo, hi)
        ores[x] = f0[x] - d0[x] * c + s

    each(8, body)
    out1 = pltpu.make_async_copy(ores, or_h.at[0], out_sem.at[1])
    out1.start()
    out0.wait()
    out1.wait()


def on_device(phase, density, rhs):
    V = lambda *s: pltpu.VMEM(s, F32)
    D = lambda *s: pltpu.SemaphoreType.DMA(s)
    scratch = [
        pltpu.VMEM((8, 64, 128), jnp.int32), V(8, 64, 128), V(8, 64, 128), V(10, 80, 128), V(2, 10, 80, 128),
        V(9, 64, 128), V(8, 80, 128), V(8, 64, 128), V(8, 64, 128), V(8, 64, 128), V(8, 64, 128),
        V(2, 8, 128), V(2, 8, 128), V(2, 8, 128), V(2, 8, 128),
        V(2, 2, 8, 128), V(2, 2, 8, 128), V(2, 2, 8, 128), V(2, 2, 8, 128),
        V(2, 6, 48, 128), V(4, 32, 128), V(5, 32, 128), V(4, 32, 128), V(4, 32, 128), V(4, 32, 128), V(4, 32, 128),
        V(4, 32, 128), V(4, 32, 128),
        V(2, 2, 8, 128), V(2, 2, 8, 128), V(2, 2, 8, 128), V(2, 2, 8, 128),
        V(128, 128), V(128, 128), V(128, 128), V(128, 128), V(256, 128), V(4, 2, 64, 128), V(4, 4, 48, 128),
        V(3, 3, 4, 4, 8, 128), V(3, 3, 4, 8, 128),
        V(8, 48, 128), V(2, 10, 64, 128), V(9, 48, 128), V(8, 64, 128), V(8, 48, 128), V(8, 48, 128), V(8, 48, 128),
        V(4, 24, 128), V(2, 6, 40, 128), V(5, 24, 128), V(4, 40, 128), V(4, 24, 128), V(4, 24, 128),
        V(8, 64, 128), V(8, 64, 128),
        D(3), D(2), D(6), D(6), D(2, 6), D(2, 6), D(2, 6), D(2, 6),
        D(3), D(3), D(4), D(4), D(3), D(3), D(4), D(4),
    ]
    shape = jax.ShapeDtypeStruct(rhs.shape, F32)
    return pl.pallas_call(
        kernel,
        out_shape=(shape, shape),
        in_specs=[pl.BlockSpec(memory_space=pl.ANY)] * 3,
        out_specs=(pl.BlockSpec(memory_space=pl.ANY),) * 2,
        scratch_shapes=scratch,
        compiler_params=pltpu.CompilerParams(collective_id=0, has_side_effects=True),
        name="vcycle",
    )(phase, density, rhs)


def solution(mesh):
    in_specs = (P("gx", "gy", "gz"), P("gx", "gy", "gz"), P(None, "gx", "gy", "gz"))
    out_specs = (P(None, "gx", "gy", "gz"), P(None, "gx", "gy", "gz"))
    return jax.shard_map(on_device, mesh=mesh, in_specs=in_specs, out_specs=out_specs, check_vma=False)
```

```python
import functools

import jax
import jax.numpy as jnp
from jax import lax
from jax.experimental import pallas as pl
from jax.experimental.pallas import tpu as pltpu
from jax.sharding import PartitionSpec as P

MESH = pl.DeviceIdType.MESH
F32 = jnp.float32
W = 2.0 / 3.0
THIRD = 1.0 / 3.0
BF16 = jnp.bfloat16


def lanes(shape):
    return lax.broadcasted_iota(jnp.int32, shape, len(shape) - 1)


def roll(v, shift):
    return pltpu.roll(v, shift, 1)


def loop(count, body, init=0):
    return lax.fori_loop(0, count, body, init, unroll=True)


def each(count, body):
    def step(i, carry):
        body(i)
        return carry

    lax.fori_loop(0, count, step, 0, unroll=True)


def maps():
    row = lax.broadcasted_iota(jnp.int32, (128, 128), 0)
    col = lax.broadcasted_iota(jnp.int32, (128, 128), 1)
    hit = col == 32 + row // 2
    both = jnp.where(hit, 1.0, 0.0)
    odd = jnp.where(hit & (row % 2 == 1), 1.0, 0.0)
    even = jnp.where(hit & (row % 2 == 0), 1.0, 0.0)
    back = jnp.where(row == 32 + col // 2, 1.0, 0.0)
    return [jnp.concatenate([m.astype(BF16)] * 3, axis=0) for m in (both, odd, even, back)]


def mm(a, b):
    hi = a.astype(BF16)
    rest = a - hi.astype(F32)
    mid = rest.astype(BF16)
    low = (rest - mid.astype(F32)).astype(BF16)
    return lax.dot(jnp.concatenate([hi, mid, low], axis=1), b, preferred_element_type=F32)


def kernel(
    ph_h, de_h, rh_h, os_h, or_h,
    ph, de, f0, rp, u0, fx, fy, fzu, fzd, w0, d0,
    rys, ryr, rzs, rzr, ys0, yr0, zs0, zr0,
    u1, f1, fx1, fy1u, fy1d, fz1u, fz1d, d1, w1, ce1,
    pkc, zpc, rxc, ryc, rzc, pkf, zpf, rxf, ryf, rzf,
    mb, mo, me, mt, t0, t1, t2, t3, t4, t5, f1e,
    cc, gg,
    f2, u2, fx2, fy2, fz2, w2, d2,
    f3, u3, fx3, fy3, fz3, w3,
    osol, ores,
    in_sem, out_sem, rss, rrs, s0s, r0s, s1c, r1c, s1f, r1f, csx, crx, csn, crn, gs, gr,
):
    gx, gy, gz = lax.axis_index("gx"), lax.axis_index("gy"), lax.axis_index("gz")
    nx, ny, nz = lax.axis_size("gx"), lax.axis_size("gy"), lax.axis_size("gz")
    near = [
        ({"gx": gx + 1}, gx < nx - 1, gx > 0),
        ({"gx": gx - 1}, gx > 0, gx < nx - 1),
        ({"gy": gy + 1}, gy < ny - 1, gy > 0),
        ({"gy": gy - 1}, gy > 0, gy < ny - 1),
        ({"gz": gz + 1}, gz < nz - 1, gz > 0),
        ({"gz": gz - 1}, gz > 0, gz < nz - 1),
    ]

    loads = [
        pltpu.make_async_copy(ph_h, ph, in_sem.at[0]),
        pltpu.make_async_copy(de_h, de, in_sem.at[1]),
        pltpu.make_async_copy(rh_h.at[0], f0, in_sem.at[2]),
    ]
    for c in loads:
        c.start()

    for b in range(3):
        for x in (0, 9):
            u0[b, x, 8:72, :] = jnp.zeros((64, 128), F32)
        for ref in (yr0, zr0):
            for s in range(2):
                ref[b, s] = jnp.zeros((8, 128), F32)

    edge = (gx == 0) | (gx == nx - 1) | (gy == 0) | (gy == ny - 1) | (gz == 0) | (gz == nz - 1)

    @pl.when(edge)
    def _():
        for ref in (cc, gg, rxc, ryc, rzc, rxf, ryf, rzf):
            ref[...] = jnp.zeros(ref.shape, F32)

    def inside(at, step, count):
        return (at >= 0) if step == 0 else (at < count - 1) if step > 0 else (at > 0)

    def yz_ok(sy, sz):
        return inside(gy, sy, ny) & inside(gz, sz, nz)

    def at(sx, sy, sz):
        return {"gx": sx, "gy": gy + sy, "gz": gz + sz}

    steps = (-1, 0, 1)
    barrier = pltpu.get_barrier_semaphore()
    arrivals = 0
    for sy in steps:
        for sz in steps:
            ok = yz_ok(sy, sz)
            n = 3 if (sy, sz) == (0, 0) else 4
            arrivals = arrivals + jnp.where(ok, n, 0)

            @pl.when(ok)
            def _(sy=sy, sz=sz, n=n):
                for d in range(4 - n, 4):
                    pl.semaphore_signal(barrier, inc=1, device_id=at(lax.rem(gx + d, nx), sy, sz), device_id_type=MESH)

    def faces(buf, n, rows, ys, yr, zs, zr, ss, rs):
        body = pl.ds(8, rows)
        pairs = [
            (buf.at[n, body], buf.at[0, body]),
            (buf.at[1, body], buf.at[n + 1, body]),
            (ys.at[1], yr.at[0]),
            (ys.at[0], yr.at[1]),
            (zs.at[1], zr.at[0]),
            (zs.at[0], zr.at[1]),
        ]

        def copy(d):
            src, dst = pairs[d]
            return pltpu.make_async_remote_copy(
                src_ref=src, dst_ref=dst, send_sem=ss.at[d], recv_sem=rs.at[d],
                device_id=near[d][0], device_id_type=MESH,
            )

        def start():
            for d in range(6):
                @pl.when(near[d][1])
                def _(d=d):
                    copy(d).start()

        def wait():
            for d in range(6):
                @pl.when(near[d][1])
                def _(d=d):
                    copy(d).wait_send()

                @pl.when(near[d][2])
                def _(d=d):
                    copy(d).wait_recv()

        return start, wait

    lane8 = lanes((8, 128))
    lane64 = lanes((64, 128))
    lane32 = lanes((32, 128))

    zero8 = jnp.zeros((8, 128), F32)

    def pack0(carry, plane, x):
        lo, hi = carry
        for t in range(8):
            v = plane[8 * t : 8 * t + 8]
            k = x * 8 + t
            here = lane8 == k
            lo = jnp.where(here, roll(v, k), lo)
            hi = jnp.where(here, roll(v, k + 1), hi)
        return lo, hi

    def z_beside0(plane, x, lo, hi):
        right = jnp.concatenate([roll(hi, 127 - (x * 8 + t)) for t in range(8)], axis=0)
        left = jnp.concatenate([roll(lo, lax.rem(128 - (x * 8 + t), 128)) for t in range(8)], axis=0)
        return (
            jnp.where(lane64 == 127, right, roll(plane, 127)),
            jnp.where(lane64 == 0, left, roll(plane, 1)),
        )

    def keep0(buf, ys, x, plane):
        buf[x + 1, 8:72, :] = plane
        ys[0, pl.ds(x, 1), :] = plane[0:1]
        ys[1, pl.ds(x, 1), :] = plane[63:64]

    def y_in(buf, yr, n, rows):
        def body(x):
            buf[x + 1, 7:8, :] = yr[0, pl.ds(x, 1), :]
            buf[x + 1, 8 + rows : 9 + rows, :] = yr[1, pl.ds(x, 1), :]

        each(n, body)

    def beside0(buf, x, lo, hi):
        c = buf[x + 1, 8:72, :]
        up, down = z_beside0(c, x, lo, hi)
        s = fx[x + 1] * buf[x + 2, 8:72, :] + fx[x] * buf[x, 8:72, :]
        s = s + fy[x, 8:72, :] * buf[x + 1, 9:73, :] + fy[x, 7:71, :] * buf[x + 1, 7:71, :]
        s = s + fzu[x] * up + fzd[x] * down
        return c, s

    def sweep0(src, dst, zr, ys, zs, out):
        lo, hi = zr[0], zr[1]

        def body(x, carry):
            c, s = beside0(src, x, lo, hi)
            new = c * THIRD + w0[x] * (f0[x] + s)
            keep0(dst, ys, x, new)
            if out:
                osol[x] = d0[x] * new
            return pack0(carry, new, x)

        packed = loop(8, body, (zero8, zero8))
        zs[0] = packed[0]
        zs[1] = packed[1]

    for c in loads[:2]:
        c.wait()

    def body(x, carry):
        plane = jnp.where(ph[x] == 1, 1000.0, 1.0).astype(F32) * de[x]
        keep0(rp, rys, x, plane)
        return pack0(carry, plane, x)

    packed = loop(8, body, (zero8, zero8))
    rzs[0] = packed[0]
    rzs[1] = packed[1]

    pl.semaphore_wait(barrier, arrivals)
    start, wait = faces(rp, 8, 64, rys, ryr, rzs, rzr, rss, rrs)
    start()
    both, odd, even, back = maps()
    mb[...] = both
    mo[...] = odd
    me[...] = even
    mt[...] = back
    loads[2].wait()
    wait()

    @pl.when(gx == 0)
    def _():
        rp[0, 8:72, :] = rp[1, 8:72, :]

    @pl.when(gx == nx - 1)
    def _():
        rp[9, 8:72, :] = rp[8, 8:72, :]

    for ok, got, own, s in ((gy == 0, ryr, rys, 0), (gy == ny - 1, ryr, rys, 1), (gz == 0, rzr, rzs, 0), (gz == nz - 1, rzr, rzs, 1)):
        @pl.when(ok)
        def _(got=got, own=own, s=s):
            got[s] = own[s]

    y_in(rp, ryr, 8, 64)
    lo, hi = rzr[0], rzr[1]
    fx[0] = 2.0 / (rp[0, 8:72, :] + rp[1, 8:72, :])

    def body(x, carry):
        c = rp[x + 1, 8:72, :]
        up, down = z_beside0(c, x, lo, hi)
        xu = 2.0 / (c + rp[x + 2, 8:72, :])
        yu = 2.0 / (c + rp[x + 1, 9:73, :])
        zu = 2.0 / (c + up)
        zd = 2.0 / (c + down)
        fx[x + 1] = xu
        fy[x, 8:72, :] = yu
        fy[x, 7:8, :] = 2.0 / (c[0:1] + rp[x + 1, 7:8, :])
        fzu[x] = zu
        fzd[x] = zd
        diag = xu + fx[x] + yu + fy[x, 7:71, :] + zu + zd
        d0[x] = diag
        w = W / diag
        w0[x] = w
        first = w * f0[x]
        keep0(u0.at[0], ys0.at[0], x, first)
        return pack0(carry, first, x)

    packed = loop(8, body, (zero8, zero8))
    zs0[0, 0] = packed[0]
    zs0[0, 1] = packed[1]

    def round0(b):
        return faces(u0.at[b], 8, 64, ys0.at[b], yr0.at[b], zs0.at[b], zr0.at[b], s0s.at[b], r0s.at[b])

    box = [(a, b, c) for a in steps for b in steps for c in steps if (a, b, c) != (0, 0, 0)]

    def box_exchange(pk, zp, rx, ry, rz, ss, rs):
        def copy(a, b, c):
            if c:
                src, dst = zp.at[(c + 1) // 2], rz.at[1 - a, 1 - b, (1 - c) // 2]
            elif b:
                src, dst = pk.at[:, :, pl.ds(24 if b > 0 else 0, 8)], ry.at[1 - a, (1 - b) // 2]
            else:
                src, dst = pk, rx.at[(1 - a) // 2]
            return pltpu.make_async_remote_copy(
                src_ref=src, dst_ref=dst, send_sem=ss.at[a + 1, b + 1, c + 1], recv_sem=rs.at[a + 1, b + 1, c + 1],
                device_id=at(gx + a, b, c), device_id_type=MESH,
            )

        def start():
            for a, b, c in sorted(box, key=lambda o: -sum(map(abs, o))):
                @pl.when(inside(gx, a, nx) & yz_ok(b, c))
                def _(a=a, b=b, c=c):
                    copy(a, b, c).start()

        def wait():
            for a, b, c in box:
                @pl.when(inside(gx, a, nx) & yz_ok(b, c))
                def _(a=a, b=b, c=c):
                    copy(a, b, c).wait_send()

                @pl.when(inside(gx, -a, nx) & yz_ok(-b, -c))
                def _(a=a, b=b, c=c):
                    copy(a, b, c).wait_recv()

        return start, wait

    def pack_box(get, pk, zp, a):
        planes = [get(x) for x in range(4)]
        lo, hi = zero8, zero8
        for i in range(2):
            pk[a, i] = jnp.where(own1, planes[2 * i], roll(planes[2 * i + 1], 64))
        for x in range(4):
            for t in range(4):
                v = planes[x][8 * t : 8 * t + 8]
                k = x * 4 + t
                here = lane8 // 8 == k
                lo = jnp.where(here, roll(v, (8 * k + 96) % 128), lo)
                hi = jnp.where(here, roll(v, (8 * k + 40) % 128), hi)
        zp[0, a] = lo
        zp[1, a] = hi

    def unpack_box(own, rx, ry, rz, a, put):
        for dx in range(3):
            for x in range(4):
                i = x // 2
                turn = (lambda v: roll(v, 64)) if x % 2 else (lambda v: v)
                mid = own(x) if dx == 1 else turn(rx[dx // 2, a, i])
                centre = jnp.concatenate([turn(ry[dx, 0, a, i]), mid, turn(ry[dx, 1, a, i])], axis=0)
                tiles = [(0, 3), (1, 0), (1, 1), (1, 2), (1, 3), (2, 0)]
                left = jnp.concatenate([roll(rz[dx, dy, 0, a], (24 - 8 * (4 * x + t)) % 128) for dy, t in tiles], axis=0)
                right = jnp.concatenate([roll(rz[dx, dy, 1, a], (96 - 8 * (4 * x + t)) % 128) for dy, t in tiles], axis=0)
                out = jnp.where((lane48 >= 96) & (lane48 < 104), right, 0.0)
                out = jnp.where((lane48 >= 32) & (lane48 < 96), centre, out)
                out = jnp.where((lane48 >= 24) & (lane48 < 32), left, out)
                put(4 * dx + x, out)

    lane48 = lanes((48, 128))
    start, wait = round0(0)
    start()

    own1 = (lane32 >= 32) & (lane32 < 96)

    def rows_of(ref, base, n, off):
        return ref[pl.ds(base + off, n, stride=2), :]

    def pair_rows(ref, base, n):
        return rows_of(ref, base, n, 0) + rows_of(ref, base, n, 1)

    for i in range(5):
        t0[0:64, :] = fx[2 * i]
        fx1[i] = mm(pair_rows(t0, 0, 32), mb[...])

    def body(i):
        yu = fy[2 * i, pl.ds(9, 32, stride=2), :] + fy[2 * i + 1, pl.ds(9, 32, stride=2), :]
        yd = fy[2 * i, pl.ds(7, 32, stride=2), :] + fy[2 * i + 1, pl.ds(7, 32, stride=2), :]
        t1[i, 0] = fzu[2 * i] + fzu[2 * i + 1]
        t1[i, 1] = fzd[2 * i] + fzd[2 * i + 1]
        zu = t1[i, 0, pl.ds(0, 32, stride=2), :] + t1[i, 0, pl.ds(1, 32, stride=2), :]
        zd = t1[i, 1, pl.ds(0, 32, stride=2), :] + t1[i, 1, pl.ds(1, 32, stride=2), :]
        yu, yd, zu, zd = mm(yu, mb[...]), mm(yd, mb[...]), mm(zu, mo[...]), mm(zd, me[...])
        fy1u[i] = yu
        fy1d[i] = yd
        fz1u[i] = zu
        fz1d[i] = zd
        diag = fx1[i] + fx1[i + 1] + yu + yd + zu + zd
        d1[i] = jnp.where(own1, diag, 0.0)

    each(4, body)
    parts1 = (lambda x: d1[x], lambda x: fx1[x + 1], lambda x: fy1u[x], lambda x: fz1u[x])
    for a, get in enumerate(parts1):
        pack_box(get, pkc, zpc, a)
    c_start, c_wait = box_exchange(pkc, zpc, rxc, ryc, rzc, s1c, r1c)
    c_start()

    def pack2(planes):
        out = zero8
        for x in range(2):
            for t in range(2):
                g = 2 * x + t
                v = roll(planes[x][8 * t : 8 * t + 8], (32 * g - 48) % 128)
                out = jnp.where((lane8 >= 32 * g) & (lane8 < 32 * g + 32), v, out)
        return out

    xu, yu, zu, dg = [], [], [], []
    for i in range(2):
        t0[0:32, :] = fx1[2 * i]
        t0[32:64, :] = fx1[2 * i + 2]
        t0[64:96, :] = fz1u[2 * i] + fz1u[2 * i + 1]
        t0[96:128, :] = fz1d[2 * i] + fz1d[2 * i + 1]
        t0[128:160, :] = fy1u[2 * i] + fy1u[2 * i + 1]
        t0[160:192, :] = fy1d[2 * i] + fy1d[2 * i + 1]
        xd_, xu_ = mm(pair_rows(t0, 0, 16), mb[...]), mm(pair_rows(t0, 32, 16), mb[...])
        zu_, zd_ = mm(pair_rows(t0, 64, 16), mo[...]), mm(pair_rows(t0, 96, 16), me[...])
        yu_, yd_ = mm(rows_of(t0, 128, 16, 1), mb[...]), mm(rows_of(t0, 160, 16, 0), mb[...])
        xu.append(xu_)
        yu.append(yu_)
        zu.append(zu_)
        dg.append(xu_ + xd_ + yu_ + yd_ + zu_ + zd_)
    for a, planes in enumerate((dg, xu, yu, zu)):
        cc[1, 1, gx, a] = pack2(planes)

    def gather(buf, sx, rx, sn, rn):
        def xcopy(d):
            return pltpu.make_async_remote_copy(
                src_ref=buf.at[1, 1, gx], dst_ref=buf.at[1, 1, gx], send_sem=sx.at[d - 1], recv_sem=rx.at[d - 1],
                device_id={"gx": lax.rem(gx + d, nx)}, device_id_type=MESH,
            )

        def ncopy(d):
            src = buf.at[1, 1] if d < 4 else buf.at[1]
            dst = [buf.at[1, 0], buf.at[1, 2], buf.at[0], buf.at[2]][d - 2]
            return pltpu.make_async_remote_copy(
                src_ref=src, dst_ref=dst, send_sem=sn.at[d - 2], recv_sem=rn.at[d - 2],
                device_id=near[d][0], device_id_type=MESH,
            )

        def xstart():
            for d in range(1, 4):
                xcopy(d).start()

        def xwait():
            for d in range(1, 4):
                pltpu.make_async_remote_copy(
                    src_ref=buf.at[1, 1, gx], dst_ref=buf.at[1, 1, lax.rem(gx + 4 - d, nx)],
                    send_sem=sx.at[d - 1], recv_sem=rx.at[d - 1],
                    device_id={"gx": lax.rem(gx + d, nx)}, device_id_type=MESH,
                ).wait()

        def nstart(ds):
            for d in ds:
                @pl.when(near[d][1])
                def _(d=d):
                    ncopy(d).start()

        def nwait(ds):
            for d in ds:
                @pl.when(near[d][1])
                def _(d=d):
                    ncopy(d).wait_send()

                @pl.when(near[d][2])
                def _(d=d):
                    ncopy(d).wait_recv()

        return (
            xstart, xwait,
            lambda: nstart((2, 3)), lambda: nwait((2, 3)),
            lambda: nstart((4, 5)), lambda: nwait((4, 5)),
        )

    cg = gather(cc, csx, crx, csn, crn)
    cg[0]()

    wait()
    y_in(u0.at[0], yr0.at[0], 8, 64)
    sweep0(u0.at[0], u0.at[1], zr0.at[0], ys0.at[1], zs0.at[1], False)
    start, wait = round0(1)
    start()
    cg[1]()
    cg[2]()
    wait()
    y_in(u0.at[1], yr0.at[1], 8, 64)

    lo, hi = zr0[1, 0], zr0[1, 1]

    def body(i):
        total = None
        for j in range(2):
            x = 2 * i + j
            c, s = beside0(u0.at[1], x, lo, hi)
            r = f0[x] - d0[x] * c + s
            total = r if total is None else total + r
        t1[i, 0] = total
        f1[i] = mm(t1[i, 0, pl.ds(0, 32, stride=2), :] + t1[i, 0, pl.ds(1, 32, stride=2), :], mb[...])

    each(4, body)

    pack_box(lambda x: f1[x], pkf, zpf, 0)
    f_start, f_wait = box_exchange(pkf, zpf, rxf, ryf, rzf, s1f, r1f)
    f_start()
    cg[3]()
    cg[4]()
    c_wait()
    for a, get in enumerate(parts1):
        def put(p, out, a=a):
            ce1[a, p, 8:56, :] = out
            if a == 0:
                ok = out > 0.0
                w1[p] = jnp.where(ok, W / jnp.where(ok, out, 1.0), 0.0)

        unpack_box(get, rxc, ryc, rzc, a, put)

    def zero_rows(ref, n, rows):
        def body(p):
            ref[p, 0:8, :] = zero8
            ref[p, 8 + rows : 16 + rows, :] = zero8

        each(n, body)

    zero_rows(ce1.at[2], 12, 48)
    for b in range(2):
        zero_rows(u1.at[b], 12, 48)
    f_wait()

    def put(p, out):
        f1e[p] = out
        u1[0, p, 8:56, :] = w1[p] * out

    unpack_box(lambda x: f1[x], rxf, ryf, rzf, 0, put)

    def beside1(buf, p, r0, n):
        c = buf[p, r0 : r0 + n, :]
        s = ce1[1, p, r0 : r0 + n, :] * buf[p + 1, r0 : r0 + n, :]
        s = s + ce1[1, p - 1, r0 : r0 + n, :] * buf[p - 1, r0 : r0 + n, :]
        s = s + ce1[2, p, r0 : r0 + n, :] * buf[p, r0 + 1 : r0 + 1 + n, :]
        s = s + ce1[2, p, r0 - 1 : r0 - 1 + n, :] * buf[p, r0 - 1 : r0 - 1 + n, :]
        z = ce1[3, p, r0 : r0 + n, :]
        return c, s + z * roll(c, 127) + roll(z * c, 1)

    def sweep1(src, dst, first, count):
        def body(i):
            p = i + first
            c, s = beside1(u1.at[src], p, 8, 48)
            u1[dst, p, 8:56, :] = c * THIRD + w1[p] * (f1e[p] + s)

        each(count, body)

    sweep1(0, 1, 1, 10)

    src2 = []
    for i in range(2):
        total = None
        for j in range(2):
            x = 2 * i + j
            c, s = beside1(u1.at[1], x + 4, 16, 32)
            r = f1[x] - d1[x] * c + s
            total = r if total is None else total + r
        t0[32 * i : 32 * i + 32, :] = jnp.where(own1, total, 0.0)
        src2.append(mm(pair_rows(t0, 32 * i, 16), mb[...]))
    gg[1, 1, gx] = pack2(src2)

    def fcopy(d, sy, sz):
        return pltpu.make_async_remote_copy(
            src_ref=gg.at[1, 1, gx], dst_ref=gg.at[1 - sz, 1 - sy, gx],
            send_sem=gs.at[d, sy + 1, sz + 1], recv_sem=gr.at[d, sy + 1, sz + 1],
            device_id=at(lax.rem(gx + d, nx), sy, sz), device_id_type=MESH,
        )

    def fback(d, sy, sz):
        return pltpu.make_async_remote_copy(
            src_ref=gg.at[1, 1, gx], dst_ref=gg.at[1 - sz, 1 - sy, lax.rem(gx + 4 - d, nx)],
            send_sem=gs.at[d, sy + 1, sz + 1], recv_sem=gr.at[d, sy + 1, sz + 1],
            device_id=at(lax.rem(gx + d, nx), sy, sz), device_id_type=MESH,
        )

    order = sorted([(sy, sz) for sy in steps for sz in steps], key=lambda o: -abs(o[0]) - abs(o[1]))

    def g_start():
        for sy, sz in order:
            @pl.when(yz_ok(sy, sz))
            def _(sy=sy, sz=sz):
                for d in (2, 1, 3, 0):
                    if (d, sy, sz) != (0, 0, 0):
                        fcopy(d, sy, sz).start()

    def g_wait():
        for sy, sz in order:
            @pl.when(yz_ok(sy, sz))
            def _(sy=sy, sz=sz):
                for d in range(4):
                    if (d, sy, sz) != (0, 0, 0):
                        fcopy(d, sy, sz).wait_send()

            @pl.when(yz_ok(-sy, -sz))
            def _(sy=sy, sz=sz):
                for d in range(4):
                    if (d, sy, sz) != (0, 0, 0):
                        fback(d, sy, sz).wait_recv()

    g_start()
    cg[5]()

    def spread2(get, put):
        def body(b):
            for y in range(3):
                v = [get(z, y, b) for z in range(3)]
                for x in range(2):
                    for t in range(2):
                        g = 2 * x + t
                        left = roll(v[0], (16 - 32 * g) % 128)
                        mid = roll(v[1], (48 - 32 * g) % 128)
                        right = roll(v[2], (80 - 32 * g) % 128)
                        out = jnp.where(lane8 < 48, left, jnp.where(lane8 < 80, mid, right))
                        out = jnp.where((lane8 >= 16) & (lane8 < 112), out, 0.0)
                        put(2 * b + x, 16 * y + 8 * t, out)

        each(4, body)

    def put_d(p, r, v):
        d2[p, r : r + 8, :] = v
        ok = v > 0.0
        w2[p, r : r + 8, :] = jnp.where(ok, W / jnp.where(ok, v, 1.0), 0.0)

    def put_x(p, r, v):
        fx2[p + 1, r : r + 8, :] = v

    def put_y(p, r, v):
        fy2[p, 8 + r : 16 + r, :] = v

    def put_z(p, r, v):
        fz2[p, r : r + 8, :] = v

    def put_f(p, r, v):
        f2[p, r : r + 8, :] = v
        u2[0, p + 2, 8 + r : 16 + r, :] = w2[p, r : r + 8, :] * v

    for a, put in enumerate((put_d, put_x, put_y, put_z)):
        spread2(lambda z, y, b, a=a: cc[z, y, b, a], put)
    fx2[0] = jnp.zeros((48, 128), F32)
    fx3[0] = jnp.zeros((24, 128), F32)

    zero_rows(fy2, 8, 48)
    zero_rows(fy3, 4, 24)
    for b in range(2):
        zero_rows(u2.at[b], 12, 48)
        zero_rows(u3.at[b], 6, 24)
        for p in (0, 1, 10, 11):
            u2[b, p, 8:56, :] = jnp.zeros((48, 128), F32)
        for p in (0, 5):
            u3[b, p, 8:32, :] = jnp.zeros((24, 128), F32)

    row48 = lax.broadcasted_iota(jnp.int32, (48, 128), 0)

    def body(p):
        a, b = 2 * p, 2 * p + 1
        t5[p, 0] = fx2[b + 1]
        t5[p, 1] = fz2[a] + fz2[b]
        ysum = fy2[a, 8:56, :] + fy2[b, 8:56, :]
        t5[p, 2] = ysum
        inner = fx2[a + 1]
        inner = inner + jnp.where(row48 % 2 == 0, ysum, 0.0)
        inner = inner + jnp.where(lane48 % 2 == 0, fz2[a] + fz2[b], 0.0)
        t5[p, 3] = d2[a] + d2[b] - 2.0 * inner
        pick = lambda q, off: t5[p, q, pl.ds(off, 24, stride=2), :]
        fx3[p + 1] = mm(pick(0, 0) + pick(0, 1), mb[...])
        fz3[p] = mm(pick(1, 0) + pick(1, 1), mo[...])
        fy3[p, 8:32, :] = mm(pick(2, 1), mb[...])
        diag = mm(pick(3, 0) + pick(3, 1), mb[...])
        ok = diag > 0.0
        w3[p] = jnp.where(ok, W / jnp.where(ok, diag, 1.0), 0.0)

    each(4, body)

    g_wait()
    spread2(lambda z, y, b: gg[z, y, b], put_f)

    def beside(buf, fxr, fyr, fzr, p, rows):
        c = buf[p + 1, 8 : 8 + rows, :]
        s = fxr[p + 1] * buf[p + 2, 8 : 8 + rows, :] + fxr[p] * buf[p, 8 : 8 + rows, :]
        s = s + fyr[p, 8 : 8 + rows, :] * buf[p + 1, 9 : 9 + rows, :]
        s = s + fyr[p, 7 : 7 + rows, :] * buf[p + 1, 7 : 7 + rows, :]
        z = fzr[p]
        return c, s + z * roll(c, 127) + roll(z * c, 1)

    def sweep2(src, dst):
        def body(p):
            c, s = beside(u2.at[src, pl.ds(1, 10)], fx2, fy2, fz2, p, 48)
            u2[dst, p + 2, 8:56, :] = c * THIRD + w2[p] * (f2[p] + s)

        each(8, body)

    def sweep3(src, dst):
        def body(p):
            c, s = beside(u3.at[src], fx3, fy3, fz3, p, 24)
            u3[dst, p + 1, 8:32, :] = c * THIRD + w3[p] * (f3[p] + s)

        each(4, body)

    sweep2(0, 1)

    def body(p):
        total = None
        for j in range(2):
            c, s = beside(u2.at[1, pl.ds(1, 10)], fx2, fy2, fz2, 2 * p + j, 48)
            r = f2[2 * p + j] - d2[2 * p + j] * c + s
            total = r if total is None else total + r
        t5[p, 0] = total
        src = mm(t5[p, 0, pl.ds(0, 24, stride=2), :] + t5[p, 0, pl.ds(1, 24, stride=2), :], mb[...])
        f3[p] = src
        u3[0, p + 1, 8:32, :] = w3[p] * src

    each(4, body)
    sweep3(0, 1)
    sweep3(1, 0)
    sweep3(0, 1)

    def body(p):
        e = mm(u3[1, p + 1, 8:32, :], mt[...])
        t5[p, 1, pl.ds(0, 24, stride=2), :] = e
        t5[p, 1, pl.ds(1, 24, stride=2), :] = e
        wide = t5[p, 1]
        for j in range(2):
            q = 2 * p + j
            u2[0, q + 2, 8:56, :] = u2[1, q + 2, 8:56, :] + jnp.where(d2[q] > 0.0, wide, 0.0)

    each(4, body)
    sweep2(0, 1)
    sweep2(1, 0)

    def body(q):
        e = mm(u2[0, 2 * gx + q, 20:44, :], mt[...])
        t2[q, pl.ds(0, 24, stride=2), :] = e
        t2[q, pl.ds(1, 24, stride=2), :] = e

    each(6, body)

    def body(i):
        p = i + 1
        u1[0, p, 8:56, :] = u1[1, p, 8:56, :] + jnp.where(w1[p] > 0.0, t2[p // 2], 0.0)

    each(10, body)
    sweep1(0, 1, 2, 8)
    sweep1(1, 0, 3, 6)

    def body(q):
        c = u1[0, q + 3, 12:52, :]
        e = mm(c, mt[...])
        t3[q, pl.ds(0, 40, stride=2), :] = e
        t3[q, pl.ds(1, 40, stride=2), :] = e
        t4[q, pl.ds(0, 40, stride=2), :] = c
        t4[q, pl.ds(1, 40, stride=2), :] = c

    each(6, body)

    def body(p):
        u0[0, p, :, :] = u0[1, p, :, :] + t3[(p + 1) // 2]

    each(10, body)

    def body(q, carry):
        lo, hi = carry
        for t in range(8):
            v = t4[q + 1, 8 + 8 * t : 16 + 8 * t, :]
            k = 16 * q + t
            here = (lane8 == k) | (lane8 == k + 8)
            a, b = roll(v, lax.rem(k + 97, 128)), roll(v, lax.rem(k + 32, 128))
            lo = jnp.where(lane8 == k, a, jnp.where(lane8 == k + 8, roll(a, 8), lo))
            hi = jnp.where(lane8 == k, b, jnp.where(lane8 == k + 8, roll(b, 8), hi))
        return lo, hi

    lo, hi = loop(4, body, (zero8, zero8))
    zr0[0, 0] = zr0[1, 0] + lo
    zr0[0, 1] = zr0[1, 1] + hi
    sweep0(u0.at[0], u0.at[2], zr0.at[0], ys0.at[2], zs0.at[2], False)
    start, wait = round0(2)
    start()
    wait()
    y_in(u0.at[2], yr0.at[2], 8, 64)
    sweep0(u0.at[2], u0.at[0], zr0.at[2], ys0.at[0], zs0.at[0], True)

    start, wait = round0(0)
    start()
    out0 = pltpu.make_async_copy(osol, os_h.at[0], out_sem.at[0])
    out0.start()
    wait()
    y_in(u0.at[0], yr0.at[0], 8, 64)
    lo, hi = zr0[0, 0], zr0[0, 1]

    def body(x):
        c, s = beside0(u0.at[0], x, lo, hi)
        ores[x] = f0[x] - d0[x] * c + s

    each(8, body)
    out1 = pltpu.make_async_copy(ores, or_h.at[0], out_sem.at[1])
    out1.start()
    out0.wait()
    out1.wait()


def on_device(phase, density, rhs):
    V = lambda *s: pltpu.VMEM(s, F32)
    M = pltpu.VMEM((384, 128), BF16)
    D = lambda *s: pltpu.SemaphoreType.DMA(s)
    scratch = [
        pltpu.VMEM((8, 64, 128), jnp.int32), V(8, 64, 128), V(8, 64, 128), V(10, 80, 128), V(3, 10, 80, 128),
        V(9, 64, 128), V(8, 80, 128), V(8, 64, 128), V(8, 64, 128), V(8, 64, 128), V(8, 64, 128),
        V(2, 8, 128), V(2, 8, 128), V(2, 8, 128), V(2, 8, 128),
        V(3, 2, 8, 128), V(3, 2, 8, 128), V(3, 2, 8, 128), V(3, 2, 8, 128),
        V(2, 12, 64, 128), V(4, 32, 128), V(5, 32, 128), V(4, 32, 128), V(4, 32, 128), V(4, 32, 128), V(4, 32, 128),
        V(4, 32, 128), V(12, 48, 128), V(4, 12, 64, 128),
        V(4, 2, 32, 128), V(2, 4, 8, 128), V(2, 4, 2, 32, 128), V(3, 2, 4, 2, 8, 128), V(3, 3, 2, 4, 8, 128),
        V(1, 2, 32, 128), V(2, 1, 8, 128), V(2, 1, 2, 32, 128), V(3, 2, 1, 2, 8, 128), V(3, 3, 2, 1, 8, 128),
        M, M, M, M, V(256, 128), V(4, 2, 64, 128), V(6, 48, 128), V(6, 80, 128), V(6, 80, 128), V(4, 4, 48, 128),
        V(12, 48, 128),
        V(3, 3, 4, 4, 8, 128), V(3, 3, 4, 8, 128),
        V(8, 48, 128), V(2, 12, 64, 128), V(9, 48, 128), V(8, 64, 128), V(8, 48, 128), V(8, 48, 128), V(8, 48, 128),
        V(4, 24, 128), V(2, 6, 40, 128), V(5, 24, 128), V(4, 40, 128), V(4, 24, 128), V(4, 24, 128),
        V(8, 64, 128), V(8, 64, 128),
        D(3), D(2), D(6), D(6), D(3, 6), D(3, 6), D(3, 3, 3), D(3, 3, 3), D(3, 3, 3), D(3, 3, 3),
        D(3), D(3), D(4), D(4), D(4, 3, 3), D(4, 3, 3),
    ]
    shape = jax.ShapeDtypeStruct(rhs.shape, F32)
    return pl.pallas_call(
        kernel,
        out_shape=(shape, shape),
        in_specs=[pl.BlockSpec(memory_space=pl.ANY)] * 3,
        out_specs=(pl.BlockSpec(memory_space=pl.ANY),) * 2,
        scratch_shapes=scratch,
        compiler_params=pltpu.CompilerParams(collective_id=0, has_side_effects=True),
        name="vcycle",
    )(phase, density, rhs)


def solution(mesh):
    in_specs = (P("gx", "gy", "gz"), P("gx", "gy", "gz"), P(None, "gx", "gy", "gz"))
    out_specs = (P(None, "gx", "gy", "gz"), P(None, "gx", "gy", "gz"))
    return jax.shard_map(on_device, mesh=mesh, in_specs=in_specs, out_specs=out_specs, check_vma=False)
```

```python
import functools

import jax
import jax.numpy as jnp
from jax import lax
from jax.experimental import pallas as pl
from jax.experimental.pallas import tpu as pltpu
from jax.sharding import PartitionSpec as P

MESH = pl.DeviceIdType.MESH
F32 = jnp.float32
W = 2.0 / 3.0
THIRD = 1.0 / 3.0
BF16 = jnp.bfloat16


def lanes(shape):
    return lax.broadcasted_iota(jnp.int32, shape, len(shape) - 1)


def roll(v, shift):
    return pltpu.roll(v, shift, 1)


def loop(count, body, init=0):
    return lax.fori_loop(0, count, body, init, unroll=True)


def each(count, body):
    def step(i, carry):
        body(i)
        return carry

    lax.fori_loop(0, count, step, 0, unroll=True)


def maps():
    row = lax.broadcasted_iota(jnp.int32, (128, 128), 0)
    col = lax.broadcasted_iota(jnp.int32, (128, 128), 1)
    hit = col == 32 + row // 2
    both = jnp.where(hit, 1.0, 0.0)
    odd = jnp.where(hit & (row % 2 == 1), 1.0, 0.0)
    even = jnp.where(hit & (row % 2 == 0), 1.0, 0.0)
    back = jnp.where(row == 32 + col // 2, 1.0, 0.0)
    return [jnp.concatenate([m.astype(BF16)] * 3, axis=0) for m in (both, odd, even, back)]


def mm(a, b):
    hi = a.astype(BF16)
    rest = a - hi.astype(F32)
    mid = rest.astype(BF16)
    low = (rest - mid.astype(F32)).astype(BF16)
    return lax.dot(jnp.concatenate([hi, mid, low], axis=1), b, preferred_element_type=F32)


def kernel(
    ph_h, de_h, rh_h, os_h, or_h,
    ph, de, f0, rp, u0, fx, fy, fzu, fzd, w0, d0,
    rys, ryr, rzs, rzr, ys0, yr0, zs0, zr0,
    u1, f1, fx1, fy1u, fy1d, fz1u, fz1d, d1, w1, ce1,
    pkc, xyc, zpc, yzc, rxc, ryc, rzc, rec, pkf, xyf, zpf, yzf, rxf, ryf, rzf, ref_,
    mb, mo, me, mt, t0, t1, t2, t3, t4, t5, f1e,
    cc, gg,
    f2, u2, fx2, fy2, fz2, w2, d2,
    f3, u3, fx3, fy3, fz3, w3,
    osol, ores,
    in_sem, out_sem, rss, rrs, s0s, r0s, s1c, r1c, s1f, r1f, csx, crx, csn, crn, gs, gr,
):
    gx, gy, gz = lax.axis_index("gx"), lax.axis_index("gy"), lax.axis_index("gz")
    nx, ny, nz = lax.axis_size("gx"), lax.axis_size("gy"), lax.axis_size("gz")
    near = [
        ({"gx": gx + 1}, gx < nx - 1, gx > 0),
        ({"gx": gx - 1}, gx > 0, gx < nx - 1),
        ({"gy": gy + 1}, gy < ny - 1, gy > 0),
        ({"gy": gy - 1}, gy > 0, gy < ny - 1),
        ({"gz": gz + 1}, gz < nz - 1, gz > 0),
        ({"gz": gz - 1}, gz > 0, gz < nz - 1),
    ]

    loads = [
        pltpu.make_async_copy(ph_h, ph, in_sem.at[0]),
        pltpu.make_async_copy(de_h, de, in_sem.at[1]),
        pltpu.make_async_copy(rh_h.at[0], f0, in_sem.at[2]),
    ]
    for c in loads:
        c.start()

    edge = (gx == 0) | (gx == nx - 1) | (gy == 0) | (gy == ny - 1) | (gz == 0) | (gz == nz - 1)

    @pl.when(edge)
    def _():
        for ref in (ryc, rzc, rec):
            ref[...] = jnp.zeros(ref.shape, F32)

    barrier = pltpu.get_barrier_semaphore()
    arrivals = 0
    for where, ok, back in near:
        arrivals = arrivals + jnp.where(back, 1, 0)

        @pl.when(ok)
        def _(where=where):
            pl.semaphore_signal(barrier, inc=1, device_id=where, device_id_type=MESH)

    for b in range(3):
        for x in (0, 9):
            u0[b, x, 8:72, :] = jnp.zeros((64, 128), F32)
        for ref in (yr0, zr0):
            for k in range(2):
                ref[b, k] = jnp.zeros((8, 128), F32)

    @pl.when(edge)
    def _():
        for ref in (gg, rxc, rxf, ryf, rzf, ref_):
            ref[...] = jnp.zeros(ref.shape, F32)
        for z in range(3):
            for y in range(3):
                if (z, y) != (1, 1):
                    cc[z, y] = jnp.zeros(cc.shape[2:], F32)

    def inside(at, step, count):
        return (at >= 0) if step == 0 else (at < count - 1) if step > 0 else (at > 0)

    def yz_ok(sy, sz):
        return inside(gy, sy, ny) & inside(gz, sz, nz)

    def at(sx, sy, sz):
        return {"gx": sx, "gy": gy + sy, "gz": gz + sz}

    steps = (-1, 0, 1)

    def faces(buf, n, rows, ys, yr, zs, zr, ss, rs):
        body = pl.ds(8, rows)
        pairs = [
            (buf.at[n, body], buf.at[0, body]),
            (buf.at[1, body], buf.at[n + 1, body]),
            (ys.at[1], yr.at[0]),
            (ys.at[0], yr.at[1]),
            (zs.at[1], zr.at[0]),
            (zs.at[0], zr.at[1]),
        ]

        def copy(d):
            src, dst = pairs[d]
            return pltpu.make_async_remote_copy(
                src_ref=src, dst_ref=dst, send_sem=ss.at[d], recv_sem=rs.at[d],
                device_id=near[d][0], device_id_type=MESH,
            )

        def start():
            for d in range(6):
                @pl.when(near[d][1])
                def _(d=d):
                    copy(d).start()

        def wait():
            for d in range(6):
                @pl.when(near[d][1])
                def _(d=d):
                    copy(d).wait_send()

                @pl.when(near[d][2])
                def _(d=d):
                    copy(d).wait_recv()

        return start, wait

    lane8 = lanes((8, 128))
    lane64 = lanes((64, 128))
    lane32 = lanes((32, 128))

    zero8 = jnp.zeros((8, 128), F32)

    def pack0(carry, plane, x):
        lo, hi = carry
        for t in range(8):
            v = plane[8 * t : 8 * t + 8]
            k = x * 8 + t
            here = lane8 == k
            lo = jnp.where(here, roll(v, k), lo)
            hi = jnp.where(here, roll(v, k + 1), hi)
        return lo, hi

    def z_beside0(plane, x, lo, hi):
        right = jnp.concatenate([roll(hi, 127 - (x * 8 + t)) for t in range(8)], axis=0)
        left = jnp.concatenate([roll(lo, lax.rem(128 - (x * 8 + t), 128)) for t in range(8)], axis=0)
        return (
            jnp.where(lane64 == 127, right, roll(plane, 127)),
            jnp.where(lane64 == 0, left, roll(plane, 1)),
        )

    def keep0(buf, ys, x, plane):
        buf[x + 1, 8:72, :] = plane
        ys[0, pl.ds(x, 1), :] = plane[0:1]
        ys[1, pl.ds(x, 1), :] = plane[63:64]

    def y_in(buf, yr, n, rows):
        def body(x):
            buf[x + 1, 7:8, :] = yr[0, pl.ds(x, 1), :]
            buf[x + 1, 8 + rows : 9 + rows, :] = yr[1, pl.ds(x, 1), :]

        each(n, body)

    def beside0(buf, x, lo, hi):
        c = buf[x + 1, 8:72, :]
        up, down = z_beside0(c, x, lo, hi)
        s = fx[x + 1] * buf[x + 2, 8:72, :] + fx[x] * buf[x, 8:72, :]
        s = s + fy[x, 8:72, :] * buf[x + 1, 9:73, :] + fy[x, 7:71, :] * buf[x + 1, 7:71, :]
        s = s + fzu[x] * up + fzd[x] * down
        return c, s

    def sweep0(src, dst, zr, ys, zs, out):
        lo, hi = zr[0], zr[1]

        def body(x, carry):
            c, s = beside0(src, x, lo, hi)
            new = c * THIRD + w0[x] * (f0[x] + s)
            keep0(dst, ys, x, new)
            if out:
                osol[x] = d0[x] * new
            return pack0(carry, new, x)

        packed = loop(8, body, (zero8, zero8))
        zs[0] = packed[0]
        zs[1] = packed[1]

    for c in loads[:2]:
        c.wait()

    def body(x, carry):
        plane = jnp.where(ph[x] == 1, 1000.0, 1.0).astype(F32) * de[x]
        keep0(rp, rys, x, plane)
        return pack0(carry, plane, x)

    packed = loop(8, body, (zero8, zero8))
    rzs[0] = packed[0]
    rzs[1] = packed[1]

    pl.semaphore_wait(barrier, arrivals)
    start, wait = faces(rp, 8, 64, rys, ryr, rzs, rzr, rss, rrs)
    start()
    both, odd, even, back = maps()
    mb[...] = both
    mo[...] = odd
    me[...] = even
    mt[...] = back
    loads[2].wait()
    wait()

    @pl.when(gx == 0)
    def _():
        rp[0, 8:72, :] = rp[1, 8:72, :]

    @pl.when(gx == nx - 1)
    def _():
        rp[9, 8:72, :] = rp[8, 8:72, :]

    for ok, got, own, s in ((gy == 0, ryr, rys, 0), (gy == ny - 1, ryr, rys, 1), (gz == 0, rzr, rzs, 0), (gz == nz - 1, rzr, rzs, 1)):
        @pl.when(ok)
        def _(got=got, own=own, s=s):
            got[s] = own[s]

    y_in(rp, ryr, 8, 64)
    lo, hi = rzr[0], rzr[1]
    fx[0] = 2.0 / (rp[0, 8:72, :] + rp[1, 8:72, :])

    def body(x, carry):
        c = rp[x + 1, 8:72, :]
        up, down = z_beside0(c, x, lo, hi)
        xu = 2.0 / (c + rp[x + 2, 8:72, :])
        yu = 2.0 / (c + rp[x + 1, 9:73, :])
        zu = 2.0 / (c + up)
        zd = 2.0 / (c + down)
        fx[x + 1] = xu
        fy[x, 8:72, :] = yu
        fy[x, 7:8, :] = 2.0 / (c[0:1] + rp[x + 1, 7:8, :])
        fzu[x] = zu
        fzd[x] = zd
        diag = xu + fx[x] + yu + fy[x, 7:71, :] + zu + zd
        d0[x] = diag
        w = W / diag
        w0[x] = w
        first = w * f0[x]
        keep0(u0.at[0], ys0.at[0], x, first)
        return pack0(carry, first, x)

    packed = loop(8, body, (zero8, zero8))
    zs0[0, 0] = packed[0]
    zs0[0, 1] = packed[1]

    def round0(b):
        return faces(u0.at[b], 8, 64, ys0.at[b], yr0.at[b], zs0.at[b], zr0.at[b], s0s.at[b], r0s.at[b])

    box = [(a, b, c) for a in steps for b in steps for c in steps if (a, b, c) != (0, 0, 0)]

    def box_exchange(pk, xy, zp, yz, rx, ry, rz, re, ss, rs):
        def copy(a, b, c):
            if b and c:
                src, dst = yz.at[(b + 1) // 2, (c + 1) // 2], re.at[1 - a, (1 - b) // 2, (1 - c) // 2]
            elif c:
                src, dst = zp.at[(c + 1) // 2], rz.at[1 - a, (1 - c) // 2]
            elif b:
                src, dst = xy.at[(b + 1) // 2], ry.at[1 - a, (1 - b) // 2]
            else:
                src, dst = pk, rx.at[(1 - a) // 2]
            return pltpu.make_async_remote_copy(
                src_ref=src, dst_ref=dst, send_sem=ss.at[a + 1, b + 1, c + 1], recv_sem=rs.at[a + 1, b + 1, c + 1],
                device_id=at(gx + a, b, c), device_id_type=MESH,
            )

        def start(far=(1, 2, 3)):
            for n in sorted(far, reverse=True):
                for a, b, c in box:
                    if abs(a) + abs(b) + abs(c) == n:
                        @pl.when(inside(gx, a, nx) & yz_ok(b, c))
                        def _(a=a, b=b, c=c):
                            copy(a, b, c).start()

        def wait():
            for a, b, c in box:
                @pl.when(inside(gx, a, nx) & yz_ok(b, c))
                def _(a=a, b=b, c=c):
                    copy(a, b, c).wait_send()

                @pl.when(inside(gx, -a, nx) & yz_ok(-b, -c))
                def _(a=a, b=b, c=c):
                    copy(a, b, c).wait_recv()

        return start, wait

    row8 = lax.broadcasted_iota(jnp.int32, (8, 128), 0)

    def half(v):
        return pltpu.roll(v, 4, 0)

    def pack_box(gets, pk, xy, zp, yz):
        edge = {(b, c): zero8 for b in range(2) for c in range(2)}
        for a, get in enumerate(gets):
            planes = [get(x) for x in range(4)]
            pairs = [jnp.where(own1, planes[2 * i], roll(planes[2 * i + 1], 64)) for i in range(2)]
            for i in range(2):
                pk[a, i] = pairs[i]
            xy[0, a] = jnp.where(row8 < 4, pairs[0][0:8], half(pairs[1][0:8]))
            xy[1, a] = jnp.where(row8 >= 4, pairs[0][24:32], half(pairs[1][24:32]))
            face = [zero8, zero8]
            for x in range(4):
                for t in range(4):
                    v = planes[x][8 * t : 8 * t + 8]
                    k = x * 4 + t
                    for c, first in ((0, 96), (1, 40)):
                        face[c] = jnp.where(lane8 // 8 == k, roll(v, (8 * k + first) % 128), face[c])
                        if t in (0, 3):
                            b = t // 3
                            edge[b, c] = jnp.where(lane8 // 8 == 4 * a + x, roll(v, (32 * a + 8 * x + first) % 128), edge[b, c])
            zp[0, a] = face[0]
            zp[1, a] = face[1]
        for b in range(2):
            for c in range(2):
                yz[b, c] = edge[b, c]

    def unpack_box(own, rx, ry, rz, re, a, put):
        def side(dx, x, c, first):
            def corner(b):
                return roll(re[dx, b, c], (first - 32 * a - 8 * x) % 128)

            mid = [roll(rz[dx, c, a], (first - 8 * (4 * x + t)) % 128) for t in range(4)]
            return jnp.concatenate([corner(0)] + mid + [corner(1)], axis=0)

        for dx in range(3):
            for x in range(4):
                i = x // 2
                turn = (lambda v: roll(v, 64)) if x % 2 else (lambda v: v)
                flip = half if i else (lambda v: v)
                mid = own(x) if dx == 1 else turn(rx[dx // 2, a, i])
                centre = jnp.concatenate([turn(flip(ry[dx, 0, a])), mid, turn(flip(ry[dx, 1, a]))], axis=0)
                out = jnp.where((lane48 >= 96) & (lane48 < 104), side(dx, x, 1, 96), 0.0)
                out = jnp.where((lane48 >= 32) & (lane48 < 96), centre, out)
                out = jnp.where((lane48 >= 24) & (lane48 < 32), side(dx, x, 0, 24), out)
                put(4 * dx + x, out)

    lane48 = lanes((48, 128))
    start, wait = round0(0)
    start()

    own1 = (lane32 >= 32) & (lane32 < 96)

    def rows_of(ref, base, n, off):
        return ref[pl.ds(base + off, n, stride=2), :]

    def pair_rows(ref, base, n):
        return rows_of(ref, base, n, 0) + rows_of(ref, base, n, 1)

    for i in range(5):
        t0[0:64, :] = fx[2 * i]
        fx1[i] = mm(pair_rows(t0, 0, 32), mb[...])

    def body(i):
        yu = fy[2 * i, pl.ds(9, 32, stride=2), :] + fy[2 * i + 1, pl.ds(9, 32, stride=2), :]
        yd = fy[2 * i, pl.ds(7, 32, stride=2), :] + fy[2 * i + 1, pl.ds(7, 32, stride=2), :]
        t1[i, 0] = fzu[2 * i] + fzu[2 * i + 1]
        t1[i, 1] = fzd[2 * i] + fzd[2 * i + 1]
        zu = t1[i, 0, pl.ds(0, 32, stride=2), :] + t1[i, 0, pl.ds(1, 32, stride=2), :]
        zd = t1[i, 1, pl.ds(0, 32, stride=2), :] + t1[i, 1, pl.ds(1, 32, stride=2), :]
        yu, yd, zu, zd = mm(yu, mb[...]), mm(yd, mb[...]), mm(zu, mo[...]), mm(zd, me[...])
        fy1u[i] = yu
        fy1d[i] = yd
        fz1u[i] = zu
        fz1d[i] = zd
        diag = fx1[i] + fx1[i + 1] + yu + yd + zu + zd
        d1[i] = jnp.where(own1, diag, 0.0)

    each(4, body)
    parts1 = (lambda x: d1[x], lambda x: fx1[x + 1], lambda x: fy1u[x], lambda x: fz1u[x])
    pack_box(parts1, pkc, xyc, zpc, yzc)
    c_start, c_wait = box_exchange(pkc, xyc, zpc, yzc, rxc, ryc, rzc, rec, s1c, r1c)
    c_start((1, 2))

    def pack2(planes):
        out = zero8
        for x in range(2):
            for t in range(2):
                g = 2 * x + t
                v = roll(planes[x][8 * t : 8 * t + 8], (32 * g - 48) % 128)
                out = jnp.where((lane8 >= 32 * g) & (lane8 < 32 * g + 32), v, out)
        return out

    xu, yu, zu, dg = [], [], [], []
    for i in range(2):
        t0[0:32, :] = fx1[2 * i]
        t0[32:64, :] = fx1[2 * i + 2]
        t0[64:96, :] = fz1u[2 * i] + fz1u[2 * i + 1]
        t0[96:128, :] = fz1d[2 * i] + fz1d[2 * i + 1]
        t0[128:160, :] = fy1u[2 * i] + fy1u[2 * i + 1]
        t0[160:192, :] = fy1d[2 * i] + fy1d[2 * i + 1]
        xd_, xu_ = mm(pair_rows(t0, 0, 16), mb[...]), mm(pair_rows(t0, 32, 16), mb[...])
        zu_, zd_ = mm(pair_rows(t0, 64, 16), mo[...]), mm(pair_rows(t0, 96, 16), me[...])
        yu_, yd_ = mm(rows_of(t0, 128, 16, 1), mb[...]), mm(rows_of(t0, 160, 16, 0), mb[...])
        xu.append(xu_)
        yu.append(yu_)
        zu.append(zu_)
        dg.append(xu_ + xd_ + yu_ + yd_ + zu_ + zd_)
    for a, planes in enumerate((dg, xu, yu, zu)):
        cc[1, 1, gx, a] = pack2(planes)

    def gather(buf, sx, rx, sn, rn):
        def xcopy(d):
            return pltpu.make_async_remote_copy(
                src_ref=buf.at[1, 1, gx], dst_ref=buf.at[1, 1, gx], send_sem=sx.at[d - 1], recv_sem=rx.at[d - 1],
                device_id={"gx": lax.rem(gx + d, nx)}, device_id_type=MESH,
            )

        def ncopy(d):
            src = buf.at[1, 1] if d < 4 else buf.at[1]
            dst = [buf.at[1, 0], buf.at[1, 2], buf.at[0], buf.at[2]][d - 2]
            return pltpu.make_async_remote_copy(
                src_ref=src, dst_ref=dst, send_sem=sn.at[d - 2], recv_sem=rn.at[d - 2],
                device_id=near[d][0], device_id_type=MESH,
            )

        def xstart():
            for d in range(1, 4):
                xcopy(d).start()

        def xwait():
            for d in range(1, 4):
                pltpu.make_async_remote_copy(
                    src_ref=buf.at[1, 1, gx], dst_ref=buf.at[1, 1, lax.rem(gx + 4 - d, nx)],
                    send_sem=sx.at[d - 1], recv_sem=rx.at[d - 1],
                    device_id={"gx": lax.rem(gx + d, nx)}, device_id_type=MESH,
                ).wait()

        def nstart(ds):
            for d in ds:
                @pl.when(near[d][1])
                def _(d=d):
                    ncopy(d).start()

        def nwait(ds):
            for d in ds:
                @pl.when(near[d][1])
                def _(d=d):
                    ncopy(d).wait_send()

                @pl.when(near[d][2])
                def _(d=d):
                    ncopy(d).wait_recv()

        return (
            xstart, xwait,
            lambda: nstart((2, 3)), lambda: nwait((2, 3)),
            lambda: nstart((4, 5)), lambda: nwait((4, 5)),
        )

    cg = gather(cc, csx, crx, csn, crn)

    wait()
    y_in(u0.at[0], yr0.at[0], 8, 64)
    sweep0(u0.at[0], u0.at[1], zr0.at[0], ys0.at[1], zs0.at[1], False)
    start, wait = round0(1)
    start()
    c_start((3,))
    cg[0]()
    wait()
    y_in(u0.at[1], yr0.at[1], 8, 64)

    lo, hi = zr0[1, 0], zr0[1, 1]

    def body(i):
        total = None
        for j in range(2):
            x = 2 * i + j
            c, s = beside0(u0.at[1], x, lo, hi)
            r = f0[x] - d0[x] * c + s
            total = r if total is None else total + r
        t1[i, 0] = total
        f1[i] = mm(t1[i, 0, pl.ds(0, 32, stride=2), :] + t1[i, 0, pl.ds(1, 32, stride=2), :], mb[...])

    each(4, body)

    pack_box([lambda x: f1[x]], pkf, xyf, zpf, yzf)
    f_start, f_wait = box_exchange(pkf, xyf, zpf, yzf, rxf, ryf, rzf, ref_, s1f, r1f)
    f_start()
    cg[1]()
    cg[2]()
    c_wait()
    for a, get in enumerate(parts1):
        def put(p, out, a=a):
            ce1[a, p, 8:56, :] = out
            if a == 0:
                ok = out > 0.0
                w1[p] = jnp.where(ok, W / jnp.where(ok, out, 1.0), 0.0)

        unpack_box(get, rxc, ryc, rzc, rec, a, put)

    def zero_rows(ref, n, rows):
        def body(p):
            ref[p, 0:8, :] = zero8
            ref[p, 8 + rows : 16 + rows, :] = zero8

        each(n, body)

    zero_rows(ce1.at[2], 12, 48)
    for b in range(2):
        zero_rows(u1.at[b], 12, 48)
    f_wait()
    cg[3]()
    cg[4]()

    def put(p, out):
        f1e[p] = out
        u1[0, p, 8:56, :] = w1[p] * out

    unpack_box(lambda x: f1[x], rxf, ryf, rzf, ref_, 0, put)

    def beside1(buf, p, r0, n):
        c = buf[p, r0 : r0 + n, :]
        s = ce1[1, p, r0 : r0 + n, :] * buf[p + 1, r0 : r0 + n, :]
        s = s + ce1[1, p - 1, r0 : r0 + n, :] * buf[p - 1, r0 : r0 + n, :]
        s = s + ce1[2, p, r0 : r0 + n, :] * buf[p, r0 + 1 : r0 + 1 + n, :]
        s = s + ce1[2, p, r0 - 1 : r0 - 1 + n, :] * buf[p, r0 - 1 : r0 - 1 + n, :]
        z = ce1[3, p, r0 : r0 + n, :]
        return c, s + z * roll(c, 127) + roll(z * c, 1)

    def sweep1(src, dst, first, count):
        def body(i):
            p = i + first
            c, s = beside1(u1.at[src], p, 8, 48)
            u1[dst, p, 8:56, :] = c * THIRD + w1[p] * (f1e[p] + s)

        each(count, body)

    sweep1(0, 1, 1, 10)

    src2 = []
    for i in range(2):
        total = None
        for j in range(2):
            x = 2 * i + j
            c, s = beside1(u1.at[1], x + 4, 16, 32)
            r = f1[x] - d1[x] * c + s
            total = r if total is None else total + r
        t0[32 * i : 32 * i + 32, :] = jnp.where(own1, total, 0.0)
        src2.append(mm(pair_rows(t0, 32 * i, 16), mb[...]))
    gg[1, 1, gx] = pack2(src2)

    def fcopy(d, sy, sz):
        return pltpu.make_async_remote_copy(
            src_ref=gg.at[1, 1, gx], dst_ref=gg.at[1 - sz, 1 - sy, gx],
            send_sem=gs.at[d, sy + 1, sz + 1], recv_sem=gr.at[d, sy + 1, sz + 1],
            device_id=at(lax.rem(gx + d, nx), sy, sz), device_id_type=MESH,
        )

    def fback(d, sy, sz):
        return pltpu.make_async_remote_copy(
            src_ref=gg.at[1, 1, gx], dst_ref=gg.at[1 - sz, 1 - sy, lax.rem(gx + 4 - d, nx)],
            send_sem=gs.at[d, sy + 1, sz + 1], recv_sem=gr.at[d, sy + 1, sz + 1],
            device_id=at(lax.rem(gx + d, nx), sy, sz), device_id_type=MESH,
        )

    order = sorted([(sy, sz) for sy in steps for sz in steps], key=lambda o: -abs(o[0]) - abs(o[1]))

    def g_start():
        for sy, sz in order:
            @pl.when(yz_ok(sy, sz))
            def _(sy=sy, sz=sz):
                for d in (2, 1, 3, 0):
                    if (d, sy, sz) != (0, 0, 0):
                        fcopy(d, sy, sz).start()

    def g_wait():
        for sy, sz in order:
            @pl.when(yz_ok(sy, sz))
            def _(sy=sy, sz=sz):
                for d in range(4):
                    if (d, sy, sz) != (0, 0, 0):
                        fcopy(d, sy, sz).wait_send()

            @pl.when(yz_ok(-sy, -sz))
            def _(sy=sy, sz=sz):
                for d in range(4):
                    if (d, sy, sz) != (0, 0, 0):
                        fback(d, sy, sz).wait_recv()

    g_start()
    cg[5]()

    def spread2(get, put):
        def body(b):
            for y in range(3):
                v = [get(z, y, b) for z in range(3)]
                for x in range(2):
                    for t in range(2):
                        g = 2 * x + t
                        left = roll(v[0], (16 - 32 * g) % 128)
                        mid = roll(v[1], (48 - 32 * g) % 128)
                        right = roll(v[2], (80 - 32 * g) % 128)
                        out = jnp.where(lane8 < 48, left, jnp.where(lane8 < 80, mid, right))
                        out = jnp.where((lane8 >= 16) & (lane8 < 112), out, 0.0)
                        put(2 * b + x, 16 * y + 8 * t, out)

        each(4, body)

    def put_d(p, r, v):
        d2[p, r : r + 8, :] = v
        ok = v > 0.0
        w2[p, r : r + 8, :] = jnp.where(ok, W / jnp.where(ok, v, 1.0), 0.0)

    def put_x(p, r, v):
        fx2[p + 1, r : r + 8, :] = v

    def put_y(p, r, v):
        fy2[p, 8 + r : 16 + r, :] = v

    def put_z(p, r, v):
        fz2[p, r : r + 8, :] = v

    def put_f(p, r, v):
        f2[p, r : r + 8, :] = v
        u2[0, p + 2, 8 + r : 16 + r, :] = w2[p, r : r + 8, :] * v

    for a, put in enumerate((put_d, put_x, put_y, put_z)):
        spread2(lambda z, y, b, a=a: cc[z, y, b, a], put)
    fx2[0] = jnp.zeros((48, 128), F32)
    fx3[0] = jnp.zeros((24, 128), F32)

    zero_rows(fy2, 8, 48)
    zero_rows(fy3, 4, 24)
    for b in range(2):
        zero_rows(u2.at[b], 12, 48)
        zero_rows(u3.at[b], 6, 24)
        for p in (0, 1, 10, 11):
            u2[b, p, 8:56, :] = jnp.zeros((48, 128), F32)
        for p in (0, 5):
            u3[b, p, 8:32, :] = jnp.zeros((24, 128), F32)

    row48 = lax.broadcasted_iota(jnp.int32, (48, 128), 0)

    def body(p):
        a, b = 2 * p, 2 * p + 1
        t5[p, 0] = fx2[b + 1]
        t5[p, 1] = fz2[a] + fz2[b]
        ysum = fy2[a, 8:56, :] + fy2[b, 8:56, :]
        t5[p, 2] = ysum
        inner = fx2[a + 1]
        inner = inner + jnp.where(row48 % 2 == 0, ysum, 0.0)
        inner = inner + jnp.where(lane48 % 2 == 0, fz2[a] + fz2[b], 0.0)
        t5[p, 3] = d2[a] + d2[b] - 2.0 * inner
        pick = lambda q, off: t5[p, q, pl.ds(off, 24, stride=2), :]
        fx3[p + 1] = mm(pick(0, 0) + pick(0, 1), mb[...])
        fz3[p] = mm(pick(1, 0) + pick(1, 1), mo[...])
        fy3[p, 8:32, :] = mm(pick(2, 1), mb[...])
        diag = mm(pick(3, 0) + pick(3, 1), mb[...])
        ok = diag > 0.0
        w3[p] = jnp.where(ok, W / jnp.where(ok, diag, 1.0), 0.0)

    each(4, body)

    g_wait()
    spread2(lambda z, y, b: gg[z, y, b], put_f)

    def beside(buf, fxr, fyr, fzr, p, rows):
        c = buf[p + 1, 8 : 8 + rows, :]
        s = fxr[p + 1] * buf[p + 2, 8 : 8 + rows, :] + fxr[p] * buf[p, 8 : 8 + rows, :]
        s = s + fyr[p, 8 : 8 + rows, :] * buf[p + 1, 9 : 9 + rows, :]
        s = s + fyr[p, 7 : 7 + rows, :] * buf[p + 1, 7 : 7 + rows, :]
        z = fzr[p]
        return c, s + z * roll(c, 127) + roll(z * c, 1)

    def sweep2(src, dst):
        def body(p):
            c, s = beside(u2.at[src, pl.ds(1, 10)], fx2, fy2, fz2, p, 48)
            u2[dst, p + 2, 8:56, :] = c * THIRD + w2[p] * (f2[p] + s)

        each(8, body)

    def sweep3(src, dst):
        def body(p):
            c, s = beside(u3.at[src], fx3, fy3, fz3, p, 24)
            u3[dst, p + 1, 8:32, :] = c * THIRD + w3[p] * (f3[p] + s)

        each(4, body)

    sweep2(0, 1)

    def body(p):
        total = None
        for j in range(2):
            c, s = beside(u2.at[1, pl.ds(1, 10)], fx2, fy2, fz2, 2 * p + j, 48)
            r = f2[2 * p + j] - d2[2 * p + j] * c + s
            total = r if total is None else total + r
        t5[p, 0] = total
        src = mm(t5[p, 0, pl.ds(0, 24, stride=2), :] + t5[p, 0, pl.ds(1, 24, stride=2), :], mb[...])
        f3[p] = src
        u3[0, p + 1, 8:32, :] = w3[p] * src

    each(4, body)
    sweep3(0, 1)
    sweep3(1, 0)
    sweep3(0, 1)

    def body(p):
        e = mm(u3[1, p + 1, 8:32, :], mt[...])
        t5[p, 1, pl.ds(0, 24, stride=2), :] = e
        t5[p, 1, pl.ds(1, 24, stride=2), :] = e
        wide = t5[p, 1]
        for j in range(2):
            q = 2 * p + j
            u2[0, q + 2, 8:56, :] = u2[1, q + 2, 8:56, :] + jnp.where(d2[q] > 0.0, wide, 0.0)

    each(4, body)
    sweep2(0, 1)
    sweep2(1, 0)

    def body(q):
        e = mm(u2[0, 2 * gx + q, 20:44, :], mt[...])
        t2[q, pl.ds(0, 24, stride=2), :] = e
        t2[q, pl.ds(1, 24, stride=2), :] = e

    each(6, body)

    def body(i):
        p = i + 1
        u1[0, p, 8:56, :] = u1[1, p, 8:56, :] + jnp.where(w1[p] > 0.0, t2[p // 2], 0.0)

    each(10, body)
    sweep1(0, 1, 2, 8)
    sweep1(1, 0, 3, 6)

    def body(q):
        c = u1[0, q + 3, 12:52, :]
        e = mm(c, mt[...])
        t3[q, pl.ds(0, 40, stride=2), :] = e
        t3[q, pl.ds(1, 40, stride=2), :] = e
        t4[q, pl.ds(0, 40, stride=2), :] = c
        t4[q, pl.ds(1, 40, stride=2), :] = c

    each(6, body)

    def body(p):
        u0[0, p, :, :] = u0[1, p, :, :] + t3[(p + 1) // 2]

    each(10, body)

    def body(q, carry):
        lo, hi = carry
        for t in range(8):
            v = t4[q + 1, 8 + 8 * t : 16 + 8 * t, :]
            k = 16 * q + t
            here = (lane8 == k) | (lane8 == k + 8)
            a, b = roll(v, lax.rem(k + 97, 128)), roll(v, lax.rem(k + 32, 128))
            lo = jnp.where(lane8 == k, a, jnp.where(lane8 == k + 8, roll(a, 8), lo))
            hi = jnp.where(lane8 == k, b, jnp.where(lane8 == k + 8, roll(b, 8), hi))
        return lo, hi

    lo, hi = loop(4, body, (zero8, zero8))
    zr0[0, 0] = zr0[1, 0] + lo
    zr0[0, 1] = zr0[1, 1] + hi
    sweep0(u0.at[0], u0.at[2], zr0.at[0], ys0.at[2], zs0.at[2], False)
    start, wait = round0(2)
    start()
    wait()
    y_in(u0.at[2], yr0.at[2], 8, 64)
    sweep0(u0.at[2], u0.at[0], zr0.at[2], ys0.at[0], zs0.at[0], True)

    start, wait = round0(0)
    start()
    out0 = pltpu.make_async_copy(osol, os_h.at[0], out_sem.at[0])
    out0.start()
    wait()
    y_in(u0.at[0], yr0.at[0], 8, 64)
    lo, hi = zr0[0, 0], zr0[0, 1]

    def body(x):
        c, s = beside0(u0.at[0], x, lo, hi)
        ores[x] = f0[x] - d0[x] * c + s

    each(8, body)
    out1 = pltpu.make_async_copy(ores, or_h.at[0], out_sem.at[1])
    out1.start()
    out0.wait()
    out1.wait()


def on_device(phase, density, rhs):
    V = lambda *s: pltpu.VMEM(s, F32)
    M = pltpu.VMEM((384, 128), BF16)
    D = lambda *s: pltpu.SemaphoreType.DMA(s)
    scratch = [
        pltpu.VMEM((8, 64, 128), jnp.int32), V(8, 64, 128), V(8, 64, 128), V(10, 80, 128), V(3, 10, 80, 128),
        V(9, 64, 128), V(8, 80, 128), V(8, 64, 128), V(8, 64, 128), V(8, 64, 128), V(8, 64, 128),
        V(2, 8, 128), V(2, 8, 128), V(2, 8, 128), V(2, 8, 128),
        V(3, 2, 8, 128), V(3, 2, 8, 128), V(3, 2, 8, 128), V(3, 2, 8, 128),
        V(2, 12, 64, 128), V(4, 32, 128), V(5, 32, 128), V(4, 32, 128), V(4, 32, 128), V(4, 32, 128), V(4, 32, 128),
        V(4, 32, 128), V(12, 48, 128), V(4, 12, 64, 128),
        V(4, 2, 32, 128), V(2, 4, 8, 128), V(2, 4, 8, 128), V(2, 2, 8, 128),
        V(2, 4, 2, 32, 128), V(3, 2, 4, 8, 128), V(3, 2, 4, 8, 128), V(3, 2, 2, 8, 128),
        V(1, 2, 32, 128), V(2, 1, 8, 128), V(2, 1, 8, 128), V(2, 2, 8, 128),
        V(2, 1, 2, 32, 128), V(3, 2, 1, 8, 128), V(3, 2, 1, 8, 128), V(3, 2, 2, 8, 128),
        M, M, M, M, V(256, 128), V(4, 2, 64, 128), V(6, 48, 128), V(6, 80, 128), V(6, 80, 128), V(4, 4, 48, 128),
        V(12, 48, 128),
        V(3, 3, 4, 4, 8, 128), V(3, 3, 4, 8, 128),
        V(8, 48, 128), V(2, 12, 64, 128), V(9, 48, 128), V(8, 64, 128), V(8, 48, 128), V(8, 48, 128), V(8, 48, 128),
        V(4, 24, 128), V(2, 6, 40, 128), V(5, 24, 128), V(4, 40, 128), V(4, 24, 128), V(4, 24, 128),
        V(8, 64, 128), V(8, 64, 128),
        D(3), D(2), D(6), D(6), D(3, 6), D(3, 6), D(3, 3, 3), D(3, 3, 3), D(3, 3, 3), D(3, 3, 3),
        D(3), D(3), D(4), D(4), D(4, 3, 3), D(4, 3, 3),
    ]
    shape = jax.ShapeDtypeStruct(rhs.shape, F32)
    return pl.pallas_call(
        kernel,
        out_shape=(shape, shape),
        in_specs=[pl.BlockSpec(memory_space=pl.ANY)] * 3,
        out_specs=(pl.BlockSpec(memory_space=pl.ANY),) * 2,
        scratch_shapes=scratch,
        compiler_params=pltpu.CompilerParams(collective_id=0, has_side_effects=True),
        name="vcycle",
    )(phase, density, rhs)


def solution(mesh):
    in_specs = (P("gx", "gy", "gz"), P("gx", "gy", "gz"), P(None, "gx", "gy", "gz"))
    out_specs = (P(None, "gx", "gy", "gz"), P(None, "gx", "gy", "gz"))
    return jax.shard_map(on_device, mesh=mesh, in_specs=in_specs, out_specs=out_specs, check_vma=False)
```

```python
import functools

import jax
import jax.numpy as jnp
from jax import lax
from jax.experimental import pallas as pl
from jax.experimental.pallas import tpu as pltpu
from jax.sharding import PartitionSpec as P

MESH = pl.DeviceIdType.MESH
F32 = jnp.float32
W = 2.0 / 3.0
THIRD = 1.0 / 3.0
BF16 = jnp.bfloat16


def lanes(shape):
    return lax.broadcasted_iota(jnp.int32, shape, len(shape) - 1)


def roll(v, shift):
    return pltpu.roll(v, shift, 1)


def loop(count, body, init=0):
    return lax.fori_loop(0, count, body, init, unroll=True)


def each(count, body):
    def step(i, carry):
        body(i)
        return carry

    lax.fori_loop(0, count, step, 0, unroll=True)


def maps():
    row = lax.broadcasted_iota(jnp.int32, (128, 128), 0)
    col = lax.broadcasted_iota(jnp.int32, (128, 128), 1)
    hit = col == 32 + row // 2
    both = jnp.where(hit, 1.0, 0.0)
    odd = jnp.where(hit & (row % 2 == 1), 1.0, 0.0)
    even = jnp.where(hit & (row % 2 == 0), 1.0, 0.0)
    back = jnp.where(row == 32 + col // 2, 1.0, 0.0)
    return [jnp.concatenate([m.astype(BF16)] * 3, axis=0) for m in (both, odd, even, back)]


def mm(a, b):
    hi = a.astype(BF16)
    rest = a - hi.astype(F32)
    mid = rest.astype(BF16)
    low = (rest - mid.astype(F32)).astype(BF16)
    return lax.dot(jnp.concatenate([hi, mid, low], axis=1), b, preferred_element_type=F32)


def kernel(
    ph_h, de_h, rh_h, osol, ores,
    ph, de, f0, rp, u0, fx, fy, fzu, fzd, w0, d0,
    rys, ryr, rzs, rzr, ys0, yr0, zs0, zr0,
    u1, f1, fx1, fy1u, fy1d, fz1u, fz1d, d1, w1, ce1,
    pkc, xyc, zpc, yzc, rxc, ryc, rzc, rec, pkf, xyf, zpf, yzf, rxf, ryf, rzf, ref_,
    mb, mo, me, mt, t0, t1, t2, t3, t4, t5, f1e,
    cc, gg,
    f2, u2, fx2, fy2, fz2, w2, d2,
    f3, u3, fx3, fy3, fz3, w3,
    in_sem, rss, rrs, s0s, r0s, s1c, r1c, s1f, r1f, csx, crx, csn, crn, gs, gr,
):
    gx, gy, gz = lax.axis_index("gx"), lax.axis_index("gy"), lax.axis_index("gz")
    nx, ny, nz = lax.axis_size("gx"), lax.axis_size("gy"), lax.axis_size("gz")
    near = [
        ({"gx": gx + 1}, gx < nx - 1, gx > 0),
        ({"gx": gx - 1}, gx > 0, gx < nx - 1),
        ({"gy": gy + 1}, gy < ny - 1, gy > 0),
        ({"gy": gy - 1}, gy > 0, gy < ny - 1),
        ({"gz": gz + 1}, gz < nz - 1, gz > 0),
        ({"gz": gz - 1}, gz > 0, gz < nz - 1),
    ]

    loads = [
        pltpu.make_async_copy(ph_h, ph, in_sem.at[0]),
        pltpu.make_async_copy(de_h, de, in_sem.at[1]),
        pltpu.make_async_copy(rh_h.at[0], f0, in_sem.at[2]),
    ]
    for c in loads:
        c.start()

    edge = (gx == 0) | (gx == nx - 1) | (gy == 0) | (gy == ny - 1) | (gz == 0) | (gz == nz - 1)

    @pl.when(edge)
    def _():
        for ref in (ryc, rzc, rec):
            ref[...] = jnp.zeros(ref.shape, F32)

    barrier = pltpu.get_barrier_semaphore()
    arrivals = 0
    for where, ok, back in near:
        arrivals = arrivals + jnp.where(back, 1, 0)

        @pl.when(ok)
        def _(where=where):
            pl.semaphore_signal(barrier, inc=1, device_id=where, device_id_type=MESH)

    for b in range(3):
        for x in (0, 9):
            u0[b, x, 8:72, :] = jnp.zeros((64, 128), F32)
        for ref in (yr0, zr0):
            for k in range(2):
                ref[b, k] = jnp.zeros((8, 128), F32)

    @pl.when(edge)
    def _():
        for ref in (gg, rxc, rxf, ryf, rzf, ref_):
            ref[...] = jnp.zeros(ref.shape, F32)
        for z in range(3):
            for y in range(3):
                if (z, y) != (1, 1):
                    cc[z, y] = jnp.zeros(cc.shape[2:], F32)

    def inside(at, step, count):
        return (at >= 0) if step == 0 else (at < count - 1) if step > 0 else (at > 0)

    def yz_ok(sy, sz):
        return inside(gy, sy, ny) & inside(gz, sz, nz)

    def at(sx, sy, sz):
        return {"gx": sx, "gy": gy + sy, "gz": gz + sz}

    steps = (-1, 0, 1)

    def faces(buf, n, rows, ys, yr, zs, zr, ss, rs):
        body = pl.ds(8, rows)
        pairs = [
            (buf.at[n, body], buf.at[0, body]),
            (buf.at[1, body], buf.at[n + 1, body]),
            (ys.at[1], yr.at[0]),
            (ys.at[0], yr.at[1]),
            (zs.at[1], zr.at[0]),
            (zs.at[0], zr.at[1]),
        ]

        def copy(d):
            src, dst = pairs[d]
            return pltpu.make_async_remote_copy(
                src_ref=src, dst_ref=dst, send_sem=ss.at[d], recv_sem=rs.at[d],
                device_id=near[d][0], device_id_type=MESH,
            )

        def start():
            for d in range(6):
                @pl.when(near[d][1])
                def _(d=d):
                    copy(d).start()

        def wait():
            for d in range(6):
                @pl.when(near[d][1])
                def _(d=d):
                    copy(d).wait_send()

                @pl.when(near[d][2])
                def _(d=d):
                    copy(d).wait_recv()

        return start, wait

    lane8 = lanes((8, 128))
    lane64 = lanes((64, 128))
    lane32 = lanes((32, 128))

    zero8 = jnp.zeros((8, 128), F32)

    def pack0(carry, plane, x):
        lo, hi = carry
        for t in range(8):
            v = plane[8 * t : 8 * t + 8]
            k = x * 8 + t
            here = lane8 == k
            lo = jnp.where(here, roll(v, k), lo)
            hi = jnp.where(here, roll(v, k + 1), hi)
        return lo, hi

    def z_beside0(plane, x, lo, hi):
        right = jnp.concatenate([roll(hi, 127 - (x * 8 + t)) for t in range(8)], axis=0)
        left = jnp.concatenate([roll(lo, lax.rem(128 - (x * 8 + t), 128)) for t in range(8)], axis=0)
        return (
            jnp.where(lane64 == 127, right, roll(plane, 127)),
            jnp.where(lane64 == 0, left, roll(plane, 1)),
        )

    def keep0(buf, ys, x, plane):
        buf[x + 1, 8:72, :] = plane
        ys[0, pl.ds(x, 1), :] = plane[0:1]
        ys[1, pl.ds(x, 1), :] = plane[63:64]

    def y_in(buf, yr, n, rows):
        def body(x):
            buf[x + 1, 7:8, :] = yr[0, pl.ds(x, 1), :]
            buf[x + 1, 8 + rows : 9 + rows, :] = yr[1, pl.ds(x, 1), :]

        each(n, body)

    def beside0(buf, x, lo, hi):
        c = buf[x + 1, 8:72, :]
        up, down = z_beside0(c, x, lo, hi)
        s = fx[x + 1] * buf[x + 2, 8:72, :] + fx[x] * buf[x, 8:72, :]
        s = s + fy[x, 8:72, :] * buf[x + 1, 9:73, :] + fy[x, 7:71, :] * buf[x + 1, 7:71, :]
        s = s + fzu[x] * up + fzd[x] * down
        return c, s

    def sweep0(src, dst, zr, ys, zs, out):
        lo, hi = zr[0], zr[1]

        def body(x, carry):
            c, s = beside0(src, x, lo, hi)
            new = c * THIRD + w0[x] * (f0[x] + s)
            keep0(dst, ys, x, new)
            if out:
                osol[0, x] = d0[x] * new
            return pack0(carry, new, x)

        packed = loop(8, body, (zero8, zero8))
        zs[0] = packed[0]
        zs[1] = packed[1]

    for c in loads[:2]:
        c.wait()

    def body(x, carry):
        plane = jnp.where(ph[x] == 1, 1000.0, 1.0).astype(F32) * de[x]
        keep0(rp, rys, x, plane)
        return pack0(carry, plane, x)

    packed = loop(8, body, (zero8, zero8))
    rzs[0] = packed[0]
    rzs[1] = packed[1]

    pl.semaphore_wait(barrier, arrivals)
    start, wait = faces(rp, 8, 64, rys, ryr, rzs, rzr, rss, rrs)
    start()
    both, odd, even, back = maps()
    mb[...] = both
    mo[...] = odd
    me[...] = even
    mt[...] = back
    loads[2].wait()
    wait()

    @pl.when(gx == 0)
    def _():
        rp[0, 8:72, :] = rp[1, 8:72, :]

    @pl.when(gx == nx - 1)
    def _():
        rp[9, 8:72, :] = rp[8, 8:72, :]

    for ok, got, own, s in ((gy == 0, ryr, rys, 0), (gy == ny - 1, ryr, rys, 1), (gz == 0, rzr, rzs, 0), (gz == nz - 1, rzr, rzs, 1)):
        @pl.when(ok)
        def _(got=got, own=own, s=s):
            got[s] = own[s]

    y_in(rp, ryr, 8, 64)
    lo, hi = rzr[0], rzr[1]
    fx[0] = 2.0 / (rp[0, 8:72, :] + rp[1, 8:72, :])

    def body(x, carry):
        c = rp[x + 1, 8:72, :]
        up, down = z_beside0(c, x, lo, hi)
        xu = 2.0 / (c + rp[x + 2, 8:72, :])
        yu = 2.0 / (c + rp[x + 1, 9:73, :])
        zu = 2.0 / (c + up)
        zd = 2.0 / (c + down)
        fx[x + 1] = xu
        fy[x, 8:72, :] = yu
        fy[x, 7:8, :] = 2.0 / (c[0:1] + rp[x + 1, 7:8, :])
        fzu[x] = zu
        fzd[x] = zd
        diag = xu + fx[x] + yu + fy[x, 7:71, :] + zu + zd
        d0[x] = diag
        w = W / diag
        w0[x] = w
        first = w * f0[x]
        keep0(u0.at[0], ys0.at[0], x, first)
        return pack0(carry, first, x)

    packed = loop(8, body, (zero8, zero8))
    zs0[0, 0] = packed[0]
    zs0[0, 1] = packed[1]

    def round0(b):
        return faces(u0.at[b], 8, 64, ys0.at[b], yr0.at[b], zs0.at[b], zr0.at[b], s0s.at[b], r0s.at[b])

    box = [(a, b, c) for a in steps for b in steps for c in steps if (a, b, c) != (0, 0, 0)]

    def box_exchange(pk, xy, zp, yz, rx, ry, rz, re, ss, rs):
        def copy(a, b, c):
            if b and c:
                src, dst = yz.at[(b + 1) // 2, (c + 1) // 2], re.at[1 - a, (1 - b) // 2, (1 - c) // 2]
            elif c:
                src, dst = zp.at[(c + 1) // 2], rz.at[1 - a, (1 - c) // 2]
            elif b:
                src, dst = xy.at[(b + 1) // 2], ry.at[1 - a, (1 - b) // 2]
            else:
                src, dst = pk, rx.at[(1 - a) // 2]
            return pltpu.make_async_remote_copy(
                src_ref=src, dst_ref=dst, send_sem=ss.at[a + 1, b + 1, c + 1], recv_sem=rs.at[a + 1, b + 1, c + 1],
                device_id=at(gx + a, b, c), device_id_type=MESH,
            )

        def start(far=(1, 2, 3)):
            for n in sorted(far, reverse=True):
                for a, b, c in box:
                    if abs(a) + abs(b) + abs(c) == n:
                        @pl.when(inside(gx, a, nx) & yz_ok(b, c))
                        def _(a=a, b=b, c=c):
                            copy(a, b, c).start()

        def wait():
            for a, b, c in box:
                @pl.when(inside(gx, a, nx) & yz_ok(b, c))
                def _(a=a, b=b, c=c):
                    copy(a, b, c).wait_send()

                @pl.when(inside(gx, -a, nx) & yz_ok(-b, -c))
                def _(a=a, b=b, c=c):
                    copy(a, b, c).wait_recv()

        return start, wait

    row8 = lax.broadcasted_iota(jnp.int32, (8, 128), 0)

    def half(v):
        return pltpu.roll(v, 4, 0)

    def pack_box(gets, pk, xy, zp, yz):
        edge = {(b, c): zero8 for b in range(2) for c in range(2)}
        for a, get in enumerate(gets):
            planes = [get(x) for x in range(4)]
            pairs = [jnp.where(own1, planes[2 * i], roll(planes[2 * i + 1], 64)) for i in range(2)]
            for i in range(2):
                pk[a, i] = pairs[i]
            xy[0, a] = jnp.where(row8 < 4, pairs[0][0:8], half(pairs[1][0:8]))
            xy[1, a] = jnp.where(row8 >= 4, pairs[0][24:32], half(pairs[1][24:32]))
            face = [zero8, zero8]
            for x in range(4):
                for t in range(4):
                    v = planes[x][8 * t : 8 * t + 8]
                    k = x * 4 + t
                    for c, first in ((0, 96), (1, 40)):
                        face[c] = jnp.where(lane8 // 8 == k, roll(v, (8 * k + first) % 128), face[c])
                        if t in (0, 3):
                            b = t // 3
                            edge[b, c] = jnp.where(lane8 // 8 == 4 * a + x, roll(v, (32 * a + 8 * x + first) % 128), edge[b, c])
            zp[0, a] = face[0]
            zp[1, a] = face[1]
        for b in range(2):
            for c in range(2):
                yz[b, c] = edge[b, c]

    def unpack_box(own, rx, ry, rz, re, a, put):
        def side(dx, x, c, first):
            def corner(b):
                return roll(re[dx, b, c], (first - 32 * a - 8 * x) % 128)

            mid = [roll(rz[dx, c, a], (first - 8 * (4 * x + t)) % 128) for t in range(4)]
            return jnp.concatenate([corner(0)] + mid + [corner(1)], axis=0)

        for dx in range(3):
            for x in range(4):
                i = x // 2
                turn = (lambda v: roll(v, 64)) if x % 2 else (lambda v: v)
                flip = half if i else (lambda v: v)
                mid = own(x) if dx == 1 else turn(rx[dx // 2, a, i])
                centre = jnp.concatenate([turn(flip(ry[dx, 0, a])), mid, turn(flip(ry[dx, 1, a]))], axis=0)
                out = jnp.where((lane48 >= 96) & (lane48 < 104), side(dx, x, 1, 96), 0.0)
                out = jnp.where((lane48 >= 32) & (lane48 < 96), centre, out)
                out = jnp.where((lane48 >= 24) & (lane48 < 32), side(dx, x, 0, 24), out)
                put(4 * dx + x, out)

    lane48 = lanes((48, 128))
    start, wait = round0(0)
    start()

    own1 = (lane32 >= 32) & (lane32 < 96)

    def rows_of(ref, base, n, off):
        return ref[pl.ds(base + off, n, stride=2), :]

    def pair_rows(ref, base, n):
        return rows_of(ref, base, n, 0) + rows_of(ref, base, n, 1)

    for i in range(5):
        t0[0:64, :] = fx[2 * i]
        fx1[i] = mm(pair_rows(t0, 0, 32), mb[...])

    def body(i):
        yu = fy[2 * i, pl.ds(9, 32, stride=2), :] + fy[2 * i + 1, pl.ds(9, 32, stride=2), :]
        yd = fy[2 * i, pl.ds(7, 32, stride=2), :] + fy[2 * i + 1, pl.ds(7, 32, stride=2), :]
        t1[i, 0] = fzu[2 * i] + fzu[2 * i + 1]
        t1[i, 1] = fzd[2 * i] + fzd[2 * i + 1]
        zu = t1[i, 0, pl.ds(0, 32, stride=2), :] + t1[i, 0, pl.ds(1, 32, stride=2), :]
        zd = t1[i, 1, pl.ds(0, 32, stride=2), :] + t1[i, 1, pl.ds(1, 32, stride=2), :]
        yu, yd, zu, zd = mm(yu, mb[...]), mm(yd, mb[...]), mm(zu, mo[...]), mm(zd, me[...])
        fy1u[i] = yu
        fy1d[i] = yd
        fz1u[i] = zu
        fz1d[i] = zd
        diag = fx1[i] + fx1[i + 1] + yu + yd + zu + zd
        d1[i] = jnp.where(own1, diag, 0.0)

    each(4, body)
    parts1 = (lambda x: d1[x], lambda x: fx1[x + 1], lambda x: fy1u[x], lambda x: fz1u[x])
    pack_box(parts1, pkc, xyc, zpc, yzc)
    c_start, c_wait = box_exchange(pkc, xyc, zpc, yzc, rxc, ryc, rzc, rec, s1c, r1c)
    c_start((1,2))

    def pack2(planes):
        out = zero8
        for x in range(2):
            for t in range(2):
                g = 2 * x + t
                v = roll(planes[x][8 * t : 8 * t + 8], (32 * g - 48) % 128)
                out = jnp.where((lane8 >= 32 * g) & (lane8 < 32 * g + 32), v, out)
        return out

    xu, yu, zu, dg = [], [], [], []
    for i in range(2):
        t0[0:32, :] = fx1[2 * i]
        t0[32:64, :] = fx1[2 * i + 2]
        t0[64:96, :] = fz1u[2 * i] + fz1u[2 * i + 1]
        t0[96:128, :] = fz1d[2 * i] + fz1d[2 * i + 1]
        t0[128:160, :] = fy1u[2 * i] + fy1u[2 * i + 1]
        t0[160:192, :] = fy1d[2 * i] + fy1d[2 * i + 1]
        xd_, xu_ = mm(pair_rows(t0, 0, 16), mb[...]), mm(pair_rows(t0, 32, 16), mb[...])
        zu_, zd_ = mm(pair_rows(t0, 64, 16), mo[...]), mm(pair_rows(t0, 96, 16), me[...])
        yu_, yd_ = mm(rows_of(t0, 128, 16, 1), mb[...]), mm(rows_of(t0, 160, 16, 0), mb[...])
        xu.append(xu_)
        yu.append(yu_)
        zu.append(zu_)
        dg.append(xu_ + xd_ + yu_ + yd_ + zu_ + zd_)
    for a, planes in enumerate((dg, xu, yu, zu)):
        cc[1, 1, gx, a] = pack2(planes)

    def gather(buf, sx, rx, sn, rn):
        def xcopy(d):
            return pltpu.make_async_remote_copy(
                src_ref=buf.at[1, 1, gx], dst_ref=buf.at[1, 1, gx], send_sem=sx.at[d - 1], recv_sem=rx.at[d - 1],
                device_id={"gx": lax.rem(gx + d, nx)}, device_id_type=MESH,
            )

        def ncopy(d):
            src = buf.at[1, 1] if d < 4 else buf.at[1]
            dst = [buf.at[1, 0], buf.at[1, 2], buf.at[0], buf.at[2]][d - 2]
            return pltpu.make_async_remote_copy(
                src_ref=src, dst_ref=dst, send_sem=sn.at[d - 2], recv_sem=rn.at[d - 2],
                device_id=near[d][0], device_id_type=MESH,
            )

        def xstart():
            for d in range(1, 4):
                xcopy(d).start()

        def xwait():
            for d in range(1, 4):
                pltpu.make_async_remote_copy(
                    src_ref=buf.at[1, 1, gx], dst_ref=buf.at[1, 1, lax.rem(gx + 4 - d, nx)],
                    send_sem=sx.at[d - 1], recv_sem=rx.at[d - 1],
                    device_id={"gx": lax.rem(gx + d, nx)}, device_id_type=MESH,
                ).wait()

        def nstart(ds):
            for d in ds:
                @pl.when(near[d][1])
                def _(d=d):
                    ncopy(d).start()

        def nwait(ds):
            for d in ds:
                @pl.when(near[d][1])
                def _(d=d):
                    ncopy(d).wait_send()

                @pl.when(near[d][2])
                def _(d=d):
                    ncopy(d).wait_recv()

        return (
            xstart, xwait,
            lambda: nstart((2, 3)), lambda: nwait((2, 3)),
            lambda: nstart((4, 5)), lambda: nwait((4, 5)),
        )

    cg = gather(cc, csx, crx, csn, crn)

    wait()
    c_start((3,))
    cg[0]()
    y_in(u0.at[0], yr0.at[0], 8, 64)
    sweep0(u0.at[0], u0.at[1], zr0.at[0], ys0.at[1], zs0.at[1], False)
    start, wait = round0(1)
    start()
    wait()
    y_in(u0.at[1], yr0.at[1], 8, 64)

    cg[1]()
    cg[2]()
    lo, hi = zr0[1, 0], zr0[1, 1]

    def body(i):
        total = None
        for j in range(2):
            x = 2 * i + j
            c, s = beside0(u0.at[1], x, lo, hi)
            r = f0[x] - d0[x] * c + s
            total = r if total is None else total + r
        t1[i, 0] = total
        f1[i] = mm(t1[i, 0, pl.ds(0, 32, stride=2), :] + t1[i, 0, pl.ds(1, 32, stride=2), :], mb[...])

    each(4, body)

    pack_box([lambda x: f1[x]], pkf, xyf, zpf, yzf)
    f_start, f_wait = box_exchange(pkf, xyf, zpf, yzf, rxf, ryf, rzf, ref_, s1f, r1f)
    f_start()
    c_wait()
    cg[3]()
    cg[4]()
    for a, get in enumerate(parts1):
        def put(p, out, a=a):
            ce1[a, p, 8:56, :] = out
            if a == 0:
                ok = out > 0.0
                w1[p] = jnp.where(ok, W / jnp.where(ok, out, 1.0), 0.0)

        unpack_box(get, rxc, ryc, rzc, rec, a, put)

    def zero_rows(ref, n, rows):
        def body(p):
            ref[p, 0:8, :] = zero8
            ref[p, 8 + rows : 16 + rows, :] = zero8

        each(n, body)

    zero_rows(ce1.at[2], 12, 48)
    for b in range(2):
        zero_rows(u1.at[b], 12, 48)
    f_wait()

    def put(p, out):
        f1e[p] = out
        u1[0, p, 8:56, :] = w1[p] * out

    unpack_box(lambda x: f1[x], rxf, ryf, rzf, ref_, 0, put)

    def beside1(buf, p, r0, n):
        c = buf[p, r0 : r0 + n, :]
        s = ce1[1, p, r0 : r0 + n, :] * buf[p + 1, r0 : r0 + n, :]
        s = s + ce1[1, p - 1, r0 : r0 + n, :] * buf[p - 1, r0 : r0 + n, :]
        s = s + ce1[2, p, r0 : r0 + n, :] * buf[p, r0 + 1 : r0 + 1 + n, :]
        s = s + ce1[2, p, r0 - 1 : r0 - 1 + n, :] * buf[p, r0 - 1 : r0 - 1 + n, :]
        z = ce1[3, p, r0 : r0 + n, :]
        return c, s + z * roll(c, 127) + roll(z * c, 1)

    def sweep1(src, dst, first, count):
        def body(i):
            p = i + first
            c, s = beside1(u1.at[src], p, 8, 48)
            u1[dst, p, 8:56, :] = c * THIRD + w1[p] * (f1e[p] + s)

        each(count, body)

    sweep1(0, 1, 1, 10)

    src2 = []
    for i in range(2):
        total = None
        for j in range(2):
            x = 2 * i + j
            c, s = beside1(u1.at[1], x + 4, 16, 32)
            r = f1[x] - d1[x] * c + s
            total = r if total is None else total + r
        t0[32 * i : 32 * i + 32, :] = jnp.where(own1, total, 0.0)
        src2.append(mm(pair_rows(t0, 32 * i, 16), mb[...]))
    gg[1, 1, gx] = pack2(src2)

    def fcopy(d, sy, sz):
        return pltpu.make_async_remote_copy(
            src_ref=gg.at[1, 1, gx], dst_ref=gg.at[1 - sz, 1 - sy, gx],
            send_sem=gs.at[d, sy + 1, sz + 1], recv_sem=gr.at[d, sy + 1, sz + 1],
            device_id=at(lax.rem(gx + d, nx), sy, sz), device_id_type=MESH,
        )

    def fback(d, sy, sz):
        return pltpu.make_async_remote_copy(
            src_ref=gg.at[1, 1, gx], dst_ref=gg.at[1 - sz, 1 - sy, lax.rem(gx + 4 - d, nx)],
            send_sem=gs.at[d, sy + 1, sz + 1], recv_sem=gr.at[d, sy + 1, sz + 1],
            device_id=at(lax.rem(gx + d, nx), sy, sz), device_id_type=MESH,
        )

    order = sorted([(sy, sz) for sy in steps for sz in steps], key=lambda o: -abs(o[0]) - abs(o[1]))

    def g_start():
        for sy, sz in order:
            @pl.when(yz_ok(sy, sz))
            def _(sy=sy, sz=sz):
                for d in (2, 1, 3, 0):
                    if (d, sy, sz) != (0, 0, 0):
                        fcopy(d, sy, sz).start()

    def g_wait():
        for sy, sz in order:
            @pl.when(yz_ok(sy, sz))
            def _(sy=sy, sz=sz):
                for d in range(4):
                    if (d, sy, sz) != (0, 0, 0):
                        fcopy(d, sy, sz).wait_send()

            @pl.when(yz_ok(-sy, -sz))
            def _(sy=sy, sz=sz):
                for d in range(4):
                    if (d, sy, sz) != (0, 0, 0):
                        fback(d, sy, sz).wait_recv()

    g_start()
    cg[5]()

    def spread2(get, put):
        def body(b):
            for y in range(3):
                v = [get(z, y, b) for z in range(3)]
                for x in range(2):
                    for t in range(2):
                        g = 2 * x + t
                        left = roll(v[0], (16 - 32 * g) % 128)
                        mid = roll(v[1], (48 - 32 * g) % 128)
                        right = roll(v[2], (80 - 32 * g) % 128)
                        out = jnp.where(lane8 < 48, left, jnp.where(lane8 < 80, mid, right))
                        out = jnp.where((lane8 >= 16) & (lane8 < 112), out, 0.0)
                        put(2 * b + x, 16 * y + 8 * t, out)

        each(4, body)

    def put_d(p, r, v):
        d2[p, r : r + 8, :] = v
        ok = v > 0.0
        w2[p, r : r + 8, :] = jnp.where(ok, W / jnp.where(ok, v, 1.0), 0.0)

    def put_x(p, r, v):
        fx2[p + 1, r : r + 8, :] = v

    def put_y(p, r, v):
        fy2[p, 8 + r : 16 + r, :] = v

    def put_z(p, r, v):
        fz2[p, r : r + 8, :] = v

    def put_f(p, r, v):
        f2[p, r : r + 8, :] = v
        u2[0, p + 2, 8 + r : 16 + r, :] = w2[p, r : r + 8, :] * v

    for a, put in enumerate((put_d, put_x, put_y, put_z)):
        spread2(lambda z, y, b, a=a: cc[z, y, b, a], put)
    fx2[0] = jnp.zeros((48, 128), F32)
    fx3[0] = jnp.zeros((24, 128), F32)

    zero_rows(fy2, 8, 48)
    zero_rows(fy3, 4, 24)
    for b in range(2):
        zero_rows(u2.at[b], 12, 48)
        zero_rows(u3.at[b], 6, 24)
        for p in (0, 1, 10, 11):
            u2[b, p, 8:56, :] = jnp.zeros((48, 128), F32)
        for p in (0, 5):
            u3[b, p, 8:32, :] = jnp.zeros((24, 128), F32)

    row48 = lax.broadcasted_iota(jnp.int32, (48, 128), 0)

    def body(p):
        a, b = 2 * p, 2 * p + 1
        t5[p, 0] = fx2[b + 1]
        t5[p, 1] = fz2[a] + fz2[b]
        ysum = fy2[a, 8:56, :] + fy2[b, 8:56, :]
        t5[p, 2] = ysum
        inner = fx2[a + 1]
        inner = inner + jnp.where(row48 % 2 == 0, ysum, 0.0)
        inner = inner + jnp.where(lane48 % 2 == 0, fz2[a] + fz2[b], 0.0)
        t5[p, 3] = d2[a] + d2[b] - 2.0 * inner
        pick = lambda q, off: t5[p, q, pl.ds(off, 24, stride=2), :]
        fx3[p + 1] = mm(pick(0, 0) + pick(0, 1), mb[...])
        fz3[p] = mm(pick(1, 0) + pick(1, 1), mo[...])
        fy3[p, 8:32, :] = mm(pick(2, 1), mb[...])
        diag = mm(pick(3, 0) + pick(3, 1), mb[...])
        ok = diag > 0.0
        w3[p] = jnp.where(ok, W / jnp.where(ok, diag, 1.0), 0.0)

    each(4, body)

    g_wait()
    spread2(lambda z, y, b: gg[z, y, b], put_f)

    def beside(buf, fxr, fyr, fzr, p, rows):
        c = buf[p + 1, 8 : 8 + rows, :]
        s = fxr[p + 1] * buf[p + 2, 8 : 8 + rows, :] + fxr[p] * buf[p, 8 : 8 + rows, :]
        s = s + fyr[p, 8 : 8 + rows, :] * buf[p + 1, 9 : 9 + rows, :]
        s = s + fyr[p, 7 : 7 + rows, :] * buf[p + 1, 7 : 7 + rows, :]
        z = fzr[p]
        return c, s + z * roll(c, 127) + roll(z * c, 1)

    def sweep2(src, dst):
        def body(p):
            c, s = beside(u2.at[src, pl.ds(1, 10)], fx2, fy2, fz2, p, 48)
            u2[dst, p + 2, 8:56, :] = c * THIRD + w2[p] * (f2[p] + s)

        each(8, body)

    def sweep3(src, dst):
        def body(p):
            c, s = beside(u3.at[src], fx3, fy3, fz3, p, 24)
            u3[dst, p + 1, 8:32, :] = c * THIRD + w3[p] * (f3[p] + s)

        each(4, body)

    sweep2(0, 1)

    def body(p):
        total = None
        for j in range(2):
            c, s = beside(u2.at[1, pl.ds(1, 10)], fx2, fy2, fz2, 2 * p + j, 48)
            r = f2[2 * p + j] - d2[2 * p + j] * c + s
            total = r if total is None else total + r
        t5[p, 0] = total
        src = mm(t5[p, 0, pl.ds(0, 24, stride=2), :] + t5[p, 0, pl.ds(1, 24, stride=2), :], mb[...])
        f3[p] = src
        u3[0, p + 1, 8:32, :] = w3[p] * src

    each(4, body)
    sweep3(0, 1)
    sweep3(1, 0)
    sweep3(0, 1)

    def body(p):
        e = mm(u3[1, p + 1, 8:32, :], mt[...])
        t5[p, 1, pl.ds(0, 24, stride=2), :] = e
        t5[p, 1, pl.ds(1, 24, stride=2), :] = e
        wide = t5[p, 1]
        for j in range(2):
            q = 2 * p + j
            u2[0, q + 2, 8:56, :] = u2[1, q + 2, 8:56, :] + jnp.where(d2[q] > 0.0, wide, 0.0)

    each(4, body)
    sweep2(0, 1)
    sweep2(1, 0)

    def body(q):
        e = mm(u2[0, 2 * gx + q, 20:44, :], mt[...])
        t2[q, pl.ds(0, 24, stride=2), :] = e
        t2[q, pl.ds(1, 24, stride=2), :] = e

    each(6, body)

    def body(i):
        p = i + 1
        u1[0, p, 8:56, :] = u1[1, p, 8:56, :] + jnp.where(w1[p] > 0.0, t2[p // 2], 0.0)

    each(10, body)
    sweep1(0, 1, 2, 8)
    sweep1(1, 0, 3, 6)

    def body(q):
        c = u1[0, q + 3, 12:52, :]
        e = mm(c, mt[...])
        t3[q, pl.ds(0, 40, stride=2), :] = e
        t3[q, pl.ds(1, 40, stride=2), :] = e
        t4[q, pl.ds(0, 40, stride=2), :] = c
        t4[q, pl.ds(1, 40, stride=2), :] = c

    each(6, body)

    def body(p):
        u0[0, p, :, :] = u0[1, p, :, :] + t3[(p + 1) // 2]

    each(10, body)

    def body(q, carry):
        lo, hi = carry
        for t in range(8):
            v = t4[q + 1, 8 + 8 * t : 16 + 8 * t, :]
            k = 16 * q + t
            here = (lane8 == k) | (lane8 == k + 8)
            a, b = roll(v, lax.rem(k + 97, 128)), roll(v, lax.rem(k + 32, 128))
            lo = jnp.where(lane8 == k, a, jnp.where(lane8 == k + 8, roll(a, 8), lo))
            hi = jnp.where(lane8 == k, b, jnp.where(lane8 == k + 8, roll(b, 8), hi))
        return lo, hi

    lo, hi = loop(4, body, (zero8, zero8))
    zr0[0, 0] = zr0[1, 0] + lo
    zr0[0, 1] = zr0[1, 1] + hi
    sweep0(u0.at[0], u0.at[2], zr0.at[0], ys0.at[2], zs0.at[2], False)
    start, wait = round0(2)
    start()
    wait()
    y_in(u0.at[2], yr0.at[2], 8, 64)
    sweep0(u0.at[2], u0.at[0], zr0.at[2], ys0.at[0], zs0.at[0], True)

    start, wait = round0(0)
    start()
    wait()
    y_in(u0.at[0], yr0.at[0], 8, 64)
    lo, hi = zr0[0, 0], zr0[0, 1]

    def body(x):
        c, s = beside0(u0.at[0], x, lo, hi)
        ores[0, x] = f0[x] - d0[x] * c + s

    each(8, body)


def on_device(phase, density, rhs):
    V = lambda *s: pltpu.VMEM(s, F32)
    M = pltpu.VMEM((384, 128), BF16)
    D = lambda *s: pltpu.SemaphoreType.DMA(s)
    scratch = [
        pltpu.VMEM((8, 64, 128), jnp.int32), V(8, 64, 128), V(8, 64, 128), V(10, 80, 128), V(3, 10, 80, 128),
        V(9, 64, 128), V(8, 80, 128), V(8, 64, 128), V(8, 64, 128), V(8, 64, 128), V(8, 64, 128),
        V(2, 8, 128), V(2, 8, 128), V(2, 8, 128), V(2, 8, 128),
        V(3, 2, 8, 128), V(3, 2, 8, 128), V(3, 2, 8, 128), V(3, 2, 8, 128),
        V(2, 12, 64, 128), V(4, 32, 128), V(5, 32, 128), V(4, 32, 128), V(4, 32, 128), V(4, 32, 128), V(4, 32, 128),
        V(4, 32, 128), V(12, 48, 128), V(4, 12, 64, 128),
        V(4, 2, 32, 128), V(2, 4, 8, 128), V(2, 4, 8, 128), V(2, 2, 8, 128),
        V(2, 4, 2, 32, 128), V(3, 2, 4, 8, 128), V(3, 2, 4, 8, 128), V(3, 2, 2, 8, 128),
        V(1, 2, 32, 128), V(2, 1, 8, 128), V(2, 1, 8, 128), V(2, 2, 8, 128),
        V(2, 1, 2, 32, 128), V(3, 2, 1, 8, 128), V(3, 2, 1, 8, 128), V(3, 2, 2, 8, 128),
        M, M, M, M, V(256, 128), V(4, 2, 64, 128), V(6, 48, 128), V(6, 80, 128), V(6, 80, 128), V(4, 4, 48, 128),
        V(12, 48, 128),
        V(3, 3, 4, 4, 8, 128), V(3, 3, 4, 8, 128),
        V(8, 48, 128), V(2, 12, 64, 128), V(9, 48, 128), V(8, 64, 128), V(8, 48, 128), V(8, 48, 128), V(8, 48, 128),
        V(4, 24, 128), V(2, 6, 40, 128), V(5, 24, 128), V(4, 40, 128), V(4, 24, 128), V(4, 24, 128),
        D(3), D(6), D(6), D(3, 6), D(3, 6), D(3, 3, 3), D(3, 3, 3), D(3, 3, 3), D(3, 3, 3),
        D(3), D(3), D(4), D(4), D(4, 3, 3), D(4, 3, 3),
    ]
    near = pl.BlockSpec(memory_space=pltpu.VMEM)
    return pl.pallas_call(
        kernel,
        out_shape=(pltpu.VMEM(rhs.shape, F32),) * 2,
        in_specs=[pl.BlockSpec(memory_space=pl.ANY)] * 3,
        out_specs=(near,) * 2,
        scratch_shapes=scratch,
        compiler_params=pltpu.CompilerParams(collective_id=0, has_side_effects=True),
        name="vcycle",
    )(phase, density, rhs)


def solution(mesh):
    in_specs = (P("gx", "gy", "gz"), P("gx", "gy", "gz"), P(None, "gx", "gy", "gz"))
    out_specs = (P(None, "gx", "gy", "gz"), P(None, "gx", "gy", "gz"))
    return jax.shard_map(on_device, mesh=mesh, in_specs=in_specs, out_specs=out_specs, check_vma=False)
```

```python
import functools

import jax
import jax.numpy as jnp
from jax import lax
from jax.experimental import pallas as pl
from jax.experimental.pallas import tpu as pltpu
from jax.sharding import PartitionSpec as P

MESH = pl.DeviceIdType.MESH
F32 = jnp.float32
W = 2.0 / 3.0
THIRD = 1.0 / 3.0
BF16 = jnp.bfloat16


def lanes(shape):
    return lax.broadcasted_iota(jnp.int32, shape, len(shape) - 1)


def roll(v, shift):
    return pltpu.roll(v, shift, 1)


def loop(count, body, init=0):
    return lax.fori_loop(0, count, body, init, unroll=True)


def each(count, body):
    def step(i, carry):
        body(i)
        return carry

    lax.fori_loop(0, count, step, 0, unroll=True)


def maps():
    row = lax.broadcasted_iota(jnp.int32, (128, 128), 0)
    col = lax.broadcasted_iota(jnp.int32, (128, 128), 1)
    hit = col == 32 + row // 2
    both = jnp.where(hit, 1.0, 0.0)
    odd = jnp.where(hit & (row % 2 == 1), 1.0, 0.0)
    even = jnp.where(hit & (row % 2 == 0), 1.0, 0.0)
    back = jnp.where(row == 32 + col // 2, 1.0, 0.0)
    return [jnp.concatenate([m.astype(BF16)] * 3, axis=0) for m in (both, odd, even, back)]


def mm(a, b):
    hi = a.astype(BF16)
    rest = a - hi.astype(F32)
    mid = rest.astype(BF16)
    low = (rest - mid.astype(F32)).astype(BF16)
    return lax.dot(jnp.concatenate([hi, mid, low], axis=1), b, preferred_element_type=F32)


def kernel(
    ph_h, de_h, rh_h, osol, ores,
    ph, de, f0, rp, u0, fx, fy, fzu, fzd, w0, d0,
    rys, ryr, rzs, rzr, ys0, yr0, zs0, zr0,
    u1, f1, fx1, fy1u, fy1d, fz1u, fz1d, d1, w1, ce1,
    pkc, xyc, zpc, xzc, yzc, rxc, ryc, rzc, rec, pkf, xyf, zpf, xzf, yzf, rxf, ryf, rzf, ref_,
    mb, mo, me, mt, t0, t1, t2, t3, t4, t5, f1e,
    cc, pz, zc, gg,
    f2, u2, fx2, fy2, fz2, w2, d2,
    f3, u3, fx3, fy3, fz3, w3,
    in_sem, rss, rrs, s0s, r0s, s1c, r1c, s1f, r1f, csx, crx, csn, crn, gs, gr,
):
    gx, gy, gz = lax.axis_index("gx"), lax.axis_index("gy"), lax.axis_index("gz")
    nx, ny, nz = lax.axis_size("gx"), lax.axis_size("gy"), lax.axis_size("gz")
    near = [
        ({"gx": gx + 1}, gx < nx - 1, gx > 0),
        ({"gx": gx - 1}, gx > 0, gx < nx - 1),
        ({"gy": gy + 1}, gy < ny - 1, gy > 0),
        ({"gy": gy - 1}, gy > 0, gy < ny - 1),
        ({"gz": gz + 1}, gz < nz - 1, gz > 0),
        ({"gz": gz - 1}, gz > 0, gz < nz - 1),
    ]

    loads = [
        pltpu.make_async_copy(ph_h, ph, in_sem.at[0]),
        pltpu.make_async_copy(de_h, de, in_sem.at[1]),
        pltpu.make_async_copy(rh_h.at[0], f0, in_sem.at[2]),
    ]
    for c in loads:
        c.start()

    edge = (gx == 0) | (gx == nx - 1) | (gy == 0) | (gy == ny - 1) | (gz == 0) | (gz == nz - 1)

    @pl.when(edge)
    def _():
        for ref in (ryc, rzc, rec):
            ref[...] = jnp.zeros(ref.shape, F32)

    barrier = pltpu.get_barrier_semaphore()
    arrivals = 0
    for where, ok, back in near:
        arrivals = arrivals + jnp.where(back, 1, 0)

        @pl.when(ok)
        def _(where=where):
            pl.semaphore_signal(barrier, inc=1, device_id=where, device_id_type=MESH)

    for b in range(3):
        for x in (0, 9):
            u0[b, x, 8:72, :] = jnp.zeros((64, 128), F32)
        for ref in (yr0, zr0):
            for k in range(2):
                ref[b, k] = jnp.zeros((8, 128), F32)

    @pl.when(edge)
    def _():
        for ref in (gg, zc, rxc, rxf, ryf, rzf, ref_):
            ref[...] = jnp.zeros(ref.shape, F32)
        for y in (0, 2):
            cc[y] = jnp.zeros(cc.shape[1:], F32)

    def inside(at, step, count):
        return (at >= 0) if step == 0 else (at < count - 1) if step > 0 else (at > 0)

    def yz_ok(sy, sz):
        return inside(gy, sy, ny) & inside(gz, sz, nz)

    def at(sx, sy, sz):
        return {"gx": sx, "gy": gy + sy, "gz": gz + sz}

    steps = (-1, 0, 1)

    def faces(buf, n, rows, ys, yr, zs, zr, ss, rs):
        body = pl.ds(8, rows)
        pairs = [
            (buf.at[n, body], buf.at[0, body]),
            (buf.at[1, body], buf.at[n + 1, body]),
            (ys.at[1], yr.at[0]),
            (ys.at[0], yr.at[1]),
            (zs.at[1], zr.at[0]),
            (zs.at[0], zr.at[1]),
        ]

        def copy(d):
            src, dst = pairs[d]
            return pltpu.make_async_remote_copy(
                src_ref=src, dst_ref=dst, send_sem=ss.at[d], recv_sem=rs.at[d],
                device_id=near[d][0], device_id_type=MESH,
            )

        def start():
            for d in range(6):
                @pl.when(near[d][1])
                def _(d=d):
                    copy(d).start()

        def wait():
            for d in range(6):
                @pl.when(near[d][1])
                def _(d=d):
                    copy(d).wait_send()

                @pl.when(near[d][2])
                def _(d=d):
                    copy(d).wait_recv()

        return start, wait

    lane8 = lanes((8, 128))
    lane64 = lanes((64, 128))
    lane32 = lanes((32, 128))

    zero8 = jnp.zeros((8, 128), F32)

    def pack0(carry, plane, x):
        lo, hi = carry
        for t in range(8):
            v = plane[8 * t : 8 * t + 8]
            k = x * 8 + t
            here = lane8 == k
            lo = jnp.where(here, roll(v, k), lo)
            hi = jnp.where(here, roll(v, k + 1), hi)
        return lo, hi

    def z_beside0(plane, x, lo, hi):
        right = jnp.concatenate([roll(hi, 127 - (x * 8 + t)) for t in range(8)], axis=0)
        left = jnp.concatenate([roll(lo, lax.rem(128 - (x * 8 + t), 128)) for t in range(8)], axis=0)
        return (
            jnp.where(lane64 == 127, right, roll(plane, 127)),
            jnp.where(lane64 == 0, left, roll(plane, 1)),
        )

    def keep0(buf, ys, x, plane):
        buf[x + 1, 8:72, :] = plane
        ys[0, pl.ds(x, 1), :] = plane[0:1]
        ys[1, pl.ds(x, 1), :] = plane[63:64]

    def y_in(buf, yr, n, rows):
        def body(x):
            buf[x + 1, 7:8, :] = yr[0, pl.ds(x, 1), :]
            buf[x + 1, 8 + rows : 9 + rows, :] = yr[1, pl.ds(x, 1), :]

        each(n, body)

    def beside0(buf, x, lo, hi):
        c = buf[x + 1, 8:72, :]
        up, down = z_beside0(c, x, lo, hi)
        s = fx[x + 1] * buf[x + 2, 8:72, :] + fx[x] * buf[x, 8:72, :]
        s = s + fy[x, 8:72, :] * buf[x + 1, 9:73, :] + fy[x, 7:71, :] * buf[x + 1, 7:71, :]
        s = s + fzu[x] * up + fzd[x] * down
        return c, s

    def sweep0(src, dst, zr, ys, zs, out):
        lo, hi = zr[0], zr[1]

        def body(x, carry):
            c, s = beside0(src, x, lo, hi)
            new = c * THIRD + w0[x] * (f0[x] + s)
            keep0(dst, ys, x, new)
            if out:
                osol[0, x] = d0[x] * new
            return pack0(carry, new, x)

        packed = loop(8, body, (zero8, zero8))
        zs[0] = packed[0]
        zs[1] = packed[1]

    for c in loads[:2]:
        c.wait()

    def body(x, carry):
        plane = jnp.where(ph[x] == 1, 1000.0, 1.0).astype(F32) * de[x]
        keep0(rp, rys, x, plane)
        return pack0(carry, plane, x)

    packed = loop(8, body, (zero8, zero8))
    rzs[0] = packed[0]
    rzs[1] = packed[1]

    pl.semaphore_wait(barrier, arrivals)
    start, wait = faces(rp, 8, 64, rys, ryr, rzs, rzr, rss, rrs)
    start()
    both, odd, even, back = maps()
    mb[...] = both
    mo[...] = odd
    me[...] = even
    mt[...] = back
    loads[2].wait()
    wait()

    @pl.when(gx == 0)
    def _():
        rp[0, 8:72, :] = rp[1, 8:72, :]

    @pl.when(gx == nx - 1)
    def _():
        rp[9, 8:72, :] = rp[8, 8:72, :]

    for ok, got, own, s in ((gy == 0, ryr, rys, 0), (gy == ny - 1, ryr, rys, 1), (gz == 0, rzr, rzs, 0), (gz == nz - 1, rzr, rzs, 1)):
        @pl.when(ok)
        def _(got=got, own=own, s=s):
            got[s] = own[s]

    y_in(rp, ryr, 8, 64)
    lo, hi = rzr[0], rzr[1]
    fx[0] = 2.0 / (rp[0, 8:72, :] + rp[1, 8:72, :])

    def body(x, carry):
        c = rp[x + 1, 8:72, :]
        up, down = z_beside0(c, x, lo, hi)
        xu = 2.0 / (c + rp[x + 2, 8:72, :])
        yu = 2.0 / (c + rp[x + 1, 9:73, :])
        zu = 2.0 / (c + up)
        zd = 2.0 / (c + down)
        fx[x + 1] = xu
        fy[x, 8:72, :] = yu
        fy[x, 7:8, :] = 2.0 / (c[0:1] + rp[x + 1, 7:8, :])
        fzu[x] = zu
        fzd[x] = zd
        diag = xu + fx[x] + yu + fy[x, 7:71, :] + zu + zd
        d0[x] = diag
        w = W / diag
        w0[x] = w
        first = w * f0[x]
        keep0(u0.at[0], ys0.at[0], x, first)
        return pack0(carry, first, x)

    packed = loop(8, body, (zero8, zero8))
    zs0[0, 0] = packed[0]
    zs0[0, 1] = packed[1]

    def round0(b):
        return faces(u0.at[b], 8, 64, ys0.at[b], yr0.at[b], zs0.at[b], zr0.at[b], s0s.at[b], r0s.at[b])

    box = [(a, b, c) for a in steps for b in steps for c in steps if (a, b, c) != (0, 0, 0)]

    def box_exchange(pk, xy, zp, xz, yz, rx, ry, rz, re, ss, rs):
        def copy(a, b, c):
            if b and c:
                src, dst = yz.at[(b + 1) // 2, (c + 1) // 2], re.at[1 - a, (1 - b) // 2, (1 - c) // 2]
            elif a and c:
                src, dst = xz.at[(c + 1) // 2], rz.at[1 - a, (1 - c) // 2, pl.ds(0, xz.shape[1])]
            elif c:
                src, dst = zp.at[(c + 1) // 2], rz.at[1 - a, (1 - c) // 2]
            elif b:
                src, dst = xy.at[(b + 1) // 2], ry.at[1 - a, (1 - b) // 2]
            else:
                src, dst = pk, rx.at[(1 - a) // 2]
            return pltpu.make_async_remote_copy(
                src_ref=src, dst_ref=dst, send_sem=ss.at[a + 1, b + 1, c + 1], recv_sem=rs.at[a + 1, b + 1, c + 1],
                device_id=at(gx + a, b, c), device_id_type=MESH,
            )

        def start(far=(1, 2, 3)):
            for n in sorted(far, reverse=True):
                for a, b, c in box:
                    if abs(a) + abs(b) + abs(c) == n:
                        @pl.when(inside(gx, a, nx) & yz_ok(b, c))
                        def _(a=a, b=b, c=c):
                            copy(a, b, c).start()

        def wait():
            for a, b, c in box:
                @pl.when(inside(gx, a, nx) & yz_ok(b, c))
                def _(a=a, b=b, c=c):
                    copy(a, b, c).wait_send()

                @pl.when(inside(gx, -a, nx) & yz_ok(-b, -c))
                def _(a=a, b=b, c=c):
                    copy(a, b, c).wait_recv()

        return start, wait

    row8 = lax.broadcasted_iota(jnp.int32, (8, 128), 0)

    low4 = lane8 % 8 < 4

    def half(v):
        return pltpu.roll(v, 4, 0)

    def pack_box(gets, pk, xy, zp, xz, yz):
        edge = {(b, c): zero8 for b in range(2) for c in range(2)}
        for a, get in enumerate(gets):
            planes = [get(x) for x in range(4)]
            pairs = [jnp.where(own1, planes[2 * i], roll(planes[2 * i + 1], 64)) for i in range(2)]
            for i in range(2):
                pk[a, i] = pairs[i]
            xy[0, a] = jnp.where(row8 < 4, pairs[0][0:8], half(pairs[1][0:8]))
            xy[1, a] = jnp.where(row8 >= 4, pairs[0][24:32], half(pairs[1][24:32]))
            face = [zero8, zero8]
            for x in range(4):
                for t in range(4):
                    v = planes[x][8 * t : 8 * t + 8]
                    k = x * 4 + t
                    for c, first in ((0, 96), (1, 40)):
                        face[c] = jnp.where(lane8 // 8 == k, roll(v, (8 * k + first) % 128), face[c])
                        if t in (0, 3):
                            b = t // 3
                            edge[b, c] = jnp.where(lane8 // 8 == 4 * a + x, roll(v, (32 * a + 8 * x + first) % 128), edge[b, c])
            zp[0, a] = face[0]
            zp[1, a] = face[1]
            if a % 2 == 0:
                even = face
            if a % 2 == 1:
                xz[0, a // 2] = jnp.where(low4, even[0], roll(face[0], 4))
                xz[1, a // 2] = jnp.where(low4, roll(face[1], 124), even[1])
            elif a == len(gets) - 1:
                xz[0, a // 2] = face[0]
                xz[1, a // 2] = face[1]
        for b in range(2):
            for c in range(2):
                yz[b, c] = edge[b, c]

    def unpack_box(own, rx, ry, rz, re, a, put):
        def side(dx, x, c, first):
            def corner(b):
                return roll(re[dx, b, c], (first - 32 * a - 8 * x) % 128)

            shift, i = (0, a) if dx == 1 else ((4 - 8 * c) * (a % 2), a // 2)
            mid = [roll(rz[dx, c, i], (first + shift - 8 * (4 * x + t)) % 128) for t in range(4)]
            return jnp.concatenate([corner(0)] + mid + [corner(1)], axis=0)

        for dx in range(3):
            for x in range(4):
                i = x // 2
                turn = (lambda v: roll(v, 64)) if x % 2 else (lambda v: v)
                flip = half if i else (lambda v: v)
                mid = own(x) if dx == 1 else turn(rx[dx // 2, a, i])
                centre = jnp.concatenate([turn(flip(ry[dx, 0, a])), mid, turn(flip(ry[dx, 1, a]))], axis=0)
                out = jnp.where((lane48 >= 96) & (lane48 < 100), side(dx, x, 1, 96), 0.0)
                out = jnp.where((lane48 >= 32) & (lane48 < 96), centre, out)
                out = jnp.where((lane48 >= 28) & (lane48 < 32), side(dx, x, 0, 24), out)
                put(4 * dx + x, out)

    lane48 = lanes((48, 128))
    start, wait = round0(0)
    start()

    own1 = (lane32 >= 32) & (lane32 < 96)

    def rows_of(ref, base, n, off):
        return ref[pl.ds(base + off, n, stride=2), :]

    def pair_rows(ref, base, n):
        return rows_of(ref, base, n, 0) + rows_of(ref, base, n, 1)

    for i in range(5):
        t0[0:64, :] = fx[2 * i]
        fx1[i] = mm(pair_rows(t0, 0, 32), mb[...])

    def body(i):
        yu = fy[2 * i, pl.ds(9, 32, stride=2), :] + fy[2 * i + 1, pl.ds(9, 32, stride=2), :]
        yd = fy[2 * i, pl.ds(7, 32, stride=2), :] + fy[2 * i + 1, pl.ds(7, 32, stride=2), :]
        t1[i, 0] = fzu[2 * i] + fzu[2 * i + 1]
        t1[i, 1] = fzd[2 * i] + fzd[2 * i + 1]
        zu = t1[i, 0, pl.ds(0, 32, stride=2), :] + t1[i, 0, pl.ds(1, 32, stride=2), :]
        zd = t1[i, 1, pl.ds(0, 32, stride=2), :] + t1[i, 1, pl.ds(1, 32, stride=2), :]
        yu, yd, zu, zd = mm(yu, mb[...]), mm(yd, mb[...]), mm(zu, mo[...]), mm(zd, me[...])
        fy1u[i] = yu
        fy1d[i] = yd
        fz1u[i] = zu
        fz1d[i] = zd
        diag = fx1[i] + fx1[i + 1] + yu + yd + zu + zd
        d1[i] = jnp.where(own1, diag, 0.0)

    each(4, body)
    parts1 = (lambda x: d1[x], lambda x: fx1[x + 1], lambda x: fy1u[x], lambda x: fz1u[x])
    pack_box(parts1, pkc, xyc, zpc, xzc, yzc)
    c_start, c_wait = box_exchange(pkc, xyc, zpc, xzc, yzc, rxc, ryc, rzc, rec, s1c, r1c)
    c_start((1,2))

    def pack2(planes):
        out = zero8
        for x in range(2):
            for t in range(2):
                g = 2 * x + t
                v = roll(planes[x][8 * t : 8 * t + 8], (32 * g - 48) % 128)
                out = jnp.where((lane8 >= 32 * g) & (lane8 < 32 * g + 32), v, out)
        return out

    xu, yu, zu, dg = [], [], [], []
    for i in range(2):
        t0[0:32, :] = fx1[2 * i]
        t0[32:64, :] = fx1[2 * i + 2]
        t0[64:96, :] = fz1u[2 * i] + fz1u[2 * i + 1]
        t0[96:128, :] = fz1d[2 * i] + fz1d[2 * i + 1]
        t0[128:160, :] = fy1u[2 * i] + fy1u[2 * i + 1]
        t0[160:192, :] = fy1d[2 * i] + fy1d[2 * i + 1]
        xd_, xu_ = mm(pair_rows(t0, 0, 16), mb[...]), mm(pair_rows(t0, 32, 16), mb[...])
        zu_, zd_ = mm(pair_rows(t0, 64, 16), mo[...]), mm(pair_rows(t0, 96, 16), me[...])
        yu_, yd_ = mm(rows_of(t0, 128, 16, 1), mb[...]), mm(rows_of(t0, 160, 16, 0), mb[...])
        xu.append(xu_)
        yu.append(yu_)
        zu.append(zu_)
        dg.append(xu_ + xd_ + yu_ + yd_ + zu_ + zd_)
    for a, planes in enumerate((dg, xu, yu, zu)):
        cc[1, gx, a] = pack2(planes)

    def gather(sx, rx, sn, rn):
        def xcopy(d):
            return pltpu.make_async_remote_copy(
                src_ref=cc.at[1, gx], dst_ref=cc.at[1, gx], send_sem=sx.at[d - 1], recv_sem=rx.at[d - 1],
                device_id={"gx": lax.rem(gx + d, nx)}, device_id_type=MESH,
            )

        def ncopy(d):
            src = [cc.at[1], cc.at[1], pz.at[1], pz.at[0]][d - 2]
            dst = [cc.at[0], cc.at[2], zc.at[0], zc.at[1]][d - 2]
            return pltpu.make_async_remote_copy(
                src_ref=src, dst_ref=dst, send_sem=sn.at[d - 2], recv_sem=rn.at[d - 2],
                device_id=near[d][0], device_id_type=MESH,
            )

        def xstart():
            for d in range(1, 4):
                xcopy(d).start()

        def xwait():
            for d in range(1, 4):
                pltpu.make_async_remote_copy(
                    src_ref=cc.at[1, gx], dst_ref=cc.at[1, lax.rem(gx + 4 - d, nx)],
                    send_sem=sx.at[d - 1], recv_sem=rx.at[d - 1],
                    device_id={"gx": lax.rem(gx + d, nx)}, device_id_type=MESH,
                ).wait()

        def nstart(ds):
            for d in ds:
                @pl.when(near[d][1])
                def _(d=d):
                    ncopy(d).start()

        def nwait(ds):
            for d in ds:
                @pl.when(near[d][1])
                def _(d=d):
                    ncopy(d).wait_send()

                @pl.when(near[d][2])
                def _(d=d):
                    ncopy(d).wait_recv()

        return (
            xstart, xwait,
            lambda: nstart((2, 3)), lambda: nwait((2, 3)),
            lambda: nstart((4, 5)), lambda: nwait((4, 5)),
        )

    cg = gather(csx, crx, csn, crn)

    wait()
    c_start((3,))
    cg[0]()
    y_in(u0.at[0], yr0.at[0], 8, 64)
    sweep0(u0.at[0], u0.at[1], zr0.at[0], ys0.at[1], zs0.at[1], False)
    start, wait = round0(1)
    start()
    wait()
    y_in(u0.at[1], yr0.at[1], 8, 64)

    cg[1]()
    cg[2]()
    lo, hi = zr0[1, 0], zr0[1, 1]

    def body(i):
        total = None
        for j in range(2):
            x = 2 * i + j
            c, s = beside0(u0.at[1], x, lo, hi)
            r = f0[x] - d0[x] * c + s
            total = r if total is None else total + r
        t1[i, 0] = total
        f1[i] = mm(t1[i, 0, pl.ds(0, 32, stride=2), :] + t1[i, 0, pl.ds(1, 32, stride=2), :], mb[...])

    each(4, body)

    pack_box([lambda x: f1[x]], pkf, xyf, zpf, xzf, yzf)
    f_start, f_wait = box_exchange(pkf, xyf, zpf, xzf, yzf, rxf, ryf, rzf, ref_, s1f, r1f)
    f_start()
    c_wait()
    cg[3]()
    low16 = lane8 % 32 < 16

    def body(y):
        for b in range(4):
            for j in range(2):
                v, w = cc[y, b, 2 * j], cc[y, b, 2 * j + 1]
                pz[0, y, b, j] = jnp.where(low16, v, roll(w, 16))
                pz[1, y, b, j] = jnp.where(low16, roll(w, 112), v)

    each(3, body)
    cg[4]()
    for a, get in enumerate(parts1):
        def put(p, out, a=a):
            ce1[a, p, 8:56, :] = out
            if a == 0:
                ok = out > 0.0
                w1[p] = jnp.where(ok, W / jnp.where(ok, out, 1.0), 0.0)

        unpack_box(get, rxc, ryc, rzc, rec, a, put)

    def zero_rows(ref, n, rows):
        def body(p):
            ref[p, 0:8, :] = zero8
            ref[p, 8 + rows : 16 + rows, :] = zero8

        each(n, body)

    zero_rows(ce1.at[2], 12, 48)
    for b in range(2):
        zero_rows(u1.at[b], 12, 48)
    f_wait()

    def put(p, out):
        f1e[p] = out
        u1[0, p, 8:56, :] = w1[p] * out

    unpack_box(lambda x: f1[x], rxf, ryf, rzf, ref_, 0, put)

    def beside1(buf, p, r0, n):
        c = buf[p, r0 : r0 + n, :]
        s = ce1[1, p, r0 : r0 + n, :] * buf[p + 1, r0 : r0 + n, :]
        s = s + ce1[1, p - 1, r0 : r0 + n, :] * buf[p - 1, r0 : r0 + n, :]
        s = s + ce1[2, p, r0 : r0 + n, :] * buf[p, r0 + 1 : r0 + 1 + n, :]
        s = s + ce1[2, p, r0 - 1 : r0 - 1 + n, :] * buf[p, r0 - 1 : r0 - 1 + n, :]
        z = ce1[3, p, r0 : r0 + n, :]
        return c, s + z * roll(c, 127) + roll(z * c, 1)

    def sweep1(src, dst, first, count):
        def body(i):
            p = i + first
            c, s = beside1(u1.at[src], p, 8, 48)
            u1[dst, p, 8:56, :] = c * THIRD + w1[p] * (f1e[p] + s)

        each(count, body)

    sweep1(0, 1, 1, 10)

    src2 = []
    for i in range(2):
        total = None
        for j in range(2):
            x = 2 * i + j
            c, s = beside1(u1.at[1], x + 4, 16, 32)
            r = f1[x] - d1[x] * c + s
            total = r if total is None else total + r
        t0[32 * i : 32 * i + 32, :] = jnp.where(own1, total, 0.0)
        src2.append(mm(pair_rows(t0, 32 * i, 16), mb[...]))
    gg[1, 1, gx] = pack2(src2)

    def fcopy(d, sy, sz):
        return pltpu.make_async_remote_copy(
            src_ref=gg.at[1, 1, gx], dst_ref=gg.at[1 - sz, 1 - sy, gx],
            send_sem=gs.at[d, sy + 1, sz + 1], recv_sem=gr.at[d, sy + 1, sz + 1],
            device_id=at(lax.rem(gx + d, nx), sy, sz), device_id_type=MESH,
        )

    def fback(d, sy, sz):
        return pltpu.make_async_remote_copy(
            src_ref=gg.at[1, 1, gx], dst_ref=gg.at[1 - sz, 1 - sy, lax.rem(gx + 4 - d, nx)],
            send_sem=gs.at[d, sy + 1, sz + 1], recv_sem=gr.at[d, sy + 1, sz + 1],
            device_id=at(lax.rem(gx + d, nx), sy, sz), device_id_type=MESH,
        )

    order = sorted([(sy, sz) for sy in steps for sz in steps], key=lambda o: -abs(o[0]) - abs(o[1]))

    def g_start():
        for sy, sz in order:
            @pl.when(yz_ok(sy, sz))
            def _(sy=sy, sz=sz):
                for d in (2, 1, 3, 0):
                    if (d, sy, sz) != (0, 0, 0):
                        fcopy(d, sy, sz).start()

    def g_wait():
        for sy, sz in order:
            @pl.when(yz_ok(sy, sz))
            def _(sy=sy, sz=sz):
                for d in range(4):
                    if (d, sy, sz) != (0, 0, 0):
                        fcopy(d, sy, sz).wait_send()

            @pl.when(yz_ok(-sy, -sz))
            def _(sy=sy, sz=sz):
                for d in range(4):
                    if (d, sy, sz) != (0, 0, 0):
                        fback(d, sy, sz).wait_recv()

    g_start()
    cg[5]()

    def spread2(get, put, shift, reach):
        def body(b):
            for y in range(3):
                v = [get(z, y, b) for z in range(3)]
                for x in range(2):
                    for t in range(2):
                        g = 2 * x + t
                        left = roll(v[0], (16 - 32 * g + shift) % 128)
                        mid = roll(v[1], (48 - 32 * g) % 128)
                        right = roll(v[2], (80 - 32 * g - shift) % 128)
                        out = jnp.where(lane8 < 48, left, jnp.where(lane8 < 80, mid, right))
                        out = jnp.where((lane8 >= 48 - reach) & (lane8 < 80 + reach), out, 0.0)
                        put(2 * b + x, 16 * y + 8 * t, out)

        each(4, body)

    def put_d(p, r, v):
        d2[p, r : r + 8, :] = v
        ok = v > 0.0
        w2[p, r : r + 8, :] = jnp.where(ok, W / jnp.where(ok, v, 1.0), 0.0)

    def put_x(p, r, v):
        fx2[p + 1, r : r + 8, :] = v

    def put_y(p, r, v):
        fy2[p, 8 + r : 16 + r, :] = v

    def put_z(p, r, v):
        fz2[p, r : r + 8, :] = v

    def put_f(p, r, v):
        f2[p, r : r + 8, :] = v
        u2[0, p + 2, 8 + r : 16 + r, :] = w2[p, r : r + 8, :] * v

    for a, put in enumerate((put_d, put_x, put_y, put_z)):
        spread2(lambda z, y, b, a=a: cc[y, b, a] if z == 1 else zc[z // 2, y, b, a // 2], put, 16 * (a % 2), 16)
    fx2[0] = jnp.zeros((48, 128), F32)
    fx3[0] = jnp.zeros((24, 128), F32)

    zero_rows(fy2, 8, 48)
    zero_rows(fy3, 4, 24)
    for b in range(2):
        zero_rows(u2.at[b], 12, 48)
        zero_rows(u3.at[b], 6, 24)
        for p in (0, 1, 10, 11):
            u2[b, p, 8:56, :] = jnp.zeros((48, 128), F32)
        for p in (0, 5):
            u3[b, p, 8:32, :] = jnp.zeros((24, 128), F32)

    row48 = lax.broadcasted_iota(jnp.int32, (48, 128), 0)

    def body(p):
        a, b = 2 * p, 2 * p + 1
        t5[p, 0] = fx2[b + 1]
        t5[p, 1] = fz2[a] + fz2[b]
        ysum = fy2[a, 8:56, :] + fy2[b, 8:56, :]
        t5[p, 2] = ysum
        inner = fx2[a + 1]
        inner = inner + jnp.where(row48 % 2 == 0, ysum, 0.0)
        inner = inner + jnp.where(lane48 % 2 == 0, fz2[a] + fz2[b], 0.0)
        t5[p, 3] = d2[a] + d2[b] - 2.0 * inner
        pick = lambda q, off: t5[p, q, pl.ds(off, 24, stride=2), :]
        fx3[p + 1] = mm(pick(0, 0) + pick(0, 1), mb[...])
        fz3[p] = mm(pick(1, 0) + pick(1, 1), mo[...])
        fy3[p, 8:32, :] = mm(pick(2, 1), mb[...])
        diag = mm(pick(3, 0) + pick(3, 1), mb[...])
        ok = diag > 0.0
        w3[p] = jnp.where(ok, W / jnp.where(ok, diag, 1.0), 0.0)

    each(4, body)

    g_wait()
    spread2(lambda z, y, b: gg[z, y, b], put_f, 0, 32)

    def beside(buf, fxr, fyr, fzr, p, rows):
        c = buf[p + 1, 8 : 8 + rows, :]
        s = fxr[p + 1] * buf[p + 2, 8 : 8 + rows, :] + fxr[p] * buf[p, 8 : 8 + rows, :]
        s = s + fyr[p, 8 : 8 + rows, :] * buf[p + 1, 9 : 9 + rows, :]
        s = s + fyr[p, 7 : 7 + rows, :] * buf[p + 1, 7 : 7 + rows, :]
        z = fzr[p]
        return c, s + z * roll(c, 127) + roll(z * c, 1)

    def sweep2(src, dst):
        def body(p):
            c, s = beside(u2.at[src, pl.ds(1, 10)], fx2, fy2, fz2, p, 48)
            u2[dst, p + 2, 8:56, :] = c * THIRD + w2[p] * (f2[p] + s)

        each(8, body)

    def sweep3(src, dst):
        def body(p):
            c, s = beside(u3.at[src], fx3, fy3, fz3, p, 24)
            u3[dst, p + 1, 8:32, :] = c * THIRD + w3[p] * (f3[p] + s)

        each(4, body)

    sweep2(0, 1)

    def body(p):
        total = None
        for j in range(2):
            c, s = beside(u2.at[1, pl.ds(1, 10)], fx2, fy2, fz2, 2 * p + j, 48)
            r = f2[2 * p + j] - d2[2 * p + j] * c + s
            total = r if total is None else total + r
        t5[p, 0] = total
        src = mm(t5[p, 0, pl.ds(0, 24, stride=2), :] + t5[p, 0, pl.ds(1, 24, stride=2), :], mb[...])
        f3[p] = src
        u3[0, p + 1, 8:32, :] = w3[p] * src

    each(4, body)
    sweep3(0, 1)
    sweep3(1, 0)
    sweep3(0, 1)

    def body(p):
        e = mm(u3[1, p + 1, 8:32, :], mt[...])
        t5[p, 1, pl.ds(0, 24, stride=2), :] = e
        t5[p, 1, pl.ds(1, 24, stride=2), :] = e
        wide = t5[p, 1]
        for j in range(2):
            q = 2 * p + j
            u2[0, q + 2, 8:56, :] = u2[1, q + 2, 8:56, :] + jnp.where(d2[q] > 0.0, wide, 0.0)

    each(4, body)
    sweep2(0, 1)
    sweep2(1, 0)

    def body(q):
        e = mm(u2[0, 2 * gx + q, 20:44, :], mt[...])
        t2[q, pl.ds(0, 24, stride=2), :] = e
        t2[q, pl.ds(1, 24, stride=2), :] = e

    each(6, body)

    def body(i):
        p = i + 1
        u1[0, p, 8:56, :] = u1[1, p, 8:56, :] + jnp.where(w1[p] > 0.0, t2[p // 2], 0.0)

    each(10, body)
    sweep1(0, 1, 2, 8)
    sweep1(1, 0, 3, 6)

    def body(q):
        c = u1[0, q + 3, 12:52, :]
        e = mm(c, mt[...])
        t3[q, pl.ds(0, 40, stride=2), :] = e
        t3[q, pl.ds(1, 40, stride=2), :] = e
        t4[q, pl.ds(0, 40, stride=2), :] = c
        t4[q, pl.ds(1, 40, stride=2), :] = c

    each(6, body)

    def body(p):
        u0[0, p, :, :] = u0[1, p, :, :] + t3[(p + 1) // 2]

    each(10, body)

    def body(q, carry):
        lo, hi = carry
        for t in range(8):
            v = t4[q + 1, 8 + 8 * t : 16 + 8 * t, :]
            k = 16 * q + t
            here = (lane8 == k) | (lane8 == k + 8)
            a, b = roll(v, lax.rem(k + 97, 128)), roll(v, lax.rem(k + 32, 128))
            lo = jnp.where(lane8 == k, a, jnp.where(lane8 == k + 8, roll(a, 8), lo))
            hi = jnp.where(lane8 == k, b, jnp.where(lane8 == k + 8, roll(b, 8), hi))
        return lo, hi

    lo, hi = loop(4, body, (zero8, zero8))
    zr0[0, 0] = zr0[1, 0] + lo
    zr0[0, 1] = zr0[1, 1] + hi
    sweep0(u0.at[0], u0.at[2], zr0.at[0], ys0.at[2], zs0.at[2], False)
    start, wait = round0(2)
    start()
    wait()
    y_in(u0.at[2], yr0.at[2], 8, 64)
    sweep0(u0.at[2], u0.at[0], zr0.at[2], ys0.at[0], zs0.at[0], True)

    start, wait = round0(0)
    start()
    wait()
    y_in(u0.at[0], yr0.at[0], 8, 64)
    lo, hi = zr0[0, 0], zr0[0, 1]

    def body(x):
        c, s = beside0(u0.at[0], x, lo, hi)
        ores[0, x] = f0[x] - d0[x] * c + s

    each(8, body)


def flush(a, b, oa, ob, sem):
    copies = [pltpu.make_async_copy(a, oa, sem.at[0]), pltpu.make_async_copy(b, ob, sem.at[1])]
    for c in copies:
        c.start()
    for c in copies:
        c.wait()


def on_device(phase, density, rhs):
    V = lambda *s: pltpu.VMEM(s, F32)
    M = pltpu.VMEM((384, 128), BF16)
    D = lambda *s: pltpu.SemaphoreType.DMA(s)
    scratch = [
        pltpu.VMEM((8, 64, 128), jnp.int32), V(8, 64, 128), V(8, 64, 128), V(10, 80, 128), V(3, 10, 80, 128),
        V(9, 64, 128), V(8, 80, 128), V(8, 64, 128), V(8, 64, 128), V(8, 64, 128), V(8, 64, 128),
        V(2, 8, 128), V(2, 8, 128), V(2, 8, 128), V(2, 8, 128),
        V(3, 2, 8, 128), V(3, 2, 8, 128), V(3, 2, 8, 128), V(3, 2, 8, 128),
        V(2, 12, 64, 128), V(4, 32, 128), V(5, 32, 128), V(4, 32, 128), V(4, 32, 128), V(4, 32, 128), V(4, 32, 128),
        V(4, 32, 128), V(12, 48, 128), V(4, 12, 64, 128),
        V(4, 2, 32, 128), V(2, 4, 8, 128), V(2, 4, 8, 128), V(2, 2, 8, 128), V(2, 2, 8, 128),
        V(2, 4, 2, 32, 128), V(3, 2, 4, 8, 128), V(3, 2, 4, 8, 128), V(3, 2, 2, 8, 128),
        V(1, 2, 32, 128), V(2, 1, 8, 128), V(2, 1, 8, 128), V(2, 1, 8, 128), V(2, 2, 8, 128),
        V(2, 1, 2, 32, 128), V(3, 2, 1, 8, 128), V(3, 2, 1, 8, 128), V(3, 2, 2, 8, 128),
        M, M, M, M, V(256, 128), V(4, 2, 64, 128), V(6, 48, 128), V(6, 80, 128), V(6, 80, 128), V(4, 4, 48, 128),
        V(12, 48, 128),
        V(3, 4, 4, 8, 128), V(2, 3, 4, 2, 8, 128), V(2, 3, 4, 2, 8, 128), V(3, 3, 4, 8, 128),
        V(8, 48, 128), V(2, 12, 64, 128), V(9, 48, 128), V(8, 64, 128), V(8, 48, 128), V(8, 48, 128), V(8, 48, 128),
        V(4, 24, 128), V(2, 6, 40, 128), V(5, 24, 128), V(4, 40, 128), V(4, 24, 128), V(4, 24, 128),
        D(3), D(6), D(6), D(3, 6), D(3, 6), D(3, 3, 3), D(3, 3, 3), D(3, 3, 3), D(3, 3, 3),
        D(3), D(3), D(4), D(4), D(4, 3, 3), D(4, 3, 3),
    ]
    near = pl.BlockSpec(memory_space=pltpu.VMEM)
    pair = pl.pallas_call(
        kernel,
        out_shape=(pltpu.VMEM(rhs.shape, F32),) * 2,
        in_specs=[pl.BlockSpec(memory_space=pl.ANY)] * 3,
        out_specs=(near,) * 2,
        scratch_shapes=scratch,
        compiler_params=pltpu.CompilerParams(collective_id=0, has_side_effects=True),
        name="vcycle",
    )(phase, density, rhs)
    pair = [pltpu.with_memory_space_constraint(v, pltpu.VMEM) for v in pair]
    return pl.pallas_call(
        flush,
        out_shape=(jax.ShapeDtypeStruct(rhs.shape, F32),) * 2,
        in_specs=[near] * 2,
        out_specs=(pl.BlockSpec(memory_space=pl.ANY),) * 2,
        scratch_shapes=[D(2)],
        name="flush",
    )(*pair)


def solution(mesh):
    in_specs = (P("gx", "gy", "gz"), P("gx", "gy", "gz"), P(None, "gx", "gy", "gz"))
    out_specs = (P(None, "gx", "gy", "gz"), P(None, "gx", "gy", "gz"))
    return jax.shard_map(on_device, mesh=mesh, in_specs=in_specs, out_specs=out_specs, check_vma=False)
```

```python
import functools

import jax
import jax.numpy as jnp
from jax import lax
from jax.experimental import pallas as pl
from jax.experimental.pallas import tpu as pltpu
from jax.sharding import PartitionSpec as P

MESH = pl.DeviceIdType.MESH
F32 = jnp.float32
W = 2.0 / 3.0
THIRD = 1.0 / 3.0
BF16 = jnp.bfloat16


def lanes(shape):
    return lax.broadcasted_iota(jnp.int32, shape, len(shape) - 1)


def roll(v, shift):
    return pltpu.roll(v, shift, 1)


def loop(count, body, init=0):
    return lax.fori_loop(0, count, body, init, unroll=True)


def each(count, body):
    def step(i, carry):
        body(i)
        return carry

    lax.fori_loop(0, count, step, 0, unroll=True)


def maps():
    row = lax.broadcasted_iota(jnp.int32, (128, 128), 0)
    col = lax.broadcasted_iota(jnp.int32, (128, 128), 1)
    hit = col == 32 + row // 2
    both = jnp.where(hit, 1.0, 0.0)
    odd = jnp.where(hit & (row % 2 == 1), 1.0, 0.0)
    even = jnp.where(hit & (row % 2 == 0), 1.0, 0.0)
    back = jnp.where(row == 32 + col // 2, 1.0, 0.0)
    return [jnp.concatenate([m.astype(BF16)] * 3, axis=0) for m in (both, odd, even, back)]


def mm(a, b):
    hi = a.astype(BF16)
    rest = a - hi.astype(F32)
    mid = rest.astype(BF16)
    low = (rest - mid.astype(F32)).astype(BF16)
    return lax.dot(jnp.concatenate([hi, mid, low], axis=1), b, preferred_element_type=F32)


def kernel(
    ph_h, de_h, rh_h, osol, ores,
    ph, de, f0, part, fze, rp, u0, fx, fy, fzu, fzd, w0, d0,
    rys, ryr, rzs, rzr, ys0, yr0, zs0, zr0,
    u1, f1, fx1, fy1u, fy1d, fz1u, fz1d, d1, w1, ce1,
    pkc, xyc, zpc, xzc, yzc, rxc, ryc, rzc, rec, pkf, xyf, zpf, xzf, yzf, rxf, ryf, rzf, ref_,
    mb, mo, me, mt, t0, t1, t2, t3, t4, t5, f1e,
    cc, pz, zc, gg,
    f2, u2, fx2, fy2, fz2, w2, d2,
    f3, u3, fx3, fy3, fz3, w3,
    in_sem, rss, rrs, s0s, r0s, s1c, r1c, s1f, r1f, csx, crx, csn, crn, gs, gr,
):
    gx, gy, gz = lax.axis_index("gx"), lax.axis_index("gy"), lax.axis_index("gz")
    nx, ny, nz = lax.axis_size("gx"), lax.axis_size("gy"), lax.axis_size("gz")
    near = [
        ({"gx": gx + 1}, gx < nx - 1, gx > 0),
        ({"gx": gx - 1}, gx > 0, gx < nx - 1),
        ({"gy": gy + 1}, gy < ny - 1, gy > 0),
        ({"gy": gy - 1}, gy > 0, gy < ny - 1),
        ({"gz": gz + 1}, gz < nz - 1, gz > 0),
        ({"gz": gz - 1}, gz > 0, gz < nz - 1),
    ]

    loads = [
        pltpu.make_async_copy(ph_h, ph, in_sem.at[0]),
        pltpu.make_async_copy(de_h, de, in_sem.at[1]),
        pltpu.make_async_copy(rh_h.at[0], f0, in_sem.at[2]),
    ]
    for c in loads:
        c.start()

    edge = (gx == 0) | (gx == nx - 1) | (gy == 0) | (gy == ny - 1) | (gz == 0) | (gz == nz - 1)

    @pl.when(edge)
    def _():
        for ref in (ryc, rzc, rec):
            ref[...] = jnp.zeros(ref.shape, F32)

    barrier = pltpu.get_barrier_semaphore()
    arrivals = 0
    for where, ok, back in near:
        arrivals = arrivals + jnp.where(back, 1, 0)

        @pl.when(ok)
        def _(where=where):
            pl.semaphore_signal(barrier, inc=1, device_id=where, device_id_type=MESH)

    for b in range(3):
        for x in (0, 9):
            u0[b, x, 8:72, :] = jnp.zeros((64, 128), F32)
        for ref in (yr0, zr0):
            for k in range(2):
                ref[b, k] = jnp.zeros((8, 128), F32)

    @pl.when(edge)
    def _():
        for ref in (gg, zc, rxc, rxf, ryf, rzf, ref_):
            ref[...] = jnp.zeros(ref.shape, F32)
        for y in (0, 2):
            cc[y] = jnp.zeros(cc.shape[1:], F32)

    def inside(at, step, count):
        return (at >= 0) if step == 0 else (at < count - 1) if step > 0 else (at > 0)

    def yz_ok(sy, sz):
        return inside(gy, sy, ny) & inside(gz, sz, nz)

    def at(sx, sy, sz):
        return {"gx": sx, "gy": gy + sy, "gz": gz + sz}

    steps = (-1, 0, 1)

    def faces(buf, n, rows, ys, yr, zs, zr, ss, rs):
        body = pl.ds(8, rows)
        pairs = [
            (buf.at[n, body], buf.at[0, body]),
            (buf.at[1, body], buf.at[n + 1, body]),
            (ys.at[1], yr.at[0]),
            (ys.at[0], yr.at[1]),
            (zs.at[1], zr.at[0]),
            (zs.at[0], zr.at[1]),
        ]

        def copy(d):
            src, dst = pairs[d]
            return pltpu.make_async_remote_copy(
                src_ref=src, dst_ref=dst, send_sem=ss.at[d], recv_sem=rs.at[d],
                device_id=near[d][0], device_id_type=MESH,
            )

        def start():
            for d in range(6):
                @pl.when(near[d][1])
                def _(d=d):
                    copy(d).start()

        def wait():
            for d in range(6):
                @pl.when(near[d][1])
                def _(d=d):
                    copy(d).wait_send()

                @pl.when(near[d][2])
                def _(d=d):
                    copy(d).wait_recv()

        return start, wait

    lane8 = lanes((8, 128))
    lane64 = lanes((64, 128))
    lane32 = lanes((32, 128))

    zero8 = jnp.zeros((8, 128), F32)

    def pack0(carry, plane, x):
        lo, hi = carry
        for t in range(8):
            v = plane[8 * t : 8 * t + 8]
            k = x * 8 + t
            here = lane8 == k
            lo = jnp.where(here, roll(v, k), lo)
            hi = jnp.where(here, roll(v, k + 1), hi)
        return lo, hi

    def z_beside0(plane, x, lo, hi):
        right = jnp.concatenate([roll(hi, 127 - (x * 8 + t)) for t in range(8)], axis=0)
        left = jnp.concatenate([roll(lo, lax.rem(128 - (x * 8 + t), 128)) for t in range(8)], axis=0)
        return (
            jnp.where(lane64 == 127, right, roll(plane, 127)),
            jnp.where(lane64 == 0, left, roll(plane, 1)),
        )

    def keep0(buf, ys, x, plane):
        buf[x + 1, 8:72, :] = plane
        ys[0, pl.ds(x, 1), :] = plane[0:1]
        ys[1, pl.ds(x, 1), :] = plane[63:64]

    def y_in(buf, yr, n, rows):
        def body(x):
            buf[x + 1, 7:8, :] = yr[0, pl.ds(x, 1), :]
            buf[x + 1, 8 + rows : 9 + rows, :] = yr[1, pl.ds(x, 1), :]

        each(n, body)

    def mod(v):
        return v % 128 if isinstance(v, int) else lax.rem(v, 128)

    def packz(acc, plane, x):
        for t in range(8):
            v = plane[8 * t : 8 * t + 8]
            k = 2 * (x * 8 + t)
            acc = jnp.where(lane8 == k, roll(v, mod(k + 1)), acc)
            acc = jnp.where(lane8 == mod(k + 127), roll(v, mod(k + 127)), acc)
        return acc

    def heldz(zr):
        return jnp.where(lane8 % 2 == 0, zr[0], zr[1])

    def keepu(buf, ys, x, plane):
        keep0(buf, ys, x, plane)
        buf[x + 1, 7:8, :] = jnp.zeros((1, 128), F32)
        buf[x + 1, 72:73, :] = jnp.zeros((1, 128), F32)

    def within0(buf, x, whole):
        c = buf[x + 1, 8:72, :]
        s = fy[x, 8:72, :] * buf[x + 1, 9:73, :] + fy[x, 7:71, :] * buf[x + 1, 7:71, :]
        s = s + fzu[x] * jnp.where(lane64 == 127, 0.0, roll(c, 127))
        s = s + fzd[x] * jnp.where(lane64 == 0, 0.0, roll(c, 1))
        if whole or x < 7:
            s = s + fx[x + 1] * buf[x + 2, 8:72, :]
        if whole or x > 0:
            s = s + fx[x] * buf[x, 8:72, :]
        return c, s

    def zface0(x, held):
        return fze[x] * jnp.concatenate([roll(held, mod(256 - 2 * (x * 8 + t))) for t in range(8)], axis=0)

    def across0(buf, yr, held, x):
        h = zface0(x, held)
        if x == 0:
            h = h + fx[0] * buf[0, 8:72, :]
        if x == 7:
            h = h + fx[8] * buf[9, 8:72, :]
        top = fy[x, 7:8, :] * yr[0, x : x + 1, :]
        end = fy[x, 71:72, :] * yr[1, x : x + 1, :]
        return jnp.concatenate(
            [h[0:8] + jnp.where(row8 == 0, top, 0.0), h[8:56], h[56:64] + jnp.where(row8 == 7, end, 0.0)], axis=0
        )

    def inner0(buf, resid):
        for x in range(8):
            c, s = within0(buf, x, False)
            part[x] = f0[x] - d0[x] * c + s if resid else c * THIRD + w0[x] * (f0[x] + s)

    def outer0(src, yr, zr, dst, ys, zs, out):
        held = heldz(zr)
        acc = zero8
        for x in range(8):
            new = part[x] + w0[x] * across0(src, yr, held, x)
            keepu(dst, ys, x, new)
            if out:
                osol[0, x] = d0[x] * new
            acc = packz(acc, new, x)
        zs[0] = acc
        zs[1] = acc

    row8 = lax.broadcasted_iota(jnp.int32, (8, 128), 0)

    for c in loads[:2]:
        c.wait()

    def body(x, carry):
        plane = jnp.where(ph[x] == 1, 1000.0, 1.0).astype(F32) * de[x]
        keep0(rp, rys, x, plane)
        return pack0(carry, plane, x)

    packed = loop(8, body, (zero8, zero8))
    rzs[0] = packed[0]
    rzs[1] = packed[1]

    pl.semaphore_wait(barrier, arrivals)
    start, wait = faces(rp, 8, 64, rys, ryr, rzs, rzr, rss, rrs)
    start()
    both, odd, even, back = maps()
    mb[...] = both
    mo[...] = odd
    me[...] = even
    mt[...] = back
    loads[2].wait()
    wait()

    @pl.when(gx == 0)
    def _():
        rp[0, 8:72, :] = rp[1, 8:72, :]

    @pl.when(gx == nx - 1)
    def _():
        rp[9, 8:72, :] = rp[8, 8:72, :]

    for ok, got, own, s in ((gy == 0, ryr, rys, 0), (gy == ny - 1, ryr, rys, 1), (gz == 0, rzr, rzs, 0), (gz == nz - 1, rzr, rzs, 1)):
        @pl.when(ok)
        def _(got=got, own=own, s=s):
            got[s] = own[s]

    y_in(rp, ryr, 8, 64)
    lo, hi = rzr[0], rzr[1]
    fx[0] = 2.0 / (rp[0, 8:72, :] + rp[1, 8:72, :])

    def body(x, carry):
        c = rp[x + 1, 8:72, :]
        up, down = z_beside0(c, x, lo, hi)
        xu = 2.0 / (c + rp[x + 2, 8:72, :])
        yu = 2.0 / (c + rp[x + 1, 9:73, :])
        zu = 2.0 / (c + up)
        zd = 2.0 / (c + down)
        fx[x + 1] = xu
        fy[x, 8:72, :] = yu
        fy[x, 7:8, :] = 2.0 / (c[0:1] + rp[x + 1, 7:8, :])
        fzu[x] = zu
        fzd[x] = zd
        diag = xu + fx[x] + yu + fy[x, 7:71, :] + zu + zd
        d0[x] = diag
        w = W / diag
        w0[x] = w
        first = w * f0[x]
        fze[x] = jnp.where(lane64 == 127, zu, jnp.where(lane64 == 0, zd, 0.0))
        keepu(u0.at[0], ys0.at[0], x, first)
        return packz(carry, first, x)

    packed = loop(8, body, zero8)
    zs0[0, 0] = packed
    zs0[0, 1] = packed

    def round0(b):
        return faces(u0.at[b], 8, 64, ys0.at[b], yr0.at[b], zs0.at[b], zr0.at[b], s0s.at[b], r0s.at[b])

    box = [(a, b, c) for a in steps for b in steps for c in steps if (a, b, c) != (0, 0, 0)]

    def box_exchange(pk, xy, zp, xz, yz, rx, ry, rz, re, ss, rs):
        def copy(a, b, c):
            if b and c:
                src, dst = yz.at[(b + 1) // 2, (c + 1) // 2], re.at[1 - a, (1 - b) // 2, (1 - c) // 2]
            elif a and c:
                src, dst = xz.at[(c + 1) // 2], rz.at[1 - a, (1 - c) // 2, pl.ds(0, xz.shape[1])]
            elif c:
                src, dst = zp.at[(c + 1) // 2], rz.at[1 - a, (1 - c) // 2]
            elif b:
                src, dst = xy.at[(b + 1) // 2], ry.at[1 - a, (1 - b) // 2]
            else:
                src, dst = pk, rx.at[(1 - a) // 2]
            return pltpu.make_async_remote_copy(
                src_ref=src, dst_ref=dst, send_sem=ss.at[a + 1, b + 1, c + 1], recv_sem=rs.at[a + 1, b + 1, c + 1],
                device_id=at(gx + a, b, c), device_id_type=MESH,
            )

        def start(far=(1, 2, 3)):
            for n in sorted(far, reverse=True):
                for a, b, c in box:
                    if abs(a) + abs(b) + abs(c) == n:
                        @pl.when(inside(gx, a, nx) & yz_ok(b, c))
                        def _(a=a, b=b, c=c):
                            copy(a, b, c).start()

        def wait():
            for a, b, c in box:
                @pl.when(inside(gx, a, nx) & yz_ok(b, c))
                def _(a=a, b=b, c=c):
                    copy(a, b, c).wait_send()

                @pl.when(inside(gx, -a, nx) & yz_ok(-b, -c))
                def _(a=a, b=b, c=c):
                    copy(a, b, c).wait_recv()

        return start, wait

    low4 = lane8 % 8 < 4

    def half(v):
        return pltpu.roll(v, 4, 0)

    def pack_box(gets, pk, xy, zp, xz, yz):
        edge = {(b, c): zero8 for b in range(2) for c in range(2)}
        for a, get in enumerate(gets):
            planes = [get(x) for x in range(4)]
            pairs = [jnp.where(own1, planes[2 * i], roll(planes[2 * i + 1], 64)) for i in range(2)]
            for i in range(2):
                pk[a, i] = pairs[i]
            xy[0, a] = jnp.where(row8 < 4, pairs[0][0:8], half(pairs[1][0:8]))
            xy[1, a] = jnp.where(row8 >= 4, pairs[0][24:32], half(pairs[1][24:32]))
            face = [zero8, zero8]
            for x in range(4):
                for t in range(4):
                    v = planes[x][8 * t : 8 * t + 8]
                    k = x * 4 + t
                    for c, first in ((0, 96), (1, 40)):
                        face[c] = jnp.where(lane8 // 8 == k, roll(v, (8 * k + first) % 128), face[c])
                        if t in (0, 3):
                            b = t // 3
                            edge[b, c] = jnp.where(lane8 // 8 == 4 * a + x, roll(v, (32 * a + 8 * x + first) % 128), edge[b, c])
            zp[0, a] = face[0]
            zp[1, a] = face[1]
            if a % 2 == 0:
                even = face
            if a % 2 == 1:
                xz[0, a // 2] = jnp.where(low4, even[0], roll(face[0], 4))
                xz[1, a // 2] = jnp.where(low4, roll(face[1], 124), even[1])
            elif a == len(gets) - 1:
                xz[0, a // 2] = face[0]
                xz[1, a // 2] = face[1]
        for b in range(2):
            for c in range(2):
                yz[b, c] = edge[b, c]

    def unpack_box(own, rx, ry, rz, re, a, put):
        def side(dx, x, c, first):
            def corner(b):
                return roll(re[dx, b, c], (first - 32 * a - 8 * x) % 128)

            shift, i = (0, a) if dx == 1 else ((4 - 8 * c) * (a % 2), a // 2)
            mid = [roll(rz[dx, c, i], (first + shift - 8 * (4 * x + t)) % 128) for t in range(4)]
            return jnp.concatenate([corner(0)] + mid + [corner(1)], axis=0)

        for dx in range(3):
            for x in range(4):
                i = x // 2
                turn = (lambda v: roll(v, 64)) if x % 2 else (lambda v: v)
                flip = half if i else (lambda v: v)
                mid = own(x) if dx == 1 else turn(rx[dx // 2, a, i])
                centre = jnp.concatenate([turn(flip(ry[dx, 0, a])), mid, turn(flip(ry[dx, 1, a]))], axis=0)
                out = jnp.where((lane48 >= 96) & (lane48 < 100), side(dx, x, 1, 96), 0.0)
                out = jnp.where((lane48 >= 32) & (lane48 < 96), centre, out)
                out = jnp.where((lane48 >= 28) & (lane48 < 32), side(dx, x, 0, 24), out)
                put(4 * dx + x, out)

    lane48 = lanes((48, 128))
    start, wait = round0(0)
    start()

    own1 = (lane32 >= 32) & (lane32 < 96)

    def rows_of(ref, base, n, off):
        return ref[pl.ds(base + off, n, stride=2), :]

    def pair_rows(ref, base, n):
        return rows_of(ref, base, n, 0) + rows_of(ref, base, n, 1)

    for i in range(5):
        t0[0:64, :] = fx[2 * i]
        fx1[i] = mm(pair_rows(t0, 0, 32), mb[...])

    def body(i):
        yu = fy[2 * i, pl.ds(9, 32, stride=2), :] + fy[2 * i + 1, pl.ds(9, 32, stride=2), :]
        yd = fy[2 * i, pl.ds(7, 32, stride=2), :] + fy[2 * i + 1, pl.ds(7, 32, stride=2), :]
        t1[i, 0] = fzu[2 * i] + fzu[2 * i + 1]
        t1[i, 1] = fzd[2 * i] + fzd[2 * i + 1]
        zu = t1[i, 0, pl.ds(0, 32, stride=2), :] + t1[i, 0, pl.ds(1, 32, stride=2), :]
        zd = t1[i, 1, pl.ds(0, 32, stride=2), :] + t1[i, 1, pl.ds(1, 32, stride=2), :]
        yu, yd, zu, zd = mm(yu, mb[...]), mm(yd, mb[...]), mm(zu, mo[...]), mm(zd, me[...])
        fy1u[i] = yu
        fy1d[i] = yd
        fz1u[i] = zu
        fz1d[i] = zd
        diag = fx1[i] + fx1[i + 1] + yu + yd + zu + zd
        d1[i] = jnp.where(own1, diag, 0.0)

    each(4, body)
    parts1 = (lambda x: d1[x], lambda x: fx1[x + 1], lambda x: fy1u[x], lambda x: fz1u[x])
    pack_box(parts1, pkc, xyc, zpc, xzc, yzc)
    c_start, c_wait = box_exchange(pkc, xyc, zpc, xzc, yzc, rxc, ryc, rzc, rec, s1c, r1c)
    c_start((1,2))

    def pack2(planes):
        out = zero8
        for x in range(2):
            for t in range(2):
                g = 2 * x + t
                v = roll(planes[x][8 * t : 8 * t + 8], (32 * g - 48) % 128)
                out = jnp.where((lane8 >= 32 * g) & (lane8 < 32 * g + 32), v, out)
        return out

    xu, yu, zu, dg = [], [], [], []
    for i in range(2):
        t0[0:32, :] = fx1[2 * i]
        t0[32:64, :] = fx1[2 * i + 2]
        t0[64:96, :] = fz1u[2 * i] + fz1u[2 * i + 1]
        t0[96:128, :] = fz1d[2 * i] + fz1d[2 * i + 1]
        t0[128:160, :] = fy1u[2 * i] + fy1u[2 * i + 1]
        t0[160:192, :] = fy1d[2 * i] + fy1d[2 * i + 1]
        xd_, xu_ = mm(pair_rows(t0, 0, 16), mb[...]), mm(pair_rows(t0, 32, 16), mb[...])
        zu_, zd_ = mm(pair_rows(t0, 64, 16), mo[...]), mm(pair_rows(t0, 96, 16), me[...])
        yu_, yd_ = mm(rows_of(t0, 128, 16, 1), mb[...]), mm(rows_of(t0, 160, 16, 0), mb[...])
        xu.append(xu_)
        yu.append(yu_)
        zu.append(zu_)
        dg.append(xu_ + xd_ + yu_ + yd_ + zu_ + zd_)
    for a, planes in enumerate((dg, xu, yu, zu)):
        cc[1, gx, a] = pack2(planes)

    def gather(sx, rx, sn, rn):
        def xcopy(d):
            return pltpu.make_async_remote_copy(
                src_ref=cc.at[1, gx], dst_ref=cc.at[1, gx], send_sem=sx.at[d - 1], recv_sem=rx.at[d - 1],
                device_id={"gx": lax.rem(gx + d, nx)}, device_id_type=MESH,
            )

        def ncopy(d):
            src = [cc.at[1], cc.at[1], pz.at[1], pz.at[0]][d - 2]
            dst = [cc.at[0], cc.at[2], zc.at[0], zc.at[1]][d - 2]
            return pltpu.make_async_remote_copy(
                src_ref=src, dst_ref=dst, send_sem=sn.at[d - 2], recv_sem=rn.at[d - 2],
                device_id=near[d][0], device_id_type=MESH,
            )

        def xstart():
            for d in range(1, 4):
                xcopy(d).start()

        def xwait():
            for d in range(1, 4):
                pltpu.make_async_remote_copy(
                    src_ref=cc.at[1, gx], dst_ref=cc.at[1, lax.rem(gx + 4 - d, nx)],
                    send_sem=sx.at[d - 1], recv_sem=rx.at[d - 1],
                    device_id={"gx": lax.rem(gx + d, nx)}, device_id_type=MESH,
                ).wait()

        def nstart(ds):
            for d in ds:
                @pl.when(near[d][1])
                def _(d=d):
                    ncopy(d).start()

        def nwait(ds):
            for d in ds:
                @pl.when(near[d][1])
                def _(d=d):
                    ncopy(d).wait_send()

                @pl.when(near[d][2])
                def _(d=d):
                    ncopy(d).wait_recv()

        return (
            xstart, xwait,
            lambda: nstart((2, 3)), lambda: nwait((2, 3)),
            lambda: nstart((4, 5)), lambda: nwait((4, 5)),
        )

    cg = gather(csx, crx, csn, crn)

    inner0(u0.at[0], False)
    wait()
    c_start((3,))
    cg[0]()
    outer0(u0.at[0], yr0.at[0], zr0.at[0], u0.at[1], ys0.at[1], zs0.at[1], False)
    start, wait = round0(1)
    start()
    inner0(u0.at[1], True)
    wait()

    cg[1]()
    cg[2]()
    held = heldz(zr0.at[1])
    for i in range(4):
        total = None
        for j in range(2):
            x = 2 * i + j
            r = part[x] + across0(u0.at[1], yr0.at[1], held, x)
            total = r if total is None else total + r
        t1[i, 0] = total
        f1[i] = mm(t1[i, 0, pl.ds(0, 32, stride=2), :] + t1[i, 0, pl.ds(1, 32, stride=2), :], mb[...])

    pack_box([lambda x: f1[x]], pkf, xyf, zpf, xzf, yzf)
    f_start, f_wait = box_exchange(pkf, xyf, zpf, xzf, yzf, rxf, ryf, rzf, ref_, s1f, r1f)
    f_start()
    c_wait()
    cg[3]()
    low16 = lane8 % 32 < 16

    def body(y):
        for b in range(4):
            for j in range(2):
                v, w = cc[y, b, 2 * j], cc[y, b, 2 * j + 1]
                pz[0, y, b, j] = jnp.where(low16, v, roll(w, 16))
                pz[1, y, b, j] = jnp.where(low16, roll(w, 112), v)

    each(3, body)
    cg[4]()
    for a, get in enumerate(parts1):
        def put(p, out, a=a):
            ce1[a, p, 8:56, :] = out
            if a == 0:
                ok = out > 0.0
                w1[p] = jnp.where(ok, W / jnp.where(ok, out, 1.0), 0.0)

        unpack_box(get, rxc, ryc, rzc, rec, a, put)

    def zero_rows(ref, n, rows):
        def body(p):
            ref[p, 0:8, :] = zero8
            ref[p, 8 + rows : 16 + rows, :] = zero8

        each(n, body)

    zero_rows(ce1.at[2], 12, 48)
    for b in range(2):
        zero_rows(u1.at[b], 12, 48)
    f_wait()

    def put(p, out):
        f1e[p] = out
        u1[0, p, 8:56, :] = w1[p] * out

    unpack_box(lambda x: f1[x], rxf, ryf, rzf, ref_, 0, put)

    def beside1(buf, p, r0, n):
        c = buf[p, r0 : r0 + n, :]
        s = ce1[1, p, r0 : r0 + n, :] * buf[p + 1, r0 : r0 + n, :]
        s = s + ce1[1, p - 1, r0 : r0 + n, :] * buf[p - 1, r0 : r0 + n, :]
        s = s + ce1[2, p, r0 : r0 + n, :] * buf[p, r0 + 1 : r0 + 1 + n, :]
        s = s + ce1[2, p, r0 - 1 : r0 - 1 + n, :] * buf[p, r0 - 1 : r0 - 1 + n, :]
        z = ce1[3, p, r0 : r0 + n, :]
        return c, s + z * roll(c, 127) + roll(z * c, 1)

    def sweep1(src, dst, first, count):
        def body(i):
            p = i + first
            c, s = beside1(u1.at[src], p, 8, 48)
            u1[dst, p, 8:56, :] = c * THIRD + w1[p] * (f1e[p] + s)

        each(count, body)

    sweep1(0, 1, 1, 10)

    src2 = []
    for i in range(2):
        total = None
        for j in range(2):
            x = 2 * i + j
            c, s = beside1(u1.at[1], x + 4, 16, 32)
            r = f1[x] - d1[x] * c + s
            total = r if total is None else total + r
        t0[32 * i : 32 * i + 32, :] = jnp.where(own1, total, 0.0)
        src2.append(mm(pair_rows(t0, 32 * i, 16), mb[...]))
    gg[1, 1, gx] = pack2(src2)

    def fcopy(d, sy, sz):
        return pltpu.make_async_remote_copy(
            src_ref=gg.at[1, 1, gx], dst_ref=gg.at[1 - sz, 1 - sy, gx],
            send_sem=gs.at[d, sy + 1, sz + 1], recv_sem=gr.at[d, sy + 1, sz + 1],
            device_id=at(lax.rem(gx + d, nx), sy, sz), device_id_type=MESH,
        )

    def fback(d, sy, sz):
        return pltpu.make_async_remote_copy(
            src_ref=gg.at[1, 1, gx], dst_ref=gg.at[1 - sz, 1 - sy, lax.rem(gx + 4 - d, nx)],
            send_sem=gs.at[d, sy + 1, sz + 1], recv_sem=gr.at[d, sy + 1, sz + 1],
            device_id=at(lax.rem(gx + d, nx), sy, sz), device_id_type=MESH,
        )

    order = sorted([(sy, sz) for sy in steps for sz in steps], key=lambda o: -abs(o[0]) - abs(o[1]))

    def g_start():
        for sy, sz in order:
            @pl.when(yz_ok(sy, sz))
            def _(sy=sy, sz=sz):
                for d in (2, 1, 3, 0):
                    if (d, sy, sz) != (0, 0, 0):
                        fcopy(d, sy, sz).start()

    def g_wait():
        for sy, sz in order:
            @pl.when(yz_ok(sy, sz))
            def _(sy=sy, sz=sz):
                for d in range(4):
                    if (d, sy, sz) != (0, 0, 0):
                        fcopy(d, sy, sz).wait_send()

            @pl.when(yz_ok(-sy, -sz))
            def _(sy=sy, sz=sz):
                for d in range(4):
                    if (d, sy, sz) != (0, 0, 0):
                        fback(d, sy, sz).wait_recv()

    g_start()
    cg[5]()

    def spread2(get, put, shift, reach):
        def body(b):
            for y in range(3):
                v = [get(z, y, b) for z in range(3)]
                for x in range(2):
                    for t in range(2):
                        g = 2 * x + t
                        left = roll(v[0], (16 - 32 * g + shift) % 128)
                        mid = roll(v[1], (48 - 32 * g) % 128)
                        right = roll(v[2], (80 - 32 * g - shift) % 128)
                        out = jnp.where(lane8 < 48, left, jnp.where(lane8 < 80, mid, right))
                        out = jnp.where((lane8 >= 48 - reach) & (lane8 < 80 + reach), out, 0.0)
                        put(2 * b + x, 16 * y + 8 * t, out)

        each(4, body)

    def put_d(p, r, v):
        d2[p, r : r + 8, :] = v
        ok = v > 0.0
        w2[p, r : r + 8, :] = jnp.where(ok, W / jnp.where(ok, v, 1.0), 0.0)

    def put_x(p, r, v):
        fx2[p + 1, r : r + 8, :] = v

    def put_y(p, r, v):
        fy2[p, 8 + r : 16 + r, :] = v

    def put_z(p, r, v):
        fz2[p, r : r + 8, :] = v

    def put_f(p, r, v):
        f2[p, r : r + 8, :] = v
        u2[0, p + 2, 8 + r : 16 + r, :] = w2[p, r : r + 8, :] * v

    for a, put in enumerate((put_d, put_x, put_y, put_z)):
        spread2(lambda z, y, b, a=a: cc[y, b, a] if z == 1 else zc[z // 2, y, b, a // 2], put, 16 * (a % 2), 16)
    fx2[0] = jnp.zeros((48, 128), F32)
    fx3[0] = jnp.zeros((24, 128), F32)

    zero_rows(fy2, 8, 48)
    zero_rows(fy3, 4, 24)
    for b in range(2):
        zero_rows(u2.at[b], 12, 48)
        zero_rows(u3.at[b], 6, 24)
        for p in (0, 1, 10, 11):
            u2[b, p, 8:56, :] = jnp.zeros((48, 128), F32)
        for p in (0, 5):
            u3[b, p, 8:32, :] = jnp.zeros((24, 128), F32)

    row48 = lax.broadcasted_iota(jnp.int32, (48, 128), 0)

    def body(p):
        a, b = 2 * p, 2 * p + 1
        t5[p, 0] = fx2[b + 1]
        t5[p, 1] = fz2[a] + fz2[b]
        ysum = fy2[a, 8:56, :] + fy2[b, 8:56, :]
        t5[p, 2] = ysum
        inner = fx2[a + 1]
        inner = inner + jnp.where(row48 % 2 == 0, ysum, 0.0)
        inner = inner + jnp.where(lane48 % 2 == 0, fz2[a] + fz2[b], 0.0)
        t5[p, 3] = d2[a] + d2[b] - 2.0 * inner
        pick = lambda q, off: t5[p, q, pl.ds(off, 24, stride=2), :]
        fx3[p + 1] = mm(pick(0, 0) + pick(0, 1), mb[...])
        fz3[p] = mm(pick(1, 0) + pick(1, 1), mo[...])
        fy3[p, 8:32, :] = mm(pick(2, 1), mb[...])
        diag = mm(pick(3, 0) + pick(3, 1), mb[...])
        ok = diag > 0.0
        w3[p] = jnp.where(ok, W / jnp.where(ok, diag, 1.0), 0.0)

    each(4, body)

    g_wait()
    spread2(lambda z, y, b: gg[z, y, b], put_f, 0, 32)

    def beside(buf, fxr, fyr, fzr, p, rows):
        c = buf[p + 1, 8 : 8 + rows, :]
        s = fxr[p + 1] * buf[p + 2, 8 : 8 + rows, :] + fxr[p] * buf[p, 8 : 8 + rows, :]
        s = s + fyr[p, 8 : 8 + rows, :] * buf[p + 1, 9 : 9 + rows, :]
        s = s + fyr[p, 7 : 7 + rows, :] * buf[p + 1, 7 : 7 + rows, :]
        z = fzr[p]
        return c, s + z * roll(c, 127) + roll(z * c, 1)

    def sweep2(src, dst):
        def body(p):
            c, s = beside(u2.at[src, pl.ds(1, 10)], fx2, fy2, fz2, p, 48)
            u2[dst, p + 2, 8:56, :] = c * THIRD + w2[p] * (f2[p] + s)

        each(8, body)

    def sweep3(src, dst):
        def body(p):
            c, s = beside(u3.at[src], fx3, fy3, fz3, p, 24)
            u3[dst, p + 1, 8:32, :] = c * THIRD + w3[p] * (f3[p] + s)

        each(4, body)

    sweep2(0, 1)

    def body(p):
        total = None
        for j in range(2):
            c, s = beside(u2.at[1, pl.ds(1, 10)], fx2, fy2, fz2, 2 * p + j, 48)
            r = f2[2 * p + j] - d2[2 * p + j] * c + s
            total = r if total is None else total + r
        t5[p, 0] = total
        src = mm(t5[p, 0, pl.ds(0, 24, stride=2), :] + t5[p, 0, pl.ds(1, 24, stride=2), :], mb[...])
        f3[p] = src
        u3[0, p + 1, 8:32, :] = w3[p] * src

    each(4, body)
    sweep3(0, 1)
    sweep3(1, 0)
    sweep3(0, 1)

    def body(p):
        e = mm(u3[1, p + 1, 8:32, :], mt[...])
        t5[p, 1, pl.ds(0, 24, stride=2), :] = e
        t5[p, 1, pl.ds(1, 24, stride=2), :] = e
        wide = t5[p, 1]
        for j in range(2):
            q = 2 * p + j
            u2[0, q + 2, 8:56, :] = u2[1, q + 2, 8:56, :] + jnp.where(d2[q] > 0.0, wide, 0.0)

    each(4, body)
    sweep2(0, 1)
    sweep2(1, 0)

    def body(q):
        e = mm(u2[0, 2 * gx + q, 20:44, :], mt[...])
        t2[q, pl.ds(0, 24, stride=2), :] = e
        t2[q, pl.ds(1, 24, stride=2), :] = e

    each(6, body)

    def body(i):
        p = i + 1
        u1[0, p, 8:56, :] = u1[1, p, 8:56, :] + jnp.where(w1[p] > 0.0, t2[p // 2], 0.0)

    each(10, body)
    sweep1(0, 1, 2, 8)
    sweep1(1, 0, 3, 6)

    def body(q):
        c = u1[0, q + 3, 12:52, :]
        e = mm(c, mt[...])
        t3[q, pl.ds(0, 40, stride=2), :] = e
        t3[q, pl.ds(1, 40, stride=2), :] = e
        t4[q, pl.ds(0, 40, stride=2), :] = c
        t4[q, pl.ds(1, 40, stride=2), :] = c

    each(6, body)

    y_in(u0.at[1], yr0.at[1], 8, 64)

    def body(p):
        u0[0, p, :, :] = u0[1, p, :, :] + t3[(p + 1) // 2]

    each(10, body)

    held = heldz(zr0.at[1])
    extra = zero8
    for q in range(4):
        for t in range(8):
            v = t4[q + 1, 8 + 8 * t : 16 + 8 * t, :]
            k = 2 * (16 * q + t)
            up, down = roll(v, (k - 31) % 128), roll(v, (k - 97) % 128)
            extra = jnp.where(lane8 == k, up, jnp.where(lane8 == (k + 127) % 128, down, extra))
            extra = jnp.where(lane8 == k + 16, roll(up, 16), jnp.where(lane8 == k + 15, roll(down, 16), extra))
    held = held + extra
    acc = zero8
    for x in range(8):
        c, s = within0(u0.at[0], x, True)
        new = c * THIRD + w0[x] * (f0[x] + s + zface0(x, held))
        keepu(u0.at[2], ys0.at[2], x, new)
        acc = packz(acc, new, x)
    zs0[2, 0] = acc
    zs0[2, 1] = acc
    start, wait = round0(2)
    start()
    inner0(u0.at[2], False)
    wait()
    outer0(u0.at[2], yr0.at[2], zr0.at[2], u0.at[1], ys0.at[1], zs0.at[1], True)

    start, wait = round0(1)
    start()
    inner0(u0.at[1], True)
    wait()
    held = heldz(zr0.at[1])
    for x in range(8):
        ores[0, x] = part[x] + across0(u0.at[1], yr0.at[1], held, x)


def flush(a, b, oa, ob, sem):
    copies = [pltpu.make_async_copy(a, oa, sem.at[0]), pltpu.make_async_copy(b, ob, sem.at[1])]
    for c in copies:
        c.start()
    for c in copies:
        c.wait()


def on_device(phase, density, rhs):
    V = lambda *s: pltpu.VMEM(s, F32)
    M = pltpu.VMEM((384, 128), BF16)
    D = lambda *s: pltpu.SemaphoreType.DMA(s)
    scratch = [
        pltpu.VMEM((8, 64, 128), jnp.int32), V(8, 64, 128), V(8, 64, 128), V(8, 64, 128), V(8, 64, 128), V(10, 80, 128), V(3, 10, 80, 128),
        V(9, 64, 128), V(8, 80, 128), V(8, 64, 128), V(8, 64, 128), V(8, 64, 128), V(8, 64, 128),
        V(2, 8, 128), V(2, 8, 128), V(2, 8, 128), V(2, 8, 128),
        V(3, 2, 8, 128), V(3, 2, 8, 128), V(3, 2, 8, 128), V(3, 2, 8, 128),
        V(2, 12, 64, 128), V(4, 32, 128), V(5, 32, 128), V(4, 32, 128), V(4, 32, 128), V(4, 32, 128), V(4, 32, 128),
        V(4, 32, 128), V(12, 48, 128), V(4, 12, 64, 128),
        V(4, 2, 32, 128), V(2, 4, 8, 128), V(2, 4, 8, 128), V(2, 2, 8, 128), V(2, 2, 8, 128),
        V(2, 4, 2, 32, 128), V(3, 2, 4, 8, 128), V(3, 2, 4, 8, 128), V(3, 2, 2, 8, 128),
        V(1, 2, 32, 128), V(2, 1, 8, 128), V(2, 1, 8, 128), V(2, 1, 8, 128), V(2, 2, 8, 128),
        V(2, 1, 2, 32, 128), V(3, 2, 1, 8, 128), V(3, 2, 1, 8, 128), V(3, 2, 2, 8, 128),
        M, M, M, M, V(256, 128), V(4, 2, 64, 128), V(6, 48, 128), V(6, 80, 128), V(6, 80, 128), V(4, 4, 48, 128),
        V(12, 48, 128),
        V(3, 4, 4, 8, 128), V(2, 3, 4, 2, 8, 128), V(2, 3, 4, 2, 8, 128), V(3, 3, 4, 8, 128),
        V(8, 48, 128), V(2, 12, 64, 128), V(9, 48, 128), V(8, 64, 128), V(8, 48, 128), V(8, 48, 128), V(8, 48, 128),
        V(4, 24, 128), V(2, 6, 40, 128), V(5, 24, 128), V(4, 40, 128), V(4, 24, 128), V(4, 24, 128),
        D(3), D(6), D(6), D(3, 6), D(3, 6), D(3, 3, 3), D(3, 3, 3), D(3, 3, 3), D(3, 3, 3),
        D(3), D(3), D(4), D(4), D(4, 3, 3), D(4, 3, 3),
    ]
    near = pl.BlockSpec(memory_space=pltpu.VMEM)
    pair = pl.pallas_call(
        kernel,
        out_shape=(pltpu.VMEM(rhs.shape, F32),) * 2,
        in_specs=[pl.BlockSpec(memory_space=pl.ANY)] * 3,
        out_specs=(near,) * 2,
        scratch_shapes=scratch,
        compiler_params=pltpu.CompilerParams(collective_id=0, has_side_effects=True),
        name="vcycle",
    )(phase, density, rhs)
    pair = [pltpu.with_memory_space_constraint(v, pltpu.VMEM) for v in pair]
    return pl.pallas_call(
        flush,
        out_shape=(jax.ShapeDtypeStruct(rhs.shape, F32),) * 2,
        in_specs=[near] * 2,
        out_specs=(pl.BlockSpec(memory_space=pl.ANY),) * 2,
        scratch_shapes=[D(2)],
        name="flush",
    )(*pair)


def solution(mesh):
    in_specs = (P("gx", "gy", "gz"), P("gx", "gy", "gz"), P(None, "gx", "gy", "gz"))
    out_specs = (P(None, "gx", "gy", "gz"), P(None, "gx", "gy", "gz"))
    return jax.shard_map(on_device, mesh=mesh, in_specs=in_specs, out_specs=out_specs, check_vma=False)
```

```python
import functools

import jax
import jax.numpy as jnp
from jax import lax
from jax.experimental import pallas as pl
from jax.experimental.pallas import tpu as pltpu
from jax.sharding import PartitionSpec as P

MESH = pl.DeviceIdType.MESH
F32 = jnp.float32
W = 2.0 / 3.0
THIRD = 1.0 / 3.0
BF16 = jnp.bfloat16


def lanes(shape):
    return lax.broadcasted_iota(jnp.int32, shape, len(shape) - 1)


def roll(v, shift):
    return pltpu.roll(v, shift, 1)


def loop(count, body, init=0):
    return lax.fori_loop(0, count, body, init, unroll=True)


def each(count, body):
    def step(i, carry):
        body(i)
        return carry

    lax.fori_loop(0, count, step, 0, unroll=True)


def maps():
    row = lax.broadcasted_iota(jnp.int32, (128, 128), 0)
    col = lax.broadcasted_iota(jnp.int32, (128, 128), 1)
    hit = col == 32 + row // 2
    both = jnp.where(hit, 1.0, 0.0)
    odd = jnp.where(hit & (row % 2 == 1), 1.0, 0.0)
    even = jnp.where(hit & (row % 2 == 0), 1.0, 0.0)
    back = jnp.where(row == 32 + col // 2, 1.0, 0.0)
    return [jnp.concatenate([m.astype(BF16)] * 3, axis=0) for m in (both, odd, even, back)]


def mm(a, b):
    hi = a.astype(BF16)
    rest = a - hi.astype(F32)
    mid = rest.astype(BF16)
    low = (rest - mid.astype(F32)).astype(BF16)
    return lax.dot(jnp.concatenate([hi, mid, low], axis=1), b, preferred_element_type=F32)


def kernel(
    ph_h, de_h, rh_h, osol, ores,
    ph, de, f0, part, fze, rp, u0, fx, fy, fzu, fzd, w0, d0,
    rys, ryr, rzs, rzr, ys0, yr0, zs0, zr0,
    u1, f1, fx1, fy1u, fy1d, fz1u, fz1d, d1, w1, ce1,
    pkc, xyc, zpc, xzc, yzc, rxc, ryc, rzc, rec, pkf, xyf, zpf, xzf, yzf, rxf, ryf, rzf, ref_,
    mb, mo, me, mt, t0, t1, t2, t3, t4, t5, f1e,
    cc, pz, zc, gg,
    f2, u2, fx2, fy2, fz2, w2, d2,
    f3, u3, fx3, fy3, fz3, w3,
    in_sem, rss, rrs, s0s, r0s, s1c, r1c, s1f, r1f, csx, crx, csn, crn, gs, gr,
):
    gx, gy, gz = lax.axis_index("gx"), lax.axis_index("gy"), lax.axis_index("gz")
    nx, ny, nz = lax.axis_size("gx"), lax.axis_size("gy"), lax.axis_size("gz")
    near = [
        ({"gx": gx + 1}, gx < nx - 1, gx > 0),
        ({"gx": gx - 1}, gx > 0, gx < nx - 1),
        ({"gy": gy + 1}, gy < ny - 1, gy > 0),
        ({"gy": gy - 1}, gy > 0, gy < ny - 1),
        ({"gz": gz + 1}, gz < nz - 1, gz > 0),
        ({"gz": gz - 1}, gz > 0, gz < nz - 1),
    ]

    loads = [
        pltpu.make_async_copy(ph_h, ph, in_sem.at[0]),
        pltpu.make_async_copy(de_h, de, in_sem.at[1]),
        pltpu.make_async_copy(rh_h.at[0], f0, in_sem.at[2]),
    ]
    for c in loads:
        c.start()

    edge = (gx == 0) | (gx == nx - 1) | (gy == 0) | (gy == ny - 1) | (gz == 0) | (gz == nz - 1)

    @pl.when(edge)
    def _():
        for ref in (ryc, rzc, rec):
            ref[...] = jnp.zeros(ref.shape, F32)

    barrier = pltpu.get_barrier_semaphore()
    arrivals = 0
    for where, ok, back in near:
        arrivals = arrivals + jnp.where(back, 1, 0)

        @pl.when(ok)
        def _(where=where):
            pl.semaphore_signal(barrier, inc=1, device_id=where, device_id_type=MESH)

    @pl.when(edge)
    def _():
        for b in range(3):
            for x in (0, 9):
                u0[b, x, 8:72, :] = jnp.zeros((64, 128), F32)
        for ref in (yr0, zr0, gg, zc, rxc, rxf, ryf, rzf, ref_):
            ref[...] = jnp.zeros(ref.shape, F32)
        for y in (0, 2):
            cc[y] = jnp.zeros(cc.shape[1:], F32)

    def inside(at, step, count):
        return (at >= 0) if step == 0 else (at < count - 1) if step > 0 else (at > 0)

    def yz_ok(sy, sz):
        return inside(gy, sy, ny) & inside(gz, sz, nz)

    def at(sx, sy, sz):
        return {"gx": sx, "gy": gy + sy, "gz": gz + sz}

    steps = (-1, 0, 1)

    def faces(buf, n, rows, ys, yr, zs, zr, ss, rs):
        body = pl.ds(8, rows)
        pairs = [
            (buf.at[n, body], buf.at[0, body]),
            (buf.at[1, body], buf.at[n + 1, body]),
            (ys.at[1], yr.at[0]),
            (ys.at[0], yr.at[1]),
            (zs.at[1], zr.at[0]),
            (zs.at[0], zr.at[1]),
        ]

        def copy(d):
            src, dst = pairs[d]
            return pltpu.make_async_remote_copy(
                src_ref=src, dst_ref=dst, send_sem=ss.at[d], recv_sem=rs.at[d],
                device_id=near[d][0], device_id_type=MESH,
            )

        def start():
            for d in range(6):
                @pl.when(near[d][1])
                def _(d=d):
                    copy(d).start()

        def wait():
            for d in range(6):
                @pl.when(near[d][1])
                def _(d=d):
                    copy(d).wait_send()

                @pl.when(near[d][2])
                def _(d=d):
                    copy(d).wait_recv()

        return start, wait

    lane8 = lanes((8, 128))
    lane64 = lanes((64, 128))
    lane32 = lanes((32, 128))

    zero8 = jnp.zeros((8, 128), F32)

    def pack0(carry, plane, x):
        lo, hi = carry
        for t in range(8):
            v = plane[8 * t : 8 * t + 8]
            k = x * 8 + t
            here = lane8 == k
            lo = jnp.where(here, roll(v, k), lo)
            hi = jnp.where(here, roll(v, k + 1), hi)
        return lo, hi

    def z_beside0(plane, x, lo, hi):
        right = jnp.concatenate([roll(hi, 127 - (x * 8 + t)) for t in range(8)], axis=0)
        left = jnp.concatenate([roll(lo, lax.rem(128 - (x * 8 + t), 128)) for t in range(8)], axis=0)
        return (
            jnp.where(lane64 == 127, right, roll(plane, 127)),
            jnp.where(lane64 == 0, left, roll(plane, 1)),
        )

    def keep0(buf, ys, x, plane):
        buf[x + 1, 8:72, :] = plane
        ys[0, pl.ds(x, 1), :] = plane[0:1]
        ys[1, pl.ds(x, 1), :] = plane[63:64]

    def y_in(buf, yr, n, rows):
        def body(x):
            buf[x + 1, 7:8, :] = yr[0, pl.ds(x, 1), :]
            buf[x + 1, 8 + rows : 9 + rows, :] = yr[1, pl.ds(x, 1), :]

        each(n, body)

    def mod(v):
        return v % 128 if isinstance(v, int) else lax.rem(v, 128)

    def packz(acc, plane, x):
        for t in range(8):
            v = plane[8 * t : 8 * t + 8]
            k = 2 * (x * 8 + t)
            acc = jnp.where(lane8 == k, roll(v, mod(k + 1)), acc)
            acc = jnp.where(lane8 == mod(k + 127), roll(v, mod(k + 127)), acc)
        return acc

    def heldz(zr):
        return jnp.where(lane8 % 2 == 0, zr[0], zr[1])

    def keepu(buf, ys, x, plane):
        keep0(buf, ys, x, plane)
        buf[x + 1, 7:8, :] = jnp.zeros((1, 128), F32)
        buf[x + 1, 72:73, :] = jnp.zeros((1, 128), F32)

    def within0(buf, x, whole):
        c = buf[x + 1, 8:72, :]
        s = fy[x, 8:72, :] * buf[x + 1, 9:73, :] + fy[x, 7:71, :] * buf[x + 1, 7:71, :]
        s = s + fzu[x] * jnp.where(lane64 == 127, 0.0, roll(c, 127))
        s = s + fzd[x] * jnp.where(lane64 == 0, 0.0, roll(c, 1))
        if whole or x < 7:
            s = s + fx[x + 1] * buf[x + 2, 8:72, :]
        if whole or x > 0:
            s = s + fx[x] * buf[x, 8:72, :]
        return c, s

    def zface0(x, held):
        return fze[x] * jnp.concatenate([roll(held, mod(256 - 2 * (x * 8 + t))) for t in range(8)], axis=0)

    def across0(buf, yr, held, x):
        h = zface0(x, held)
        if x == 0:
            h = h + fx[0] * buf[0, 8:72, :]
        if x == 7:
            h = h + fx[8] * buf[9, 8:72, :]
        top = fy[x, 7:8, :] * yr[0, x : x + 1, :]
        end = fy[x, 71:72, :] * yr[1, x : x + 1, :]
        return jnp.concatenate(
            [h[0:8] + jnp.where(row8 == 0, top, 0.0), h[8:56], h[56:64] + jnp.where(row8 == 7, end, 0.0)], axis=0
        )

    def inner0(buf, resid):
        for x in range(8):
            c, s = within0(buf, x, False)
            part[x] = f0[x] - d0[x] * c + s if resid else c * THIRD + w0[x] * (f0[x] + s)

    def outer0(src, yr, zr, dst, ys, zs, out):
        held = heldz(zr)
        acc = zero8
        for x in range(8):
            new = part[x] + w0[x] * across0(src, yr, held, x)
            keepu(dst, ys, x, new)
            if out:
                osol[0, x] = d0[x] * new
            acc = packz(acc, new, x)
        zs[0] = acc
        zs[1] = acc

    row8 = lax.broadcasted_iota(jnp.int32, (8, 128), 0)

    for c in loads[:2]:
        c.wait()

    def body(x, carry):
        plane = jnp.where(ph[x] == 1, 1000.0, 1.0).astype(F32) * de[x]
        keep0(rp, rys, x, plane)
        return pack0(carry, plane, x)

    packed = loop(8, body, (zero8, zero8))
    rzs[0] = packed[0]
    rzs[1] = packed[1]

    pl.semaphore_wait(barrier, arrivals)
    start, wait = faces(rp, 8, 64, rys, ryr, rzs, rzr, rss, rrs)
    start()
    both, odd, even, back = maps()
    mb[...] = both
    mo[...] = odd
    me[...] = even
    mt[...] = back
    loads[2].wait()
    wait()

    @pl.when(gx == 0)
    def _():
        rp[0, 8:72, :] = rp[1, 8:72, :]

    @pl.when(gx == nx - 1)
    def _():
        rp[9, 8:72, :] = rp[8, 8:72, :]

    for ok, got, own, s in ((gy == 0, ryr, rys, 0), (gy == ny - 1, ryr, rys, 1), (gz == 0, rzr, rzs, 0), (gz == nz - 1, rzr, rzs, 1)):
        @pl.when(ok)
        def _(got=got, own=own, s=s):
            got[s] = own[s]

    y_in(rp, ryr, 8, 64)
    lo, hi = rzr[0], rzr[1]
    fx[0] = 2.0 / (rp[0, 8:72, :] + rp[1, 8:72, :])

    def body(x, carry):
        c = rp[x + 1, 8:72, :]
        up, down = z_beside0(c, x, lo, hi)
        xu = 2.0 / (c + rp[x + 2, 8:72, :])
        yu = 2.0 / (c + rp[x + 1, 9:73, :])
        zu = 2.0 / (c + up)
        zd = 2.0 / (c + down)
        fx[x + 1] = xu
        fy[x, 8:72, :] = yu
        fy[x, 7:8, :] = 2.0 / (c[0:1] + rp[x + 1, 7:8, :])
        fzu[x] = zu
        fzd[x] = zd
        diag = xu + fx[x] + yu + fy[x, 7:71, :] + zu + zd
        d0[x] = diag
        w = W / diag
        w0[x] = w
        first = w * f0[x]
        fze[x] = jnp.where(lane64 == 127, zu, jnp.where(lane64 == 0, zd, 0.0))
        keepu(u0.at[0], ys0.at[0], x, first)
        return packz(carry, first, x)

    packed = loop(8, body, zero8)
    zs0[0, 0] = packed
    zs0[0, 1] = packed

    def round0(b):
        return faces(u0.at[b], 8, 64, ys0.at[b], yr0.at[b], zs0.at[b], zr0.at[b], s0s.at[b], r0s.at[b])

    box = [(a, b, c) for a in steps for b in steps for c in steps if (a, b, c) != (0, 0, 0)]

    def box_exchange(pk, xy, zp, xz, yz, rx, ry, rz, re, ss, rs):
        def copy(a, b, c):
            if b and c:
                src, dst = yz.at[(b + 1) // 2, (c + 1) // 2], re.at[1 - a, (1 - b) // 2, (1 - c) // 2]
            elif a and c:
                src, dst = xz.at[(c + 1) // 2], rz.at[1 - a, (1 - c) // 2, pl.ds(0, xz.shape[1])]
            elif c:
                src, dst = zp.at[(c + 1) // 2], rz.at[1 - a, (1 - c) // 2]
            elif b:
                src, dst = xy.at[(b + 1) // 2], ry.at[1 - a, (1 - b) // 2]
            else:
                src, dst = pk, rx.at[(1 - a) // 2]
            return pltpu.make_async_remote_copy(
                src_ref=src, dst_ref=dst, send_sem=ss.at[a + 1, b + 1, c + 1], recv_sem=rs.at[a + 1, b + 1, c + 1],
                device_id=at(gx + a, b, c), device_id_type=MESH,
            )

        def start(far=(1, 2, 3)):
            for n in sorted(far, reverse=True):
                for a, b, c in box:
                    if abs(a) + abs(b) + abs(c) == n:
                        @pl.when(inside(gx, a, nx) & yz_ok(b, c))
                        def _(a=a, b=b, c=c):
                            copy(a, b, c).start()

        def wait():
            for a, b, c in box:
                @pl.when(inside(gx, a, nx) & yz_ok(b, c))
                def _(a=a, b=b, c=c):
                    copy(a, b, c).wait_send()

                @pl.when(inside(gx, -a, nx) & yz_ok(-b, -c))
                def _(a=a, b=b, c=c):
                    copy(a, b, c).wait_recv()

        return start, wait

    low4 = lane8 % 8 < 4

    def half(v):
        return pltpu.roll(v, 4, 0)

    def pack_box(gets, pk, xy, zp, xz, yz):
        edge = {(b, c): zero8 for b in range(2) for c in range(2)}
        for a, get in enumerate(gets):
            planes = [get(x) for x in range(4)]
            pairs = [jnp.where(own1, planes[2 * i], roll(planes[2 * i + 1], 64)) for i in range(2)]
            for i in range(2):
                pk[a, i] = pairs[i]
            xy[0, a] = jnp.where(row8 < 4, pairs[0][0:8], half(pairs[1][0:8]))
            xy[1, a] = jnp.where(row8 >= 4, pairs[0][24:32], half(pairs[1][24:32]))
            face = [zero8, zero8]
            for x in range(4):
                for t in range(4):
                    v = planes[x][8 * t : 8 * t + 8]
                    k = x * 4 + t
                    for c, first in ((0, 96), (1, 40)):
                        face[c] = jnp.where(lane8 // 8 == k, roll(v, (8 * k + first) % 128), face[c])
                        if t in (0, 3):
                            b = t // 3
                            edge[b, c] = jnp.where(lane8 // 8 == 4 * a + x, roll(v, (32 * a + 8 * x + first) % 128), edge[b, c])
            zp[0, a] = face[0]
            zp[1, a] = face[1]
            if a % 2 == 0:
                even = face
            if a % 2 == 1:
                xz[0, a // 2] = jnp.where(low4, even[0], roll(face[0], 4))
                xz[1, a // 2] = jnp.where(low4, roll(face[1], 124), even[1])
            elif a == len(gets) - 1:
                xz[0, a // 2] = face[0]
                xz[1, a // 2] = face[1]
        for b in range(2):
            for c in range(2):
                yz[b, c] = edge[b, c]

    def unpack_box(own, rx, ry, rz, re, a, put):
        def side(dx, x, c, first):
            def corner(b):
                return roll(re[dx, b, c], (first - 32 * a - 8 * x) % 128)

            shift, i = (0, a) if dx == 1 else ((4 - 8 * c) * (a % 2), a // 2)
            mid = [roll(rz[dx, c, i], (first + shift - 8 * (4 * x + t)) % 128) for t in range(4)]
            return jnp.concatenate([corner(0)] + mid + [corner(1)], axis=0)

        for dx in range(3):
            for x in range(4):
                i = x // 2
                turn = (lambda v: roll(v, 64)) if x % 2 else (lambda v: v)
                flip = half if i else (lambda v: v)
                mid = own(x) if dx == 1 else turn(rx[dx // 2, a, i])
                centre = jnp.concatenate([turn(flip(ry[dx, 0, a])), mid, turn(flip(ry[dx, 1, a]))], axis=0)
                out = jnp.where((lane48 >= 96) & (lane48 < 100), side(dx, x, 1, 96), 0.0)
                out = jnp.where((lane48 >= 32) & (lane48 < 96), centre, out)
                out = jnp.where((lane48 >= 28) & (lane48 < 32), side(dx, x, 0, 24), out)
                put(4 * dx + x, out)

    lane48 = lanes((48, 128))
    start, wait = round0(0)
    start()

    own1 = (lane32 >= 32) & (lane32 < 96)

    def rows_of(ref, base, n, off):
        return ref[pl.ds(base + off, n, stride=2), :]

    def pair_rows(ref, base, n):
        return rows_of(ref, base, n, 0) + rows_of(ref, base, n, 1)

    for i in range(5):
        t0[0:64, :] = fx[2 * i]
        fx1[i] = mm(pair_rows(t0, 0, 32), mb[...])

    def body(i):
        yu = fy[2 * i, pl.ds(9, 32, stride=2), :] + fy[2 * i + 1, pl.ds(9, 32, stride=2), :]
        yd = fy[2 * i, pl.ds(7, 32, stride=2), :] + fy[2 * i + 1, pl.ds(7, 32, stride=2), :]
        t1[i, 0] = fzu[2 * i] + fzu[2 * i + 1]
        t1[i, 1] = fzd[2 * i] + fzd[2 * i + 1]
        zu = t1[i, 0, pl.ds(0, 32, stride=2), :] + t1[i, 0, pl.ds(1, 32, stride=2), :]
        zd = t1[i, 1, pl.ds(0, 32, stride=2), :] + t1[i, 1, pl.ds(1, 32, stride=2), :]
        yu, yd, zu, zd = mm(yu, mb[...]), mm(yd, mb[...]), mm(zu, mo[...]), mm(zd, me[...])
        fy1u[i] = yu
        fy1d[i] = yd
        fz1u[i] = zu
        fz1d[i] = zd
        diag = fx1[i] + fx1[i + 1] + yu + yd + zu + zd
        d1[i] = jnp.where(own1, diag, 0.0)

    each(4, body)
    parts1 = (lambda x: d1[x], lambda x: fx1[x + 1], lambda x: fy1u[x], lambda x: fz1u[x])
    pack_box(parts1, pkc, xyc, zpc, xzc, yzc)
    c_start, c_wait = box_exchange(pkc, xyc, zpc, xzc, yzc, rxc, ryc, rzc, rec, s1c, r1c)
    c_start((1,2))

    def pack2(planes):
        out = zero8
        for x in range(2):
            for t in range(2):
                g = 2 * x + t
                v = roll(planes[x][8 * t : 8 * t + 8], (32 * g - 48) % 128)
                out = jnp.where((lane8 >= 32 * g) & (lane8 < 32 * g + 32), v, out)
        return out

    xu, yu, zu, dg = [], [], [], []
    for i in range(2):
        t0[0:32, :] = fx1[2 * i]
        t0[32:64, :] = fx1[2 * i + 2]
        t0[64:96, :] = fz1u[2 * i] + fz1u[2 * i + 1]
        t0[96:128, :] = fz1d[2 * i] + fz1d[2 * i + 1]
        t0[128:160, :] = fy1u[2 * i] + fy1u[2 * i + 1]
        t0[160:192, :] = fy1d[2 * i] + fy1d[2 * i + 1]
        xd_, xu_ = mm(pair_rows(t0, 0, 16), mb[...]), mm(pair_rows(t0, 32, 16), mb[...])
        zu_, zd_ = mm(pair_rows(t0, 64, 16), mo[...]), mm(pair_rows(t0, 96, 16), me[...])
        yu_, yd_ = mm(rows_of(t0, 128, 16, 1), mb[...]), mm(rows_of(t0, 160, 16, 0), mb[...])
        xu.append(xu_)
        yu.append(yu_)
        zu.append(zu_)
        dg.append(xu_ + xd_ + yu_ + yd_ + zu_ + zd_)
    for a, planes in enumerate((dg, xu, yu, zu)):
        cc[1, gx, a] = pack2(planes)

    def gather(sx, rx, sn, rn):
        def xcopy(d):
            return pltpu.make_async_remote_copy(
                src_ref=cc.at[1, gx], dst_ref=cc.at[1, gx], send_sem=sx.at[d - 1], recv_sem=rx.at[d - 1],
                device_id={"gx": lax.rem(gx + d, nx)}, device_id_type=MESH,
            )

        def ncopy(d):
            src = [cc.at[1], cc.at[1], pz.at[1], pz.at[0]][d - 2]
            dst = [cc.at[0], cc.at[2], zc.at[0], zc.at[1]][d - 2]
            return pltpu.make_async_remote_copy(
                src_ref=src, dst_ref=dst, send_sem=sn.at[d - 2], recv_sem=rn.at[d - 2],
                device_id=near[d][0], device_id_type=MESH,
            )

        def xstart():
            for d in range(1, 4):
                xcopy(d).start()

        def xwait():
            for d in range(1, 4):
                pltpu.make_async_remote_copy(
                    src_ref=cc.at[1, gx], dst_ref=cc.at[1, lax.rem(gx + 4 - d, nx)],
                    send_sem=sx.at[d - 1], recv_sem=rx.at[d - 1],
                    device_id={"gx": lax.rem(gx + d, nx)}, device_id_type=MESH,
                ).wait()

        def nstart(ds):
            for d in ds:
                @pl.when(near[d][1])
                def _(d=d):
                    ncopy(d).start()

        def nwait(ds):
            for d in ds:
                @pl.when(near[d][1])
                def _(d=d):
                    ncopy(d).wait_send()

                @pl.when(near[d][2])
                def _(d=d):
                    ncopy(d).wait_recv()

        return (
            xstart, xwait,
            lambda: nstart((2, 3)), lambda: nwait((2, 3)),
            lambda: nstart((4, 5)), lambda: nwait((4, 5)),
        )

    cg = gather(csx, crx, csn, crn)

    inner0(u0.at[0], False)
    wait()
    c_start((3,))
    cg[0]()
    outer0(u0.at[0], yr0.at[0], zr0.at[0], u0.at[1], ys0.at[1], zs0.at[1], False)
    start, wait = round0(1)
    start()
    inner0(u0.at[1], True)
    wait()

    cg[1]()
    cg[2]()
    held = heldz(zr0.at[1])
    for i in range(4):
        total = None
        for j in range(2):
            x = 2 * i + j
            r = part[x] + across0(u0.at[1], yr0.at[1], held, x)
            total = r if total is None else total + r
        t1[i, 0] = total
        f1[i] = mm(t1[i, 0, pl.ds(0, 32, stride=2), :] + t1[i, 0, pl.ds(1, 32, stride=2), :], mb[...])

    pack_box([lambda x: f1[x]], pkf, xyf, zpf, xzf, yzf)
    f_start, f_wait = box_exchange(pkf, xyf, zpf, xzf, yzf, rxf, ryf, rzf, ref_, s1f, r1f)
    f_start()
    cg[3]()
    low16 = lane8 % 32 < 16

    def body(y):
        for b in range(4):
            for j in range(2):
                v, w = cc[y, b, 2 * j], cc[y, b, 2 * j + 1]
                pz[0, y, b, j] = jnp.where(low16, v, roll(w, 16))
                pz[1, y, b, j] = jnp.where(low16, roll(w, 112), v)

    each(3, body)
    cg[4]()
    c_wait()
    for a, get in enumerate(parts1):
        def put(p, out, a=a):
            ce1[a, p, 8:56, :] = out
            if a == 0:
                ok = out > 0.0
                w1[p] = jnp.where(ok, W / jnp.where(ok, out, 1.0), 0.0)

        unpack_box(get, rxc, ryc, rzc, rec, a, put)

    def zero_rows(ref, n, rows):
        def body(p):
            ref[p, 0:8, :] = zero8
            ref[p, 8 + rows : 16 + rows, :] = zero8

        each(n, body)

    zero_rows(ce1.at[2], 12, 48)
    for b in range(2):
        zero_rows(u1.at[b], 12, 48)
    f_wait()

    def put(p, out):
        f1e[p] = out
        u1[0, p, 8:56, :] = w1[p] * out

    unpack_box(lambda x: f1[x], rxf, ryf, rzf, ref_, 0, put)

    def beside1(buf, p, r0, n):
        c = buf[p, r0 : r0 + n, :]
        s = ce1[1, p, r0 : r0 + n, :] * buf[p + 1, r0 : r0 + n, :]
        s = s + ce1[1, p - 1, r0 : r0 + n, :] * buf[p - 1, r0 : r0 + n, :]
        s = s + ce1[2, p, r0 : r0 + n, :] * buf[p, r0 + 1 : r0 + 1 + n, :]
        s = s + ce1[2, p, r0 - 1 : r0 - 1 + n, :] * buf[p, r0 - 1 : r0 - 1 + n, :]
        z = ce1[3, p, r0 : r0 + n, :]
        return c, s + z * roll(c, 127) + roll(z * c, 1)

    def sweep1(src, dst, first, count):
        def body(i):
            p = i + first
            c, s = beside1(u1.at[src], p, 8, 48)
            u1[dst, p, 8:56, :] = c * THIRD + w1[p] * (f1e[p] + s)

        each(count, body)

    sweep1(0, 1, 1, 10)

    src2 = []
    for i in range(2):
        total = None
        for j in range(2):
            x = 2 * i + j
            c, s = beside1(u1.at[1], x + 4, 16, 32)
            r = f1[x] - d1[x] * c + s
            total = r if total is None else total + r
        t0[32 * i : 32 * i + 32, :] = jnp.where(own1, total, 0.0)
        src2.append(mm(pair_rows(t0, 32 * i, 16), mb[...]))
    gg[1, 1, gx] = pack2(src2)

    def fcopy(d, sy, sz):
        return pltpu.make_async_remote_copy(
            src_ref=gg.at[1, 1, gx], dst_ref=gg.at[1 - sz, 1 - sy, gx],
            send_sem=gs.at[d, sy + 1, sz + 1], recv_sem=gr.at[d, sy + 1, sz + 1],
            device_id=at(lax.rem(gx + d, nx), sy, sz), device_id_type=MESH,
        )

    def fback(d, sy, sz):
        return pltpu.make_async_remote_copy(
            src_ref=gg.at[1, 1, gx], dst_ref=gg.at[1 - sz, 1 - sy, lax.rem(gx + 4 - d, nx)],
            send_sem=gs.at[d, sy + 1, sz + 1], recv_sem=gr.at[d, sy + 1, sz + 1],
            device_id=at(lax.rem(gx + d, nx), sy, sz), device_id_type=MESH,
        )

    order = sorted([(sy, sz) for sy in steps for sz in steps], key=lambda o: -abs(o[0]) - abs(o[1]))

    def g_start():
        for sy, sz in order:
            @pl.when(yz_ok(sy, sz))
            def _(sy=sy, sz=sz):
                for d in (2, 1, 3, 0):
                    if (d, sy, sz) != (0, 0, 0):
                        fcopy(d, sy, sz).start()

    def g_wait():
        for sy, sz in order:
            @pl.when(yz_ok(sy, sz))
            def _(sy=sy, sz=sz):
                for d in range(4):
                    if (d, sy, sz) != (0, 0, 0):
                        fcopy(d, sy, sz).wait_send()

            @pl.when(yz_ok(-sy, -sz))
            def _(sy=sy, sz=sz):
                for d in range(4):
                    if (d, sy, sz) != (0, 0, 0):
                        fback(d, sy, sz).wait_recv()

    g_start()
    cg[5]()

    def spread2(get, put, shift, reach):
        def body(b):
            for y in range(3):
                v = [get(z, y, b) for z in range(3)]
                for x in range(2):
                    for t in range(2):
                        g = 2 * x + t
                        left = roll(v[0], (16 - 32 * g + shift) % 128)
                        mid = roll(v[1], (48 - 32 * g) % 128)
                        right = roll(v[2], (80 - 32 * g - shift) % 128)
                        out = jnp.where(lane8 < 48, left, jnp.where(lane8 < 80, mid, right))
                        out = jnp.where((lane8 >= 48 - reach) & (lane8 < 80 + reach), out, 0.0)
                        put(2 * b + x, 16 * y + 8 * t, out)

        each(4, body)

    def put_d(p, r, v):
        d2[p, r : r + 8, :] = v
        ok = v > 0.0
        w2[p, r : r + 8, :] = jnp.where(ok, W / jnp.where(ok, v, 1.0), 0.0)

    def put_x(p, r, v):
        fx2[p + 1, r : r + 8, :] = v

    def put_y(p, r, v):
        fy2[p, 8 + r : 16 + r, :] = v

    def put_z(p, r, v):
        fz2[p, r : r + 8, :] = v

    def put_f(p, r, v):
        f2[p, r : r + 8, :] = v
        u2[0, p + 2, 8 + r : 16 + r, :] = w2[p, r : r + 8, :] * v

    for a, put in enumerate((put_d, put_x, put_y, put_z)):
        spread2(lambda z, y, b, a=a: cc[y, b, a] if z == 1 else zc[z // 2, y, b, a // 2], put, 16 * (a % 2), 16)
    fx2[0] = jnp.zeros((48, 128), F32)
    fx3[0] = jnp.zeros((24, 128), F32)

    zero_rows(fy2, 8, 48)
    zero_rows(fy3, 4, 24)
    for b in range(2):
        zero_rows(u2.at[b], 12, 48)
        zero_rows(u3.at[b], 6, 24)
        for p in (0, 1, 10, 11):
            u2[b, p, 8:56, :] = jnp.zeros((48, 128), F32)
        for p in (0, 5):
            u3[b, p, 8:32, :] = jnp.zeros((24, 128), F32)

    row48 = lax.broadcasted_iota(jnp.int32, (48, 128), 0)

    def body(p):
        a, b = 2 * p, 2 * p + 1
        t5[p, 0] = fx2[b + 1]
        t5[p, 1] = fz2[a] + fz2[b]
        ysum = fy2[a, 8:56, :] + fy2[b, 8:56, :]
        t5[p, 2] = ysum
        inner = fx2[a + 1]
        inner = inner + jnp.where(row48 % 2 == 0, ysum, 0.0)
        inner = inner + jnp.where(lane48 % 2 == 0, fz2[a] + fz2[b], 0.0)
        t5[p, 3] = d2[a] + d2[b] - 2.0 * inner
        pick = lambda q, off: t5[p, q, pl.ds(off, 24, stride=2), :]
        fx3[p + 1] = mm(pick(0, 0) + pick(0, 1), mb[...])
        fz3[p] = mm(pick(1, 0) + pick(1, 1), mo[...])
        fy3[p, 8:32, :] = mm(pick(2, 1), mb[...])
        diag = mm(pick(3, 0) + pick(3, 1), mb[...])
        ok = diag > 0.0
        w3[p] = jnp.where(ok, W / jnp.where(ok, diag, 1.0), 0.0)

    each(4, body)

    g_wait()
    spread2(lambda z, y, b: gg[z, y, b], put_f, 0, 32)

    def beside(buf, fxr, fyr, fzr, p, rows, o=0):
        a, b = o + 8, o + 8 + rows
        c = buf[p + 1, a:b, :]
        s = fxr[p + 1, o : o + rows, :] * buf[p + 2, a:b, :] + fxr[p, o : o + rows, :] * buf[p, a:b, :]
        s = s + fyr[p, a:b, :] * buf[p + 1, a + 1 : b + 1, :]
        s = s + fyr[p, a - 1 : b - 1, :] * buf[p + 1, a - 1 : b - 1, :]
        z = fzr[p, o : o + rows, :]
        return c, s + z * roll(c, 127) + roll(z * c, 1)

    def sweep2(src, dst, o, rows):
        def body(p):
            c, s = beside(u2.at[src, pl.ds(1, 10)], fx2, fy2, fz2, p, rows, o)
            here = slice(o, o + rows)
            u2[dst, p + 2, o + 8 : o + 8 + rows, :] = c * THIRD + w2[p, here, :] * (f2[p, here, :] + s)

        each(8, body)

    def sweep3(src, dst):
        def body(p):
            c, s = beside(u3.at[src], fx3, fy3, fz3, p, 24)
            u3[dst, p + 1, 8:32, :] = c * THIRD + w3[p] * (f3[p] + s)

        each(4, body)

    sweep2(0, 1, 0, 48)

    def body(p):
        total = None
        for j in range(2):
            c, s = beside(u2.at[1, pl.ds(1, 10)], fx2, fy2, fz2, 2 * p + j, 48)
            r = f2[2 * p + j] - d2[2 * p + j] * c + s
            total = r if total is None else total + r
        t5[p, 0] = total
        src = mm(t5[p, 0, pl.ds(0, 24, stride=2), :] + t5[p, 0, pl.ds(1, 24, stride=2), :], mb[...])
        f3[p] = src
        u3[0, p + 1, 8:32, :] = w3[p] * src

    each(4, body)
    sweep3(0, 1)
    sweep3(1, 0)
    sweep3(0, 1)

    def body(p):
        e = mm(u3[1, p + 1, 8:32, :], mt[...])
        t5[p, 1, pl.ds(0, 24, stride=2), :] = e
        t5[p, 1, pl.ds(1, 24, stride=2), :] = e
        wide = t5[p, 1]
        for j in range(2):
            q = 2 * p + j
            u2[0, q + 2, 8:56, :] = u2[1, q + 2, 8:56, :] + jnp.where(d2[q] > 0.0, wide, 0.0)

    each(4, body)
    sweep2(0, 1, 8, 32)
    sweep2(1, 0, 8, 32)

    def body(q):
        e = mm(u2[0, 2 * gx + q, 20:44, :], mt[...])
        t2[q, pl.ds(0, 24, stride=2), :] = e
        t2[q, pl.ds(1, 24, stride=2), :] = e

    each(6, body)

    def body(i):
        p = i + 1
        u1[0, p, 8:56, :] = u1[1, p, 8:56, :] + jnp.where(w1[p] > 0.0, t2[p // 2], 0.0)

    each(10, body)
    sweep1(0, 1, 2, 8)
    sweep1(1, 0, 3, 6)

    def body(q):
        c = u1[0, q + 3, 12:52, :]
        e = mm(c, mt[...])
        t3[q, pl.ds(0, 40, stride=2), :] = e
        t3[q, pl.ds(1, 40, stride=2), :] = e
        t4[q, pl.ds(0, 40, stride=2), :] = c
        t4[q, pl.ds(1, 40, stride=2), :] = c

    each(6, body)

    y_in(u0.at[1], yr0.at[1], 8, 64)

    def body(p):
        u0[0, p, :, :] = u0[1, p, :, :] + t3[(p + 1) // 2]

    each(10, body)

    held = heldz(zr0.at[1])
    extra = zero8
    for q in range(4):
        for t in range(8):
            v = t4[q + 1, 8 + 8 * t : 16 + 8 * t, :]
            k = 2 * (16 * q + t)
            up, down = roll(v, (k - 31) % 128), roll(v, (k - 97) % 128)
            extra = jnp.where(lane8 == k, up, jnp.where(lane8 == (k + 127) % 128, down, extra))
            extra = jnp.where(lane8 == k + 16, roll(up, 16), jnp.where(lane8 == k + 15, roll(down, 16), extra))
    held = held + extra
    acc = zero8
    for x in range(8):
        c, s = within0(u0.at[0], x, True)
        new = c * THIRD + w0[x] * (f0[x] + s + zface0(x, held))
        keepu(u0.at[2], ys0.at[2], x, new)
        acc = packz(acc, new, x)
    zs0[2, 0] = acc
    zs0[2, 1] = acc
    start, wait = round0(2)
    start()
    inner0(u0.at[2], False)
    wait()
    outer0(u0.at[2], yr0.at[2], zr0.at[2], u0.at[1], ys0.at[1], zs0.at[1], True)

    start, wait = round0(1)
    start()
    inner0(u0.at[1], True)
    wait()
    held = heldz(zr0.at[1])
    for x in range(8):
        ores[0, x] = part[x] + across0(u0.at[1], yr0.at[1], held, x)


def flush(a, b, oa, ob, sem):
    copies = [pltpu.make_async_copy(a, oa, sem.at[0]), pltpu.make_async_copy(b, ob, sem.at[1])]
    for c in copies:
        c.start()
    for c in copies:
        c.wait()


def on_device(phase, density, rhs):
    V = lambda *s: pltpu.VMEM(s, F32)
    M = pltpu.VMEM((384, 128), BF16)
    D = lambda *s: pltpu.SemaphoreType.DMA(s)
    scratch = [
        pltpu.VMEM((8, 64, 128), jnp.int32), V(8, 64, 128), V(8, 64, 128), V(8, 64, 128), V(8, 64, 128), V(10, 80, 128), V(3, 10, 80, 128),
        V(9, 64, 128), V(8, 80, 128), V(8, 64, 128), V(8, 64, 128), V(8, 64, 128), V(8, 64, 128),
        V(2, 8, 128), V(2, 8, 128), V(2, 8, 128), V(2, 8, 128),
        V(3, 2, 8, 128), V(3, 2, 8, 128), V(3, 2, 8, 128), V(3, 2, 8, 128),
        V(2, 12, 64, 128), V(4, 32, 128), V(5, 32, 128), V(4, 32, 128), V(4, 32, 128), V(4, 32, 128), V(4, 32, 128),
        V(4, 32, 128), V(12, 48, 128), V(4, 12, 64, 128),
        V(4, 2, 32, 128), V(2, 4, 8, 128), V(2, 4, 8, 128), V(2, 2, 8, 128), V(2, 2, 8, 128),
        V(2, 4, 2, 32, 128), V(3, 2, 4, 8, 128), V(3, 2, 4, 8, 128), V(3, 2, 2, 8, 128),
        V(1, 2, 32, 128), V(2, 1, 8, 128), V(2, 1, 8, 128), V(2, 1, 8, 128), V(2, 2, 8, 128),
        V(2, 1, 2, 32, 128), V(3, 2, 1, 8, 128), V(3, 2, 1, 8, 128), V(3, 2, 2, 8, 128),
        M, M, M, M, V(256, 128), V(4, 2, 64, 128), V(6, 48, 128), V(6, 80, 128), V(6, 80, 128), V(4, 4, 48, 128),
        V(12, 48, 128),
        V(3, 4, 4, 8, 128), V(2, 3, 4, 2, 8, 128), V(2, 3, 4, 2, 8, 128), V(3, 3, 4, 8, 128),
        V(8, 48, 128), V(2, 12, 64, 128), V(9, 48, 128), V(8, 64, 128), V(8, 48, 128), V(8, 48, 128), V(8, 48, 128),
        V(4, 24, 128), V(2, 6, 40, 128), V(5, 24, 128), V(4, 40, 128), V(4, 24, 128), V(4, 24, 128),
        D(3), D(6), D(6), D(3, 6), D(3, 6), D(3, 3, 3), D(3, 3, 3), D(3, 3, 3), D(3, 3, 3),
        D(3), D(3), D(4), D(4), D(4, 3, 3), D(4, 3, 3),
    ]
    near = pl.BlockSpec(memory_space=pltpu.VMEM)
    pair = pl.pallas_call(
        kernel,
        out_shape=(pltpu.VMEM(rhs.shape, F32),) * 2,
        in_specs=[pl.BlockSpec(memory_space=pl.ANY)] * 3,
        out_specs=(near,) * 2,
        scratch_shapes=scratch,
        compiler_params=pltpu.CompilerParams(collective_id=0, has_side_effects=True),
        name="vcycle",
    )(phase, density, rhs)
    pair = [pltpu.with_memory_space_constraint(v, pltpu.VMEM) for v in pair]
    return pl.pallas_call(
        flush,
        out_shape=(jax.ShapeDtypeStruct(rhs.shape, F32),) * 2,
        in_specs=[near] * 2,
        out_specs=(pl.BlockSpec(memory_space=pl.ANY),) * 2,
        scratch_shapes=[D(2)],
        name="flush",
    )(*pair)


def solution(mesh):
    in_specs = (P("gx", "gy", "gz"), P("gx", "gy", "gz"), P(None, "gx", "gy", "gz"))
    out_specs = (P(None, "gx", "gy", "gz"), P(None, "gx", "gy", "gz"))
    return jax.shard_map(on_device, mesh=mesh, in_specs=in_specs, out_specs=out_specs, check_vma=False)
```

```python
import functools

import jax
import jax.numpy as jnp
from jax import lax
from jax.experimental import pallas as pl
from jax.experimental.pallas import tpu as pltpu
from jax.sharding import PartitionSpec as P

MESH = pl.DeviceIdType.MESH
F32 = jnp.float32
W = 2.0 / 3.0
THIRD = 1.0 / 3.0
BF16 = jnp.bfloat16


def lanes(shape):
    return lax.broadcasted_iota(jnp.int32, shape, len(shape) - 1)


def roll(v, shift):
    return pltpu.roll(v, shift, 1)


def loop(count, body, init=0):
    return lax.fori_loop(0, count, body, init, unroll=True)


def each(count, body):
    def step(i, carry):
        body(i)
        return carry

    lax.fori_loop(0, count, step, 0, unroll=True)


def maps():
    row = lax.broadcasted_iota(jnp.int32, (128, 128), 0)
    col = lax.broadcasted_iota(jnp.int32, (128, 128), 1)
    hit = col == 32 + row // 2
    both = jnp.where(hit, 1.0, 0.0)
    odd = jnp.where(hit & (row % 2 == 1), 1.0, 0.0)
    even = jnp.where(hit & (row % 2 == 0), 1.0, 0.0)
    back = jnp.where(row == 32 + col // 2, 1.0, 0.0)
    return [jnp.concatenate([m.astype(BF16)] * 3, axis=0) for m in (both, odd, even, back)]


def mm(a, b):
    hi = a.astype(BF16)
    rest = a - hi.astype(F32)
    mid = rest.astype(BF16)
    low = (rest - mid.astype(F32)).astype(BF16)
    return lax.dot(jnp.concatenate([hi, mid, low], axis=1), b, preferred_element_type=F32)


def kernel(
    ph_h, de_h, rh_h, osol, ores,
    ph, de, f0, part, fze, rp, u0, fx, fy, fzu, fzd, w0, d0,
    rys, ryr, rzs, rzr, ys0, yr0, zs0, zr0,
    u1, f1, fx1, fy1u, fy1d, fz1u, fz1d, d1, w1, ce1,
    pkc, xyc, zpc, xzc, yzc, rxc, ryc, rzc, rec, pkf, xyf, zpf, xzf, yzf, rxf, ryf, rzf, ref_,
    mb, mo, me, mt, t0, t1, t2, t3, t4, t5, f1e,
    cc, pz, zc, gg,
    f2, u2, fx2, fy2, fz2, w2, d2,
    f3, u3, fx3, fy3, fz3, w3,
    in_sem, rss, rrs, s0s, r0s, s1c, r1c, s1f, r1f, csx, crx, csn, crn, gs, gr,
):
    gx, gy, gz = lax.axis_index("gx"), lax.axis_index("gy"), lax.axis_index("gz")
    nx, ny, nz = lax.axis_size("gx"), lax.axis_size("gy"), lax.axis_size("gz")
    near = [
        ({"gx": gx + 1}, gx < nx - 1, gx > 0),
        ({"gx": gx - 1}, gx > 0, gx < nx - 1),
        ({"gy": gy + 1}, gy < ny - 1, gy > 0),
        ({"gy": gy - 1}, gy > 0, gy < ny - 1),
        ({"gz": gz + 1}, gz < nz - 1, gz > 0),
        ({"gz": gz - 1}, gz > 0, gz < nz - 1),
    ]

    loads = [
        pltpu.make_async_copy(ph_h, ph, in_sem.at[0]),
        pltpu.make_async_copy(de_h, de, in_sem.at[1]),
        pltpu.make_async_copy(rh_h.at[0], f0, in_sem.at[2]),
    ]
    for c in loads:
        c.start()

    edge = (gx == 0) | (gx == nx - 1) | (gy == 0) | (gy == ny - 1) | (gz == 0) | (gz == nz - 1)

    @pl.when(edge)
    def _():
        for ref in (ryc, rzc, rec):
            ref[...] = jnp.zeros(ref.shape, F32)

    barrier = pltpu.get_barrier_semaphore()
    arrivals = 0
    for where, ok, back in near:
        arrivals = arrivals + jnp.where(back, 1, 0)

        @pl.when(ok)
        def _(where=where):
            pl.semaphore_signal(barrier, inc=1, device_id=where, device_id_type=MESH)

    @pl.when(edge)
    def _():
        for b in range(3):
            for x in (0, 9):
                u0[b, x, 8:72, :] = jnp.zeros((64, 128), F32)
        for ref in (yr0, zr0, gg, zc, rxc, rxf, ryf, rzf, ref_):
            ref[...] = jnp.zeros(ref.shape, F32)
        for y in (0, 2):
            cc[y] = jnp.zeros(cc.shape[1:], F32)

    def inside(at, step, count):
        return (at >= 0) if step == 0 else (at < count - 1) if step > 0 else (at > 0)

    def yz_ok(sy, sz):
        return inside(gy, sy, ny) & inside(gz, sz, nz)

    def at(sx, sy, sz):
        return {"gx": sx, "gy": gy + sy, "gz": gz + sz}

    steps = (-1, 0, 1)

    def faces(buf, n, rows, ys, yr, zs, zr, ss, rs):
        body = pl.ds(8, rows)
        pairs = [
            (buf.at[n, body], buf.at[0, body]),
            (buf.at[1, body], buf.at[n + 1, body]),
            (ys.at[1], yr.at[0]),
            (ys.at[0], yr.at[1]),
            (zs.at[1], zr.at[0]),
            (zs.at[0], zr.at[1]),
        ]

        def copy(d):
            src, dst = pairs[d]
            return pltpu.make_async_remote_copy(
                src_ref=src, dst_ref=dst, send_sem=ss.at[d], recv_sem=rs.at[d],
                device_id=near[d][0], device_id_type=MESH,
            )

        def start():
            for d in (4, 5, 2, 3, 0, 1):
                @pl.when(near[d][1])
                def _(d=d):
                    copy(d).start()

        def wait():
            for d in range(6):
                @pl.when(near[d][1])
                def _(d=d):
                    copy(d).wait_send()

                @pl.when(near[d][2])
                def _(d=d):
                    copy(d).wait_recv()

        return start, wait

    lane8 = lanes((8, 128))
    lane64 = lanes((64, 128))
    lane32 = lanes((32, 128))

    zero8 = jnp.zeros((8, 128), F32)

    def pack0(carry, plane, x):
        lo, hi = carry
        for t in range(8):
            v = plane[8 * t : 8 * t + 8]
            k = x * 8 + t
            here = lane8 == k
            lo = jnp.where(here, roll(v, k), lo)
            hi = jnp.where(here, roll(v, k + 1), hi)
        return lo, hi

    def z_beside0(plane, x, lo, hi):
        right = jnp.concatenate([roll(hi, 127 - (x * 8 + t)) for t in range(8)], axis=0)
        left = jnp.concatenate([roll(lo, lax.rem(128 - (x * 8 + t), 128)) for t in range(8)], axis=0)
        return (
            jnp.where(lane64 == 127, right, roll(plane, 127)),
            jnp.where(lane64 == 0, left, roll(plane, 1)),
        )

    def keep0(buf, ys, x, plane):
        buf[x + 1, 8:72, :] = plane
        ys[0, pl.ds(x, 1), :] = plane[0:1]
        ys[1, pl.ds(x, 1), :] = plane[63:64]

    def y_in(buf, yr, n, rows):
        def body(x):
            buf[x + 1, 7:8, :] = yr[0, pl.ds(x, 1), :]
            buf[x + 1, 8 + rows : 9 + rows, :] = yr[1, pl.ds(x, 1), :]

        each(n, body)

    def mod(v):
        return v % 128 if isinstance(v, int) else lax.rem(v, 128)

    def packz(acc, plane, x):
        for t in range(8):
            v = plane[8 * t : 8 * t + 8]
            k = 2 * (x * 8 + t)
            acc = jnp.where(lane8 == k, roll(v, mod(k + 1)), acc)
            acc = jnp.where(lane8 == mod(k + 127), roll(v, mod(k + 127)), acc)
        return acc

    def heldz(zr):
        return jnp.where(lane8 % 2 == 0, zr[0], zr[1])

    def keepu(buf, ys, x, plane):
        keep0(buf, ys, x, plane)
        buf[x + 1, 7:8, :] = jnp.zeros((1, 128), F32)
        buf[x + 1, 72:73, :] = jnp.zeros((1, 128), F32)

    def within0(buf, x, whole):
        c = buf[x + 1, 8:72, :]
        s = fy[x, 8:72, :] * buf[x + 1, 9:73, :] + fy[x, 7:71, :] * buf[x + 1, 7:71, :]
        s = s + fzu[x] * jnp.where(lane64 == 127, 0.0, roll(c, 127))
        s = s + fzd[x] * jnp.where(lane64 == 0, 0.0, roll(c, 1))
        if whole or x < 7:
            s = s + fx[x + 1] * buf[x + 2, 8:72, :]
        if whole or x > 0:
            s = s + fx[x] * buf[x, 8:72, :]
        return c, s

    def zface0(x, held):
        return fze[x] * jnp.concatenate([roll(held, mod(256 - 2 * (x * 8 + t))) for t in range(8)], axis=0)

    def across0(buf, yr, held, x):
        h = zface0(x, held)
        if x == 0:
            h = h + fx[0] * buf[0, 8:72, :]
        if x == 7:
            h = h + fx[8] * buf[9, 8:72, :]
        top = fy[x, 7:8, :] * yr[0, x : x + 1, :]
        end = fy[x, 71:72, :] * yr[1, x : x + 1, :]
        return jnp.concatenate(
            [h[0:8] + jnp.where(row8 == 0, top, 0.0), h[8:56], h[56:64] + jnp.where(row8 == 7, end, 0.0)], axis=0
        )

    def inner0(buf, resid):
        for x in range(8):
            c, s = within0(buf, x, False)
            part[x] = f0[x] - d0[x] * c + s if resid else c * THIRD + w0[x] * (f0[x] + s)

    def outer0(src, yr, zr, dst, ys, zs, out):
        held = heldz(zr)
        acc = zero8
        for x in range(8):
            new = part[x] + w0[x] * across0(src, yr, held, x)
            keepu(dst, ys, x, new)
            if out:
                osol[0, x] = d0[x] * new
            acc = packz(acc, new, x)
        zs[0] = acc
        zs[1] = acc

    row8 = lax.broadcasted_iota(jnp.int32, (8, 128), 0)

    for c in loads[:2]:
        c.wait()

    def body(x, carry):
        plane = jnp.where(ph[x] == 1, 1000.0, 1.0).astype(F32) * de[x]
        keep0(rp, rys, x, plane)
        return pack0(carry, plane, x)

    packed = loop(8, body, (zero8, zero8))
    rzs[0] = packed[0]
    rzs[1] = packed[1]

    pl.semaphore_wait(barrier, arrivals)
    start, wait = faces(rp, 8, 64, rys, ryr, rzs, rzr, rss, rrs)
    start()
    both, odd, even, back = maps()
    mb[...] = both
    mo[...] = odd
    me[...] = even
    mt[...] = back
    loads[2].wait()
    wait()

    @pl.when(gx == 0)
    def _():
        rp[0, 8:72, :] = rp[1, 8:72, :]

    @pl.when(gx == nx - 1)
    def _():
        rp[9, 8:72, :] = rp[8, 8:72, :]

    for ok, got, own, s in ((gy == 0, ryr, rys, 0), (gy == ny - 1, ryr, rys, 1), (gz == 0, rzr, rzs, 0), (gz == nz - 1, rzr, rzs, 1)):
        @pl.when(ok)
        def _(got=got, own=own, s=s):
            got[s] = own[s]

    y_in(rp, ryr, 8, 64)
    lo, hi = rzr[0], rzr[1]
    fx[0] = 2.0 / (rp[0, 8:72, :] + rp[1, 8:72, :])

    def body(x, carry):
        c = rp[x + 1, 8:72, :]
        up, down = z_beside0(c, x, lo, hi)
        xu = 2.0 / (c + rp[x + 2, 8:72, :])
        yu = 2.0 / (c + rp[x + 1, 9:73, :])
        zu = 2.0 / (c + up)
        zd = 2.0 / (c + down)
        fx[x + 1] = xu
        fy[x, 8:72, :] = yu
        fy[x, 7:8, :] = 2.0 / (c[0:1] + rp[x + 1, 7:8, :])
        fzu[x] = zu
        fzd[x] = zd
        diag = xu + fx[x] + yu + fy[x, 7:71, :] + zu + zd
        d0[x] = diag
        w = W / diag
        w0[x] = w
        first = w * f0[x]
        fze[x] = jnp.where(lane64 == 127, zu, jnp.where(lane64 == 0, zd, 0.0))
        keepu(u0.at[0], ys0.at[0], x, first)
        return packz(carry, first, x)

    packed = loop(8, body, zero8)
    zs0[0, 0] = packed
    zs0[0, 1] = packed

    def round0(b):
        return faces(u0.at[b], 8, 64, ys0.at[b], yr0.at[b], zs0.at[b], zr0.at[b], s0s.at[b], r0s.at[b])

    box = [(a, b, c) for a in steps for b in steps for c in steps if (a, b, c) != (0, 0, 0)]

    def box_exchange(pk, xy, zp, xz, yz, rx, ry, rz, re, ss, rs):
        def copy(a, b, c):
            if b and c:
                src, dst = yz.at[(b + 1) // 2, (c + 1) // 2], re.at[1 - a, (1 - b) // 2, (1 - c) // 2]
            elif a and c:
                src, dst = xz.at[(c + 1) // 2], rz.at[1 - a, (1 - c) // 2, pl.ds(0, xz.shape[1])]
            elif c:
                src, dst = zp.at[(c + 1) // 2], rz.at[1 - a, (1 - c) // 2]
            elif b:
                src, dst = xy.at[(b + 1) // 2], ry.at[1 - a, (1 - b) // 2]
            else:
                src, dst = pk, rx.at[(1 - a) // 2]
            return pltpu.make_async_remote_copy(
                src_ref=src, dst_ref=dst, send_sem=ss.at[a + 1, b + 1, c + 1], recv_sem=rs.at[a + 1, b + 1, c + 1],
                device_id=at(gx + a, b, c), device_id_type=MESH,
            )

        def start(far=(1, 2, 3)):
            for n in sorted(far, reverse=True):
                for a, b, c in box:
                    if abs(a) + abs(b) + abs(c) == n:
                        @pl.when(inside(gx, a, nx) & yz_ok(b, c))
                        def _(a=a, b=b, c=c):
                            copy(a, b, c).start()

        def wait():
            for a, b, c in box:
                @pl.when(inside(gx, a, nx) & yz_ok(b, c))
                def _(a=a, b=b, c=c):
                    copy(a, b, c).wait_send()

                @pl.when(inside(gx, -a, nx) & yz_ok(-b, -c))
                def _(a=a, b=b, c=c):
                    copy(a, b, c).wait_recv()

        return start, wait

    low4 = lane8 % 8 < 4

    def half(v):
        return pltpu.roll(v, 4, 0)

    def pack_box(gets, pk, xy, zp, xz, yz):
        edge = {(b, c): zero8 for b in range(2) for c in range(2)}
        for a, get in enumerate(gets):
            planes = [get(x) for x in range(4)]
            pairs = [jnp.where(own1, planes[2 * i], roll(planes[2 * i + 1], 64)) for i in range(2)]
            for i in range(2):
                pk[a, i] = pairs[i]
            xy[0, a] = jnp.where(row8 < 4, pairs[0][0:8], half(pairs[1][0:8]))
            xy[1, a] = jnp.where(row8 >= 4, pairs[0][24:32], half(pairs[1][24:32]))
            face = [zero8, zero8]
            for x in range(4):
                for t in range(4):
                    v = planes[x][8 * t : 8 * t + 8]
                    k = x * 4 + t
                    for c, first in ((0, 96), (1, 40)):
                        face[c] = jnp.where(lane8 // 8 == k, roll(v, (8 * k + first) % 128), face[c])
                        if t in (0, 3):
                            b = t // 3
                            edge[b, c] = jnp.where(lane8 // 8 == 4 * a + x, roll(v, (32 * a + 8 * x + first) % 128), edge[b, c])
            zp[0, a] = face[0]
            zp[1, a] = face[1]
            if a % 2 == 0:
                even = face
            if a % 2 == 1:
                xz[0, a // 2] = jnp.where(low4, even[0], roll(face[0], 4))
                xz[1, a // 2] = jnp.where(low4, roll(face[1], 124), even[1])
            elif a == len(gets) - 1:
                xz[0, a // 2] = face[0]
                xz[1, a // 2] = face[1]
        for b in range(2):
            for c in range(2):
                yz[b, c] = edge[b, c]

    def unpack_box(own, rx, ry, rz, re, a, put):
        def side(dx, x, c, first):
            def corner(b):
                return roll(re[dx, b, c], (first - 32 * a - 8 * x) % 128)

            shift, i = (0, a) if dx == 1 else ((4 - 8 * c) * (a % 2), a // 2)
            mid = [roll(rz[dx, c, i], (first + shift - 8 * (4 * x + t)) % 128) for t in range(4)]
            return jnp.concatenate([corner(0)] + mid + [corner(1)], axis=0)

        for dx in range(3):
            for x in range(4):
                i = x // 2
                turn = (lambda v: roll(v, 64)) if x % 2 else (lambda v: v)
                flip = half if i else (lambda v: v)
                mid = own(x) if dx == 1 else turn(rx[dx // 2, a, i])
                centre = jnp.concatenate([turn(flip(ry[dx, 0, a])), mid, turn(flip(ry[dx, 1, a]))], axis=0)
                out = jnp.where((lane48 >= 96) & (lane48 < 100), side(dx, x, 1, 96), 0.0)
                out = jnp.where((lane48 >= 32) & (lane48 < 96), centre, out)
                out = jnp.where((lane48 >= 28) & (lane48 < 32), side(dx, x, 0, 24), out)
                put(4 * dx + x, out)

    lane48 = lanes((48, 128))
    start, wait = round0(0)
    start()

    own1 = (lane32 >= 32) & (lane32 < 96)

    def rows_of(ref, base, n, off):
        return ref[pl.ds(base + off, n, stride=2), :]

    def pair_rows(ref, base, n):
        return rows_of(ref, base, n, 0) + rows_of(ref, base, n, 1)

    for i in range(5):
        t0[0:64, :] = fx[2 * i]
        fx1[i] = mm(pair_rows(t0, 0, 32), mb[...])

    def body(i):
        yu = fy[2 * i, pl.ds(9, 32, stride=2), :] + fy[2 * i + 1, pl.ds(9, 32, stride=2), :]
        yd = fy[2 * i, pl.ds(7, 32, stride=2), :] + fy[2 * i + 1, pl.ds(7, 32, stride=2), :]
        t1[i, 0] = fzu[2 * i] + fzu[2 * i + 1]
        t1[i, 1] = fzd[2 * i] + fzd[2 * i + 1]
        zu = t1[i, 0, pl.ds(0, 32, stride=2), :] + t1[i, 0, pl.ds(1, 32, stride=2), :]
        zd = t1[i, 1, pl.ds(0, 32, stride=2), :] + t1[i, 1, pl.ds(1, 32, stride=2), :]
        yu, yd, zu, zd = mm(yu, mb[...]), mm(yd, mb[...]), mm(zu, mo[...]), mm(zd, me[...])
        fy1u[i] = yu
        fy1d[i] = yd
        fz1u[i] = zu
        fz1d[i] = zd
        diag = fx1[i] + fx1[i + 1] + yu + yd + zu + zd
        d1[i] = jnp.where(own1, diag, 0.0)

    each(4, body)
    parts1 = (lambda x: d1[x], lambda x: fx1[x + 1], lambda x: fy1u[x], lambda x: fz1u[x])
    pack_box(parts1, pkc, xyc, zpc, xzc, yzc)
    c_start, c_wait = box_exchange(pkc, xyc, zpc, xzc, yzc, rxc, ryc, rzc, rec, s1c, r1c)
    c_start((1,2))

    def pack2(planes):
        out = zero8
        for x in range(2):
            for t in range(2):
                g = 2 * x + t
                v = roll(planes[x][8 * t : 8 * t + 8], (32 * g - 48) % 128)
                out = jnp.where((lane8 >= 32 * g) & (lane8 < 32 * g + 32), v, out)
        return out

    xu, yu, zu, dg = [], [], [], []
    for i in range(2):
        t0[0:32, :] = fx1[2 * i]
        t0[32:64, :] = fx1[2 * i + 2]
        t0[64:96, :] = fz1u[2 * i] + fz1u[2 * i + 1]
        t0[96:128, :] = fz1d[2 * i] + fz1d[2 * i + 1]
        t0[128:160, :] = fy1u[2 * i] + fy1u[2 * i + 1]
        t0[160:192, :] = fy1d[2 * i] + fy1d[2 * i + 1]
        xd_, xu_ = mm(pair_rows(t0, 0, 16), mb[...]), mm(pair_rows(t0, 32, 16), mb[...])
        zu_, zd_ = mm(pair_rows(t0, 64, 16), mo[...]), mm(pair_rows(t0, 96, 16), me[...])
        yu_, yd_ = mm(rows_of(t0, 128, 16, 1), mb[...]), mm(rows_of(t0, 160, 16, 0), mb[...])
        xu.append(xu_)
        yu.append(yu_)
        zu.append(zu_)
        dg.append(xu_ + xd_ + yu_ + yd_ + zu_ + zd_)
    for a, planes in enumerate((dg, xu, yu, zu)):
        cc[1, gx, a] = pack2(planes)

    def gather(sx, rx, sn, rn):
        def xcopy(d):
            return pltpu.make_async_remote_copy(
                src_ref=cc.at[1, gx], dst_ref=cc.at[1, gx], send_sem=sx.at[d - 1], recv_sem=rx.at[d - 1],
                device_id={"gx": lax.rem(gx + d, nx)}, device_id_type=MESH,
            )

        def ncopy(d):
            src = [cc.at[1], cc.at[1], pz.at[1], pz.at[0]][d - 2]
            dst = [cc.at[0], cc.at[2], zc.at[0], zc.at[1]][d - 2]
            return pltpu.make_async_remote_copy(
                src_ref=src, dst_ref=dst, send_sem=sn.at[d - 2], recv_sem=rn.at[d - 2],
                device_id=near[d][0], device_id_type=MESH,
            )

        def xstart():
            for d in range(1, 4):
                xcopy(d).start()

        def xwait():
            for d in range(1, 4):
                pltpu.make_async_remote_copy(
                    src_ref=cc.at[1, gx], dst_ref=cc.at[1, lax.rem(gx + 4 - d, nx)],
                    send_sem=sx.at[d - 1], recv_sem=rx.at[d - 1],
                    device_id={"gx": lax.rem(gx + d, nx)}, device_id_type=MESH,
                ).wait()

        def nstart(ds):
            for d in ds:
                @pl.when(near[d][1])
                def _(d=d):
                    ncopy(d).start()

        def nwait(ds):
            for d in ds:
                @pl.when(near[d][1])
                def _(d=d):
                    ncopy(d).wait_send()

                @pl.when(near[d][2])
                def _(d=d):
                    ncopy(d).wait_recv()

        return (
            xstart, xwait,
            lambda: nstart((2, 3)), lambda: nwait((2, 3)),
            lambda: nstart((4, 5)), lambda: nwait((4, 5)),
        )

    cg = gather(csx, crx, csn, crn)

    inner0(u0.at[0], False)
    wait()
    c_start((3,))
    cg[0]()
    outer0(u0.at[0], yr0.at[0], zr0.at[0], u0.at[1], ys0.at[1], zs0.at[1], False)
    start, wait = round0(1)
    start()
    inner0(u0.at[1], True)
    wait()

    cg[1]()
    cg[2]()
    held = heldz(zr0.at[1])
    for i in range(4):
        total = None
        for j in range(2):
            x = 2 * i + j
            r = part[x] + across0(u0.at[1], yr0.at[1], held, x)
            total = r if total is None else total + r
        t1[i, 0] = total
        f1[i] = mm(t1[i, 0, pl.ds(0, 32, stride=2), :] + t1[i, 0, pl.ds(1, 32, stride=2), :], mb[...])

    pack_box([lambda x: f1[x]], pkf, xyf, zpf, xzf, yzf)
    f_start, f_wait = box_exchange(pkf, xyf, zpf, xzf, yzf, rxf, ryf, rzf, ref_, s1f, r1f)
    f_start()
    cg[3]()
    low16 = lane8 % 32 < 16

    def body(y):
        for b in range(4):
            for j in range(2):
                v, w = cc[y, b, 2 * j], cc[y, b, 2 * j + 1]
                pz[0, y, b, j] = jnp.where(low16, v, roll(w, 16))
                pz[1, y, b, j] = jnp.where(low16, roll(w, 112), v)

    each(3, body)
    cg[4]()
    c_wait()
    for a, get in enumerate(parts1):
        def put(p, out, a=a):
            ce1[a, p, 8:56, :] = out
            if a == 0:
                ok = out > 0.0
                w1[p] = jnp.where(ok, W / jnp.where(ok, out, 1.0), 0.0)

        unpack_box(get, rxc, ryc, rzc, rec, a, put)

    def zero_rows(ref, n, rows):
        def body(p):
            ref[p, 0:8, :] = zero8
            ref[p, 8 + rows : 16 + rows, :] = zero8

        each(n, body)

    zero_rows(ce1.at[2], 12, 48)
    for b in range(2):
        zero_rows(u1.at[b], 12, 48)
    f_wait()

    def put(p, out):
        f1e[p] = out
        u1[0, p, 8:56, :] = w1[p] * out

    unpack_box(lambda x: f1[x], rxf, ryf, rzf, ref_, 0, put)

    def beside1(buf, p, r0, n):
        c = buf[p, r0 : r0 + n, :]
        s = ce1[1, p, r0 : r0 + n, :] * buf[p + 1, r0 : r0 + n, :]
        s = s + ce1[1, p - 1, r0 : r0 + n, :] * buf[p - 1, r0 : r0 + n, :]
        s = s + ce1[2, p, r0 : r0 + n, :] * buf[p, r0 + 1 : r0 + 1 + n, :]
        s = s + ce1[2, p, r0 - 1 : r0 - 1 + n, :] * buf[p, r0 - 1 : r0 - 1 + n, :]
        z = ce1[3, p, r0 : r0 + n, :]
        return c, s + z * roll(c, 127) + roll(z * c, 1)

    def sweep1(src, dst, first, count):
        def body(i):
            p = i + first
            c, s = beside1(u1.at[src], p, 8, 48)
            u1[dst, p, 8:56, :] = c * THIRD + w1[p] * (f1e[p] + s)

        each(count, body)

    sweep1(0, 1, 1, 10)

    src2 = []
    for i in range(2):
        total = None
        for j in range(2):
            x = 2 * i + j
            c, s = beside1(u1.at[1], x + 4, 16, 32)
            r = f1[x] - d1[x] * c + s
            total = r if total is None else total + r
        t0[32 * i : 32 * i + 32, :] = jnp.where(own1, total, 0.0)
        src2.append(mm(pair_rows(t0, 32 * i, 16), mb[...]))
    gg[1, 1, gx] = pack2(src2)

    def fcopy(d, sy, sz):
        return pltpu.make_async_remote_copy(
            src_ref=gg.at[1, 1, gx], dst_ref=gg.at[1 - sz, 1 - sy, gx],
            send_sem=gs.at[d, sy + 1, sz + 1], recv_sem=gr.at[d, sy + 1, sz + 1],
            device_id=at(lax.rem(gx + d, nx), sy, sz), device_id_type=MESH,
        )

    def fback(d, sy, sz):
        return pltpu.make_async_remote_copy(
            src_ref=gg.at[1, 1, gx], dst_ref=gg.at[1 - sz, 1 - sy, lax.rem(gx + 4 - d, nx)],
            send_sem=gs.at[d, sy + 1, sz + 1], recv_sem=gr.at[d, sy + 1, sz + 1],
            device_id=at(lax.rem(gx + d, nx), sy, sz), device_id_type=MESH,
        )

    order = sorted([(sy, sz) for sy in steps for sz in steps], key=lambda o: -abs(o[0]) - abs(o[1]))

    def g_start():
        for sy, sz in order:
            @pl.when(yz_ok(sy, sz))
            def _(sy=sy, sz=sz):
                for d in (2, 1, 3, 0):
                    if (d, sy, sz) != (0, 0, 0):
                        fcopy(d, sy, sz).start()

    def g_wait():
        for sy, sz in order:
            @pl.when(yz_ok(sy, sz))
            def _(sy=sy, sz=sz):
                for d in range(4):
                    if (d, sy, sz) != (0, 0, 0):
                        fcopy(d, sy, sz).wait_send()

            @pl.when(yz_ok(-sy, -sz))
            def _(sy=sy, sz=sz):
                for d in range(4):
                    if (d, sy, sz) != (0, 0, 0):
                        fback(d, sy, sz).wait_recv()

    g_start()
    cg[5]()

    def spread2(get, put, shift, reach):
        def body(b):
            for y in range(3):
                v = [get(z, y, b) for z in range(3)]
                for x in range(2):
                    for t in range(2):
                        g = 2 * x + t
                        left = roll(v[0], (16 - 32 * g + shift) % 128)
                        mid = roll(v[1], (48 - 32 * g) % 128)
                        right = roll(v[2], (80 - 32 * g - shift) % 128)
                        out = jnp.where(lane8 < 48, left, jnp.where(lane8 < 80, mid, right))
                        out = jnp.where((lane8 >= 48 - reach) & (lane8 < 80 + reach), out, 0.0)
                        put(2 * b + x, 16 * y + 8 * t, out)

        each(4, body)

    def put_d(p, r, v):
        d2[p, r : r + 8, :] = v
        ok = v > 0.0
        w2[p, r : r + 8, :] = jnp.where(ok, W / jnp.where(ok, v, 1.0), 0.0)

    def put_x(p, r, v):
        fx2[p + 1, r : r + 8, :] = v

    def put_y(p, r, v):
        fy2[p, 8 + r : 16 + r, :] = v

    def put_z(p, r, v):
        fz2[p, r : r + 8, :] = v

    def put_f(p, r, v):
        f2[p, r : r + 8, :] = v
        u2[0, p + 2, 8 + r : 16 + r, :] = w2[p, r : r + 8, :] * v

    for a, put in enumerate((put_d, put_x, put_y, put_z)):
        spread2(lambda z, y, b, a=a: cc[y, b, a] if z == 1 else zc[z // 2, y, b, a // 2], put, 16 * (a % 2), 16)
    fx2[0] = jnp.zeros((48, 128), F32)
    fx3[0] = jnp.zeros((24, 128), F32)

    zero_rows(fy2, 8, 48)
    zero_rows(fy3, 4, 24)
    for b in range(2):
        zero_rows(u2.at[b], 12, 48)
        zero_rows(u3.at[b], 6, 24)
        for p in (0, 1, 10, 11):
            u2[b, p, 8:56, :] = jnp.zeros((48, 128), F32)
        for p in (0, 5):
            u3[b, p, 8:32, :] = jnp.zeros((24, 128), F32)

    row48 = lax.broadcasted_iota(jnp.int32, (48, 128), 0)

    def body(p):
        a, b = 2 * p, 2 * p + 1
        t5[p, 0] = fx2[b + 1]
        t5[p, 1] = fz2[a] + fz2[b]
        ysum = fy2[a, 8:56, :] + fy2[b, 8:56, :]
        t5[p, 2] = ysum
        inner = fx2[a + 1]
        inner = inner + jnp.where(row48 % 2 == 0, ysum, 0.0)
        inner = inner + jnp.where(lane48 % 2 == 0, fz2[a] + fz2[b], 0.0)
        t5[p, 3] = d2[a] + d2[b] - 2.0 * inner
        pick = lambda q, off: t5[p, q, pl.ds(off, 24, stride=2), :]
        fx3[p + 1] = mm(pick(0, 0) + pick(0, 1), mb[...])
        fz3[p] = mm(pick(1, 0) + pick(1, 1), mo[...])
        fy3[p, 8:32, :] = mm(pick(2, 1), mb[...])
        diag = mm(pick(3, 0) + pick(3, 1), mb[...])
        ok = diag > 0.0
        w3[p] = jnp.where(ok, W / jnp.where(ok, diag, 1.0), 0.0)

    each(4, body)

    g_wait()
    spread2(lambda z, y, b: gg[z, y, b], put_f, 0, 32)

    def beside(buf, fxr, fyr, fzr, p, rows, o=0):
        a, b = o + 8, o + 8 + rows
        c = buf[p + 1, a:b, :]
        s = fxr[p + 1, o : o + rows, :] * buf[p + 2, a:b, :] + fxr[p, o : o + rows, :] * buf[p, a:b, :]
        s = s + fyr[p, a:b, :] * buf[p + 1, a + 1 : b + 1, :]
        s = s + fyr[p, a - 1 : b - 1, :] * buf[p + 1, a - 1 : b - 1, :]
        z = fzr[p, o : o + rows, :]
        return c, s + z * roll(c, 127) + roll(z * c, 1)

    def sweep2(src, dst, o, rows):
        def body(p):
            c, s = beside(u2.at[src, pl.ds(1, 10)], fx2, fy2, fz2, p, rows, o)
            here = slice(o, o + rows)
            u2[dst, p + 2, o + 8 : o + 8 + rows, :] = c * THIRD + w2[p, here, :] * (f2[p, here, :] + s)

        each(8, body)

    def sweep3(src, dst):
        def body(p):
            c, s = beside(u3.at[src], fx3, fy3, fz3, p, 24)
            u3[dst, p + 1, 8:32, :] = c * THIRD + w3[p] * (f3[p] + s)

        each(4, body)

    sweep2(0, 1, 0, 48)

    def body(p):
        total = None
        for j in range(2):
            c, s = beside(u2.at[1, pl.ds(1, 10)], fx2, fy2, fz2, 2 * p + j, 48)
            r = f2[2 * p + j] - d2[2 * p + j] * c + s
            total = r if total is None else total + r
        t5[p, 0] = total
        src = mm(t5[p, 0, pl.ds(0, 24, stride=2), :] + t5[p, 0, pl.ds(1, 24, stride=2), :], mb[...])
        f3[p] = src
        u3[0, p + 1, 8:32, :] = w3[p] * src

    each(4, body)
    sweep3(0, 1)
    sweep3(1, 0)
    sweep3(0, 1)

    def body(p):
        e = mm(u3[1, p + 1, 8:32, :], mt[...])
        t5[p, 1, pl.ds(0, 24, stride=2), :] = e
        t5[p, 1, pl.ds(1, 24, stride=2), :] = e
        wide = t5[p, 1]
        for j in range(2):
            q = 2 * p + j
            u2[0, q + 2, 8:56, :] = u2[1, q + 2, 8:56, :] + jnp.where(d2[q] > 0.0, wide, 0.0)

    each(4, body)
    sweep2(0, 1, 8, 32)
    sweep2(1, 0, 8, 32)

    def body(q):
        e = mm(u2[0, 2 * gx + q, 20:44, :], mt[...])
        t2[q, pl.ds(0, 24, stride=2), :] = e
        t2[q, pl.ds(1, 24, stride=2), :] = e

    each(6, body)

    def body(i):
        p = i + 1
        u1[0, p, 8:56, :] = u1[1, p, 8:56, :] + jnp.where(w1[p] > 0.0, t2[p // 2], 0.0)

    each(10, body)
    sweep1(0, 1, 2, 8)
    sweep1(1, 0, 3, 6)

    def body(q):
        c = u1[0, q + 3, 12:52, :]
        e = mm(c, mt[...])
        t3[q, pl.ds(0, 40, stride=2), :] = e
        t3[q, pl.ds(1, 40, stride=2), :] = e
        t4[q, pl.ds(0, 40, stride=2), :] = c
        t4[q, pl.ds(1, 40, stride=2), :] = c

    each(6, body)

    y_in(u0.at[1], yr0.at[1], 8, 64)

    def body(p):
        u0[0, p, :, :] = u0[1, p, :, :] + t3[(p + 1) // 2]

    each(10, body)

    held = heldz(zr0.at[1])
    extra = zero8
    for q in range(4):
        for t in range(8):
            v = t4[q + 1, 8 + 8 * t : 16 + 8 * t, :]
            k = 2 * (16 * q + t)
            up, down = roll(v, (k - 31) % 128), roll(v, (k - 97) % 128)
            extra = jnp.where(lane8 == k, up, jnp.where(lane8 == (k + 127) % 128, down, extra))
            extra = jnp.where(lane8 == k + 16, roll(up, 16), jnp.where(lane8 == k + 15, roll(down, 16), extra))
    held = held + extra
    acc = zero8
    for x in range(8):
        c, s = within0(u0.at[0], x, True)
        new = c * THIRD + w0[x] * (f0[x] + s + zface0(x, held))
        keepu(u0.at[2], ys0.at[2], x, new)
        acc = packz(acc, new, x)
    zs0[2, 0] = acc
    zs0[2, 1] = acc
    start, wait = round0(2)
    start()
    inner0(u0.at[2], False)
    wait()
    outer0(u0.at[2], yr0.at[2], zr0.at[2], u0.at[1], ys0.at[1], zs0.at[1], True)

    start, wait = round0(1)
    start()
    inner0(u0.at[1], True)
    wait()
    held = heldz(zr0.at[1])
    for x in range(8):
        ores[0, x] = part[x] + across0(u0.at[1], yr0.at[1], held, x)


def flush(a, b, oa, ob, sem):
    copies = [pltpu.make_async_copy(a, oa, sem.at[0]), pltpu.make_async_copy(b, ob, sem.at[1])]
    for c in copies:
        c.start()
    for c in copies:
        c.wait()


def on_device(phase, density, rhs):
    V = lambda *s: pltpu.VMEM(s, F32)
    M = pltpu.VMEM((384, 128), BF16)
    D = lambda *s: pltpu.SemaphoreType.DMA(s)
    scratch = [
        pltpu.VMEM((8, 64, 128), jnp.int32), V(8, 64, 128), V(8, 64, 128), V(8, 64, 128), V(8, 64, 128), V(10, 80, 128), V(3, 10, 80, 128),
        V(9, 64, 128), V(8, 80, 128), V(8, 64, 128), V(8, 64, 128), V(8, 64, 128), V(8, 64, 128),
        V(2, 8, 128), V(2, 8, 128), V(2, 8, 128), V(2, 8, 128),
        V(3, 2, 8, 128), V(3, 2, 8, 128), V(3, 2, 8, 128), V(3, 2, 8, 128),
        V(2, 12, 64, 128), V(4, 32, 128), V(5, 32, 128), V(4, 32, 128), V(4, 32, 128), V(4, 32, 128), V(4, 32, 128),
        V(4, 32, 128), V(12, 48, 128), V(4, 12, 64, 128),
        V(4, 2, 32, 128), V(2, 4, 8, 128), V(2, 4, 8, 128), V(2, 2, 8, 128), V(2, 2, 8, 128),
        V(2, 4, 2, 32, 128), V(3, 2, 4, 8, 128), V(3, 2, 4, 8, 128), V(3, 2, 2, 8, 128),
        V(1, 2, 32, 128), V(2, 1, 8, 128), V(2, 1, 8, 128), V(2, 1, 8, 128), V(2, 2, 8, 128),
        V(2, 1, 2, 32, 128), V(3, 2, 1, 8, 128), V(3, 2, 1, 8, 128), V(3, 2, 2, 8, 128),
        M, M, M, M, V(256, 128), V(4, 2, 64, 128), V(6, 48, 128), V(6, 80, 128), V(6, 80, 128), V(4, 4, 48, 128),
        V(12, 48, 128),
        V(3, 4, 4, 8, 128), V(2, 3, 4, 2, 8, 128), V(2, 3, 4, 2, 8, 128), V(3, 3, 4, 8, 128),
        V(8, 48, 128), V(2, 12, 64, 128), V(9, 48, 128), V(8, 64, 128), V(8, 48, 128), V(8, 48, 128), V(8, 48, 128),
        V(4, 24, 128), V(2, 6, 40, 128), V(5, 24, 128), V(4, 40, 128), V(4, 24, 128), V(4, 24, 128),
        D(3), D(6), D(6), D(3, 6), D(3, 6), D(3, 3, 3), D(3, 3, 3), D(3, 3, 3), D(3, 3, 3),
        D(3), D(3), D(4), D(4), D(4, 3, 3), D(4, 3, 3),
    ]
    near = pl.BlockSpec(memory_space=pltpu.VMEM)
    pair = pl.pallas_call(
        kernel,
        out_shape=(pltpu.VMEM(rhs.shape, F32),) * 2,
        in_specs=[pl.BlockSpec(memory_space=pl.ANY)] * 3,
        out_specs=(near,) * 2,
        scratch_shapes=scratch,
        compiler_params=pltpu.CompilerParams(collective_id=0, has_side_effects=True),
        name="vcycle",
    )(phase, density, rhs)
    pair = [pltpu.with_memory_space_constraint(v, pltpu.VMEM) for v in pair]
    return pl.pallas_call(
        flush,
        out_shape=(jax.ShapeDtypeStruct(rhs.shape, F32),) * 2,
        in_specs=[near] * 2,
        out_specs=(pl.BlockSpec(memory_space=pl.ANY),) * 2,
        scratch_shapes=[D(2)],
        name="flush",
    )(*pair)


def solution(mesh):
    in_specs = (P("gx", "gy", "gz"), P("gx", "gy", "gz"), P(None, "gx", "gy", "gz"))
    out_specs = (P(None, "gx", "gy", "gz"), P(None, "gx", "gy", "gz"))
    return jax.shard_map(on_device, mesh=mesh, in_specs=in_specs, out_specs=out_specs, check_vma=False)
```
